32 devices in a mesh: grp: 8 (over y, x, core), tile: 4 (over z).
Axes of the slice: x: 2, y: 2, z: 4, core: 2. Of those that a mesh axis runs over, the one named last changes fastest.
Arguments:
- coeff: bfloat16 [32, 256, 4096], P('grp', None, 'tile'), may hold values from -0.09375 to 0.09375
- energy: float32 [32, 4096], P('grp', 'tile'), may hold values from 1 to 3
- ranks: int32 [32, 32], replicated, may hold values from 32 to 256, as said below
- assign: int32 [1024], P(('grp', 'tile')), may hold values from 0 to 1023, each once
- screen: bfloat16 [1024, 256, 256], P(('grp', 'tile')), may hold values from -0.375 to 0.375
- initial: float32 [32, 8, 4096], P('grp', None, 'tile'), may hold values from -6 to 6
Outputs:
- rayleigh: float32 [2, 8, 8], replicated
- basis: float32 [32, 8, 4096], P('grp', None, 'tile')
- residual: float32 [32, 8, 4096], P('grp', None, 'tile')
The draws below stay inside these ranges and needn't reach their ends.
Inputs may be any that keep to these rules, and one draw needn't show every extreme that they name: ranks is symmetric and its diagonal equals 256. `assign`: every pair index appears exactly once.
All inputs are finite; a program needn't handle non-finite values.
Results may differ from the reference program's by a relative error of at most 0.0075.
Values may be sent and summed in bfloat16 or wider, within the bound.
No kernel may reach another device: no remote copies, remote signals or barrier semaphores. Data moves between devices by JAX's collectives and lax.ppermute only.
A program may use at most 64 MiB of HBM per device.

```python
import jax
import jax.numpy as jnp
from jax import lax

P_SIZE = 4096
RMAX = 256
NV = 8
ITERS = 2
K = 32


def draw_ranks(key, part):
    base = jax.random.randint(key, (K, K), RMAX // 8, RMAX + 1)
    upper = jnp.triu(base, 1)
    ident = jnp.eye(K, dtype=jnp.int32)
    return (upper + upper.T + ident * RMAX).astype(jnp.int32)


def level_of(rng, extent, split, smallest, high):
    factor_of = 1.0
    for dim, parts in split:
        heights = jax.random.uniform(jax.random.fold_in(jax.random.fold_in(rng, 6), dim), (parts,), jnp.float32, smallest / len(split), high / len(split))
        factor_of = factor_of * jnp.repeat(jnp.exp(heights), extent[dim] // parts).reshape((-1,) + (1,) * (len(extent) - 1 - dim))
    return factor_of


def gaussian(stream_key, extent, scale, bound, split=(), held_as=jnp.bfloat16):
    gain = level_of(stream_key, extent, split, -0.22, 0.18) if split else 1.0
    values = jax.random.normal(stream_key, extent, jnp.float32) * scale * gain
    return jnp.minimum(jnp.maximum(values, -bound), bound).astype(held_as)


def setup_inputs(seed: int = 0) -> dict:
    seeds = jax.random.split(jax.random.key(seed), 7)
    coeff = gaussian(seeds[0], (K, RMAX, P_SIZE), P_SIZE ** -0.5, 0.09375, ((0, 8), (2, 4)))
    energy = jnp.clip(1.0 + 2.0 * jax.random.uniform(seeds[1], (K, P_SIZE), jnp.float32) ** level_of(seeds[1], (K, P_SIZE), ((0, 8), (1, 4)), -0.2, 0.2), 1.0, 3.0)
    ranks = draw_ranks(jax.random.fold_in(seeds[6], 71), 0)
    assign = jax.random.permutation(seeds[3], K * K).astype(jnp.int32)
    screen = gaussian(seeds[4], (K * K, RMAX, RMAX), RMAX ** -0.5, 0.375, ((0, 32),))
    initial = gaussian(seeds[5], (K, NV, P_SIZE), 1.0, 6.0, ((0, 8), (2, 4)), jnp.float32)
    return dict(coeff=coeff, energy=energy, ranks=ranks, assign=assign, screen=screen, initial=initial)


def inner_sum(left, right):
    return jnp.einsum('knp,kmp->nm', left, right, precision=lax.Precision.HIGHEST)

def combine_rows(weights, block):
    return jnp.einsum('mn,kmp->knp', weights, block, precision=lax.Precision.HIGHEST)

def orthonormal(block, count):
    gram = inner_sum(block, block) / count
    lower = jnp.linalg.cholesky(gram)
    inverse = lax.linalg.triangular_solve(lower, jnp.eye(NV, dtype=jnp.float32), left_side=True, lower=True)
    return combine_rows(inverse.T, block)

def apply_kernel(block, coeff, energy, ranks, assign, screen):
    block_b = block.astype(jnp.bfloat16)

    def project_one(pair):
        return jnp.dot(pair[1].astype(jnp.float32), pair[0].T.astype(jnp.float32), preferred_element_type=jnp.float32)
    dens = lax.map(project_one, (coeff, block_b))
    dens_b = dens.astype(jnp.bfloat16)
    task_row = (assign // K).astype(jnp.int32)
    task_col = (assign % K).astype(jnp.int32)
    task_rank = ranks[task_row, task_col]
    levels = jnp.arange(RMAX, dtype=jnp.int32)

    def task_one(item):
        blocks, column, rank_now = item
        keep = (levels < rank_now).astype(jnp.float32)
        masked = dens_b[column] * keep.astype(jnp.bfloat16)[None, :]
        result = jnp.dot(masked.astype(jnp.float32), blocks.T.astype(jnp.float32), preferred_element_type=jnp.float32)
        return result * keep[None, :]
    terms = lax.map(task_one, (screen, task_col, task_rank))
    rows = jax.ops.segment_sum(terms, task_row, num_segments=K)
    rows_b = rows.astype(jnp.bfloat16)

    def expand_one(pair):
        return jnp.dot(pair[1].astype(jnp.float32), pair[0].astype(jnp.float32), preferred_element_type=jnp.float32)
    coupled = lax.map(expand_one, (coeff, rows_b))
    return energy[:, None, :] * block + coupled

def reference(coeff, energy, ranks, assign, screen, initial):
    count = K * P_SIZE
    basis = orthonormal(initial, count)
    collected = []
    residual = initial
    for step in range(ITERS):
        sigma = apply_kernel(basis, coeff, energy, ranks, assign, screen)
        projected = inner_sum(basis, sigma) / count
        collected.append(projected)
        residual = sigma - combine_rows(projected, basis)
        precond = residual / energy[:, None, :]
        correlation = inner_sum(basis, precond) / count
        direction = precond - combine_rows(correlation, basis)
        basis = orthonormal(direction, count)
    return (jnp.stack(collected), basis, residual)
```

```python
import functools

import jax
import jax.numpy as jnp
from jax import lax
from jax.experimental import pallas as pl
from jax.experimental.pallas import tpu as pltpu
from jax.sharding import PartitionSpec as P

ITERS = 2
LANES = 128
BF = jnp.bfloat16
F4 = jnp.float32
NT = (((1,), (1,)), ((), ()))
NN = (((1,), (0,)), ((), ()))


def split2(x):
    high = x.astype(BF)
    return high, (x - high.astype(F4)).astype(BF)


def mm(left, right, dims):
    return lax.dot_general(left, right, dims, preferred_element_type=F4)


def exact(left, right, dims):
    return lax.dot_general(
        left, right, dims, preferred_element_type=F4, precision=lax.Precision.HIGHEST
    )


def apply_small(weights, block):
    total = weights[:, 0:1] * block[0:1, :]
    for m in range(1, weights.shape[1]):
        total = total + weights[:, m : m + 1] * block[m : m + 1, :]
    return total


def inverse_cholesky(gram):
    v = gram.shape[0]
    row_id = lax.broadcasted_iota(jnp.int32, (v, v), 0)
    col_id = lax.broadcasted_iota(jnp.int32, (v, v), 1)
    inverse = (row_id == col_id).astype(F4)
    rest = gram
    for j in range(v):
        scale = 1.0 / jnp.sqrt(rest[j : j + 1, j : j + 1])
        col = rest[:, j : j + 1] * scale
        row = rest[j : j + 1, :] * scale
        inv_row = inverse[j : j + 1, :] * scale
        below = jnp.where(row_id[:, 0:1] > j, col, 0.0)
        inverse = jnp.where(row_id == j, inv_row, inverse - below * inv_row)
        if j + 1 < v:
            rest = rest - col * row
    return inverse


def pack_moments(scratch, parts):
    total = None
    for i, part in enumerate(parts):
        width = part.shape[1]
        scratch[...] = jnp.zeros(scratch.shape, F4)
        scratch[:, 0:width] = part
        placed = scratch[...]
        if i:
            placed = pltpu.roll(placed, i * width, 1)
        total = placed if total is None else total + placed
    used = sum(part.shape[1] for part in parts)
    first = total.astype(BF).astype(F4)
    left = total - first
    second = left.astype(BF).astype(F4)
    third = (left - second).astype(BF).astype(F4)
    packed = first + pltpu.roll(second, used, 1) + pltpu.roll(third, 2 * used, 1)
    return packed.astype(BF)


def unpack_moments(total, used):
    width = total.shape[1]
    return total + pltpu.roll(total, width - used, 1) + pltpu.roll(total, width - 2 * used, 1)


def store_for_all(out_ref, dens_halves, moments):
    pairs, _, tiles, blocks = out_ref.shape[:4]

    def one(g, carry):
        for h in range(2):
            for t in range(tiles):
                for k in range(blocks - 1):
                    out_ref[g, h, t, k] = dens_halves[k][h]
                out_ref[g, h, t, blocks - 1] = moments
        return carry

    lax.fori_loop(0, pairs, one, 0, unroll=True)


def project(block, coeff):
    high, low = split2(block)
    both = mm(jnp.concatenate([high, low], 0), coeff, NT)
    v = block.shape[0]
    total = both[:v] + both[v:]
    half = total.shape[1] // 2
    return [total[:, :half].astype(BF), total[:, half:].astype(BF)]


def start_kernel(x_ref, e_ref, c_ref, out_ref, scratch):
    local_k, v, _ = x_ref.shape
    halves = []
    moments = None
    for k in range(local_k):
        x = x_ref[k]
        halves.append(project(x, c_ref[k]))
        xh, xl = split2(x)
        eh, el = split2(x * e_ref[k : k + 1, :])
        big = mm(jnp.concatenate([xh, xl], 0), jnp.concatenate([xh, eh], 0), NT)
        small = mm(xh, jnp.concatenate([xl, el], 0), NT)
        part = big[:v] + big[v:] + small
        moments = part if moments is None else moments + part
    store_for_all(out_ref, halves, pack_moments(scratch, [moments]))


def gather_dens(core_ref, mine_ref, other_ref, dens_ref):
    groups, tiles, blocks = mine_ref.shape[:3]
    local_k = blocks - 1
    core = core_ref[0]
    moments = None
    for g in range(groups):
        for k in range(local_k):
            for ref, slot in ((mine_ref, core), (other_ref, 1 - core)):
                total = ref[g, 0, k].astype(F4)
                for t in range(1, tiles):
                    total = total + ref[g, t, k].astype(F4)
                dens_ref[slot, g * local_k + k] = total
        for t in range(tiles):
            block = mine_ref[g, t, local_k].astype(F4)
            moments = block if moments is None else moments + block
    return moments


def run_tasks(assign_ref, ranks_ref, screen_ref, core_ref, dens_ref, dens_b, acc, keep_ref, send_ref, scratch, local_k):
    total_k, v = dens_b.shape[1:3]
    half = dens_b.shape[3]
    slots = acc.shape[1]
    core = core_ref[0]
    for which in range(2):
        for slot in range(slots):
            acc[which, slot] = jnp.zeros((v, 2 * half), F4)
    lane = lax.broadcasted_iota(jnp.int32, (v, 2 * half), 1)

    def one(t, carry):
        pair = assign_ref[t]
        row = pair // total_k
        col = pair - row * total_k
        keep = lane < ranks_ref[row, col]
        vec = jnp.concatenate([dens_b[0, col], dens_b[1, col]], 1)
        vec = jnp.where(keep, vec, 0.0).astype(BF)
        term = jnp.where(keep, mm(vec, screen_ref[t], NT), 0.0)
        owner = row // local_k
        slot = (owner // 2) * local_k + row - owner * local_k
        which = (owner + core) % 2
        acc[which, slot] = acc[which, slot] + term
        return carry

    lax.fori_loop(0, assign_ref.shape[0], one, 0, unroll=8)
    total = None
    for which in range(2):
        for slot in range(slots):
            owner_pair = slot // local_k
            k = (owner_pair * 2 + (core + which) % 2) * local_k + slot % local_k
            rows = acc[which, slot]
            rh, rl = split2(rows)
            dens = jnp.concatenate([dens_ref[0, k], dens_ref[1, k]], 1)
            dh, dl = split2(dens)
            big = mm(jnp.concatenate([rh, rl], 0), dh, NT)
            part = big[:v] + big[v:] + mm(rh, dl, NT)
            total = part if total is None else total + part
            (send_ref if which else keep_ref)[slot] = rows
    scratch[...] = jnp.zeros(scratch.shape, F4)
    scratch[:, 0:v] = total
    for ref, value in ((keep_ref, scratch[...]), (send_ref, scratch[...])):
        ref[slots] = jnp.concatenate([value, jnp.zeros_like(value)], 1)


def pad_small(scratch, small):
    scratch[...] = jnp.zeros(scratch.shape, F4)
    scratch[:, 0 : small.shape[1]] = small
    return scratch[...]


def first_tasks_kernel(core_ref, assign_ref, ranks_ref, mine_ref, other_ref, screen_ref,
                       keep_ref, send_ref, dens_ref, small_ref, dens_b, acc, scratch, *, count):
    v = mine_ref.shape[3]
    local_k = mine_ref.shape[2] - 1
    moments = unpack_moments(gather_dens(core_ref, mine_ref, other_ref, dens_ref), 2 * v)
    inverse = inverse_cholesky(moments[:, 0:v] / count)
    weighted = moments[:, v : 2 * v] / count
    diag = exact(exact(inverse, weighted, NN), inverse, NT)
    for h in range(2):
        for k in range(dens_ref.shape[1]):
            dens = apply_small(inverse, dens_ref[h, k])
            dens_ref[h, k] = dens
            dens_b[h, k] = dens.astype(BF)
    small_ref[0] = pad_small(scratch, inverse)
    small_ref[1] = pad_small(scratch, diag)
    run_tasks(assign_ref, ranks_ref, screen_ref, core_ref, dens_ref, dens_b, acc,
              keep_ref, send_ref, scratch, local_k)


def next_tasks_kernel(core_ref, assign_ref, ranks_ref, mine_ref, other_ref, prev_dens_ref,
                      prev_small_ref, screen_ref, keep_ref, send_ref, dens_ref, small_ref,
                      dens_b, acc, scratch, *, count):
    v = mine_ref.shape[3]
    local_k = mine_ref.shape[2] - 1
    moments = unpack_moments(gather_dens(core_ref, mine_ref, other_ref, dens_ref), 4 * v) / count
    pp = moments[:, 0:v]
    mix = moments[:, v : 2 * v]
    rp = moments[:, 2 * v : 3 * v]
    rv = moments[:, 3 * v : 4 * v]
    prev_diag = prev_small_ref[1][:, 0:v]
    inverse = inverse_cholesky(pp - exact(mix, mix, NT))
    cross = exact(rv, mix, NT)
    cross_t = exact(mix, rv, NT)
    weighted = rp - cross - cross_t + exact(exact(mix, prev_diag, NN), mix, NT)
    diag = exact(exact(inverse, weighted, NN), inverse, NT)
    both = exact(inverse, mix, NN)
    for h in range(2):
        for k in range(dens_ref.shape[1]):
            dens = apply_small(inverse, dens_ref[h, k]) - apply_small(both, prev_dens_ref[h, k])
            dens_ref[h, k] = dens
            dens_b[h, k] = dens.astype(BF)
    small_ref[0] = pad_small(scratch, inverse)
    small_ref[1] = pad_small(scratch, diag)
    small_ref[2] = pad_small(scratch, both)
    run_tasks(assign_ref, ranks_ref, screen_ref, core_ref, dens_ref, dens_b, acc,
              keep_ref, send_ref, scratch, local_k)


def rows_kernel(keep_ref, recv_ref, out_ref):
    pairs, tiles, blocks, v, half = out_ref.shape
    local_k = (blocks - 1) // 2
    slots = pairs * local_k
    diag = (keep_ref[slots] + recv_ref[slots])[:, :half]
    first = diag.astype(BF).astype(F4)
    left = diag - first
    second = left.astype(BF).astype(F4)
    third = (left - second).astype(BF).astype(F4)
    packed = (first + pltpu.roll(second, v, 1) + pltpu.roll(third, 2 * v, 1)).astype(BF)
    for g in range(pairs):
        for k in range(local_k):
            rows = (keep_ref[g * local_k + k] + recv_ref[g * local_k + k]).astype(BF)
            for t in range(tiles):
                out_ref[g, t, 2 * k] = rows[:, :half]
                out_ref[g, t, 2 * k + 1] = rows[:, half:]
        for t in range(tiles):
            out_ref[g, t, blocks - 1] = packed


def sum_rows(recv_ref):
    sources, blocks, v, half = recv_ref.shape
    sums = []
    for b in range(blocks):
        total = recv_ref[0, b].astype(F4)
        for s in range(1, sources):
            total = total + recv_ref[s, b].astype(F4)
        sums.append(total)
    local_k = (blocks - 1) // 2
    rows = [jnp.concatenate([sums[2 * k], sums[2 * k + 1]], 1).astype(BF) for k in range(local_k)]
    return rows, unpack_moments(sums[-1], v)[:, 0:v]


def after_first_kernel(recv_ref, x_ref, e_ref, c_ref, small_ref, out_ref, v_ref, p_ref, ray_ref, scratch, *, count):
    local_k, v, _ = x_ref.shape
    rows, coupled_part = sum_rows(recv_ref)
    inverse = small_ref[0][:, 0:v]
    ray = small_ref[1][:, 0:v] + coupled_part / count
    ray_ref[...] = pad_small(scratch, ray)
    halves = []
    moments = None
    for k in range(local_k):
        basis = apply_small(inverse, x_ref[k])
        energy = e_ref[k : k + 1, :]
        sigma = energy * basis + mm(rows[k], c_ref[k], NN)
        residual = sigma - apply_small(ray, basis)
        precond = residual / energy
        v_ref[k] = basis
        p_ref[k] = precond
        halves.append(project(precond, c_ref[k]))
        bh, bl = split2(basis)
        rh, rl = split2(residual)
        ph, pw = split2(precond)
        big = mm(jnp.concatenate([ph, rh, pw, rl], 0), jnp.concatenate([ph, bh], 0), NT)
        small = mm(jnp.concatenate([ph, rh], 0), jnp.concatenate([pw, bl], 0), NT)
        part = big[: 2 * v] + big[2 * v :] + small
        moments = part if moments is None else moments + part
    store_for_all(out_ref, halves, pack_moments(scratch, [moments[:v], moments[v:]]))


def last_rows_kernel(recv_ref, v_ref, p_ref, e_ref, c_ref, small_ref, out_ref, res_ref, basis_ref, q_ref, ray_ref, scratch, *, count):
    local_k, v, _ = v_ref.shape
    rows, coupled_part = sum_rows(recv_ref)
    inverse = small_ref[0][:, 0:v]
    both = small_ref[2][:, 0:v]
    ray = small_ref[1][:, 0:v] + coupled_part / count
    ray_ref[...] = pad_small(scratch, ray)
    moments = None
    for k in range(local_k):
        basis = apply_small(inverse, p_ref[k]) - apply_small(both, v_ref[k])
        energy = e_ref[k : k + 1, :]
        sigma = energy * basis + mm(rows[k], c_ref[k], NN)
        residual = sigma - apply_small(ray, basis)
        precond = residual / energy
        res_ref[k] = residual
        basis_ref[k] = basis
        q_ref[k] = precond
        bh, bl = split2(basis)
        ph, pw = split2(precond)
        big = mm(jnp.concatenate([ph, pw], 0), jnp.concatenate([ph, bh], 0), NT)
        part = big[:v] + big[v:] + mm(ph, jnp.concatenate([pw, bl], 0), NT)
        moments = part if moments is None else moments + part
    packed = pack_moments(scratch, [moments])
    for d in range(out_ref.shape[0]):
        out_ref[d] = packed


def finish_kernel(recv_ref, q_ref, b_ref, out_ref, *, count):
    local_k, v, _ = q_ref.shape
    total = recv_ref[0].astype(F4)
    for d in range(1, recv_ref.shape[0]):
        total = total + recv_ref[d].astype(F4)
    moments = unpack_moments(total, 2 * v) / count
    mix = moments[:, v : 2 * v]
    inverse = inverse_cholesky(moments[:, 0:v] - exact(mix, mix, NT))
    both = exact(inverse, mix, NN)
    for k in range(local_k):
        out_ref[k] = apply_small(inverse, q_ref[k]) - apply_small(both, b_ref[k])


VM = pl.BlockSpec(memory_space=pltpu.VMEM)
SM = pl.BlockSpec(memory_space=pltpu.SMEM)


def call(body, outs, ins, args, scratch=()):
    return pl.pallas_call(
        body,
        out_shape=outs,
        in_specs=ins,
        out_specs=jax.tree.map(lambda _: VM, outs),
        scratch_shapes=scratch,
    )(*args)


def per_device(coeff, energy, ranks, assign, screen, initial):
    groups = lax.axis_size("grp")
    tiles = lax.axis_size("tile")
    devices = groups * tiles
    pairs = groups // 2
    local_k, v, width = initial.shape
    levels = coeff.shape[1]
    half = levels // 2
    total_k = local_k * groups
    count = float(total_k * width * tiles)
    core = (lax.axis_index("grp") % 2).reshape(1)
    axes = ("grp", "tile")
    same_core = [[g * tiles + t for g in range(c, groups, 2) for t in range(tiles)] for c in range(2)]
    swap = [(g, g ^ 1) for g in range(groups)]
    sds = jax.ShapeDtypeStruct
    small_scratch = pltpu.VMEM((v, half), F4)

    def to_all(blocks):
        sent = blocks.reshape((devices,) + blocks.shape[3:])
        got = lax.all_to_all(sent, axes, 0, 0, tiled=True)
        other = lax.ppermute(got, "grp", swap)
        shape = (groups, tiles) + got.shape[1:]
        return got.reshape(shape), other.reshape(shape)

    def to_owner(keep, send):
        recv = lax.ppermute(send, "grp", swap)
        out = call(rows_kernel, sds((pairs, tiles, 2 * local_k + 1, v, half), BF), [VM, VM], (keep, recv))
        out = out.reshape((pairs * tiles,) + out.shape[2:])
        return lax.all_to_all(out, axes, 0, 0, tiled=True, axis_index_groups=same_core)

    all_shape = sds((pairs, 2, tiles, local_k + 1, v, half), BF)
    slots = pairs * local_k + 1
    task_outs = (
        sds((slots, v, levels), F4),
        sds((slots, v, levels), F4),
        sds((2, total_k, v, half), F4),
    )
    task_scratch = (
        pltpu.VMEM((2, total_k, v, half), BF),
        pltpu.VMEM((2, slots - 1, v, levels), F4),
        small_scratch,
    )
    flat = sds((local_k, v, width), F4)
    ray_shape = sds((v, half), F4)

    sent = call(start_kernel, all_shape, [VM] * 3, (initial, energy, coeff), (small_scratch,))
    mine, other = to_all(sent)
    keep, send, dens, small = call(
        functools.partial(first_tasks_kernel, count=count),
        task_outs + (sds((2, v, half), F4),),
        [SM, SM, SM, VM, VM, VM],
        (core, assign, ranks, mine, other, screen),
        task_scratch,
    )
    got = to_owner(keep, send)
    sent, basis, precond, ray0 = call(
        functools.partial(after_first_kernel, count=count),
        (all_shape, flat, flat, ray_shape),
        [VM] * 5,
        (got, initial, energy, coeff, small),
        (small_scratch,),
    )
    mine, other = to_all(sent)
    keep, send, dens, small = call(
        functools.partial(next_tasks_kernel, count=count),
        task_outs + (sds((3, v, half), F4),),
        [SM, SM, SM, VM, VM, VM, VM, VM],
        (core, assign, ranks, mine, other, dens, small, screen),
        task_scratch,
    )
    got = to_owner(keep, send)
    sent, residual, basis, precond, ray1 = call(
        functools.partial(last_rows_kernel, count=count),
        (sds((devices, v, half), BF), flat, flat, flat, ray_shape),
        [VM] * 6,
        (got, basis, precond, energy, coeff, small),
        (small_scratch,),
    )
    got = lax.all_to_all(sent, axes, 0, 0, tiled=True)
    basis = call(
        functools.partial(finish_kernel, count=count), flat, [VM] * 3, (got, precond, basis)
    )
    rayleigh = jnp.stack([ray0[:, :v].T, ray1[:, :v].T])
    return (rayleigh, basis, residual)


def solution(mesh):
    placed = (
        P("grp", None, "tile"),
        P("grp", "tile"),
        P(),
        P(("grp", "tile")),
        P(("grp", "tile"), None, None),
        P("grp", None, "tile"),
    )
    return jax.shard_map(
        per_device,
        mesh=mesh,
        in_specs=placed,
        out_specs=(P(), P("grp", None, "tile"), P("grp", None, "tile")),
        check_vma=False,
    )
```

```python
import functools

import jax
import jax.numpy as jnp
from jax import lax
from jax.experimental import pallas as pl
from jax.experimental.pallas import tpu as pltpu
from jax.sharding import PartitionSpec as P

ITERS = 2
LANES = 128
BF = jnp.bfloat16
F4 = jnp.float32
NT = (((1,), (1,)), ((), ()))
NN = (((1,), (0,)), ((), ()))


def split2(x):
    high = x.astype(BF)
    return high, (x - high.astype(F4)).astype(BF)


def mm(left, right, dims):
    return lax.dot_general(left, right, dims, preferred_element_type=F4)


def exact(left, right, dims):
    return lax.dot_general(
        left, right, dims, preferred_element_type=F4, precision=lax.Precision.HIGHEST
    )


def apply_small(weights, block):
    total = weights[:, 0:1] * block[0:1, :]
    for m in range(1, weights.shape[1]):
        total = total + weights[:, m : m + 1] * block[m : m + 1, :]
    return total


def inverse_cholesky(gram):
    v = gram.shape[0]
    row_id = lax.broadcasted_iota(jnp.int32, (v, v), 0)
    col_id = lax.broadcasted_iota(jnp.int32, (v, v), 1)
    inverse = (row_id == col_id).astype(F4)
    rest = gram
    for j in range(v):
        scale = 1.0 / jnp.sqrt(rest[j : j + 1, j : j + 1])
        col = rest[:, j : j + 1] * scale
        row = rest[j : j + 1, :] * scale
        inv_row = inverse[j : j + 1, :] * scale
        below = jnp.where(row_id[:, 0:1] > j, col, 0.0)
        inverse = jnp.where(row_id == j, inv_row, inverse - below * inv_row)
        if j + 1 < v:
            rest = rest - col * row
    return inverse


def pack_moments(scratch, parts):
    total = None
    for i, part in enumerate(parts):
        width = part.shape[1]
        scratch[...] = jnp.zeros(scratch.shape, F4)
        scratch[:, 0:width] = part
        placed = scratch[...]
        if i:
            placed = pltpu.roll(placed, i * width, 1)
        total = placed if total is None else total + placed
    used = sum(part.shape[1] for part in parts)
    first = total.astype(BF).astype(F4)
    left = total - first
    second = left.astype(BF).astype(F4)
    third = (left - second).astype(BF).astype(F4)
    packed = first + pltpu.roll(second, used, 1) + pltpu.roll(third, 2 * used, 1)
    return packed.astype(BF)


def unpack_moments(total, used):
    width = total.shape[1]
    return total + pltpu.roll(total, width - used, 1) + pltpu.roll(total, width - 2 * used, 1)


def store_for_all(out_ref, dens_halves, moments):
    pairs, _, tiles, blocks = out_ref.shape[:4]

    def one(g, carry):
        for h in range(2):
            for t in range(tiles):
                for k in range(blocks - 1):
                    out_ref[g, h, t, k] = dens_halves[k][h]
                out_ref[g, h, t, blocks - 1] = moments
        return carry

    lax.fori_loop(0, pairs, one, 0, unroll=True)


def project(block, coeff):
    high, low = split2(block)
    both = mm(jnp.concatenate([high, low], 0), coeff, NT)
    v = block.shape[0]
    total = both[:v] + both[v:]
    half = total.shape[1] // 2
    return [total[:, :half].astype(BF), total[:, half:].astype(BF)]


def start_kernel(x_hbm, e_hbm, c_hbm, out_ref, x_ref, e_ref, c_ref, sems, c_sems, scratch):
    local_k, v, _ = x_ref.shape
    copies = [
        pltpu.make_async_copy(x_hbm, x_ref, sems.at[0]),
        pltpu.make_async_copy(e_hbm, e_ref, sems.at[1]),
    ]
    c_copies = [pltpu.make_async_copy(c_hbm.at[k], c_ref.at[k], c_sems.at[k]) for k in range(local_k)]
    for copy in copies + c_copies:
        copy.start()
    for copy in copies:
        copy.wait()
    halves = []
    moments = None
    for k in range(local_k):
        x = x_ref[k]
        xh, xl = split2(x)
        eh, el = split2(x * e_ref[k : k + 1, :])
        big = mm(jnp.concatenate([xh, xl], 0), jnp.concatenate([xh, eh], 0), NT)
        small = mm(xh, jnp.concatenate([xl, el], 0), NT)
        part = big[:v] + big[v:] + small
        moments = part if moments is None else moments + part
        c_copies[k].wait()
        halves.append(project(x, c_ref[k]))
    store_for_all(out_ref, halves, pack_moments(scratch, [moments]))


def gather_kernel(mine_ref, dens_ref, moments_ref):
    groups, tiles, blocks = mine_ref.shape[:3]
    local_k = blocks - 1
    moments = None
    for g in range(groups):
        for k in range(local_k):
            total = mine_ref[g, 0, k].astype(F4)
            for t in range(1, tiles):
                total = total + mine_ref[g, t, k].astype(F4)
            dens_ref[g * local_k + k] = total
        for t in range(tiles):
            block = mine_ref[g, t, local_k].astype(F4)
            moments = block if moments is None else moments + block
    moments_ref[...] = moments


CHUNKS = 4


class Tasks:
    def __init__(self, assign_hbm, ranks_hbm, screen_hbm, core_ref, scratch):
        self.assign, self.ranks, self.screen, self.acc, self.dens_b, self.sems, self.small = scratch
        self.core = core_ref[0]
        chunk = self.screen.shape[0] // CHUNKS
        self.heads = [
            pltpu.make_async_copy(assign_hbm, self.assign, self.sems.at[CHUNKS]),
            pltpu.make_async_copy(ranks_hbm, self.ranks, self.sems.at[CHUNKS + 1]),
        ]
        self.chunks = []
        for i in range(CHUNKS):
            part = pl.ds(i * chunk, chunk)
            self.chunks.append(
                pltpu.make_async_copy(screen_hbm.at[part], self.screen.at[part], self.sems.at[i])
            )
        for copy in self.heads + self.chunks:
            copy.start()
        self.acc[...] = jnp.zeros(self.acc.shape, F4)

    def set_dens(self, dens_ref, which, k, dens):
        slot = (self.core + which) % 2
        dens_ref[slot, k] = dens
        self.dens_b[slot, k] = dens.astype(BF)

    def run(self, dens_ref, keep_ref, send_ref, coupled_ref):
        total_k, v, half = self.dens_b.shape[1:]
        lane = lax.broadcasted_iota(jnp.int32, (v, 2 * half), 1)
        for copy in self.heads:
            copy.wait()

        def one(t, carry):
            pair = self.assign[t]
            row = pair // total_k
            col = pair - row * total_k
            keep = lane < self.ranks[row, col]
            vec = jnp.concatenate([self.dens_b[0, col], self.dens_b[1, col]], 1)
            vec = jnp.where(keep, vec, 0.0).astype(BF)
            term = jnp.where(keep, mm(vec, self.screen[t], NT), 0.0)
            self.acc[0, row] = self.acc[0, row] + term[:, :half]
            self.acc[1, row] = self.acc[1, row] + term[:, half:]
            return carry

        chunk = self.screen.shape[0] // CHUNKS
        for i in range(CHUNKS):
            self.chunks[i].wait()
            lax.fori_loop(i * chunk, (i + 1) * chunk, one, 0, unroll=True)
        total = None
        for k in range(total_k):
            for h in range(2):
                rh, rl = split2(self.acc[h, k])
                dh, dl = split2(dens_ref[h, k])
                big = mm(jnp.concatenate([rh, rl], 0), dh, NT)
                part = big[:v] + big[v:] + mm(rh, dl, NT)
                total = part if total is None else total + part
            keep_ref[k] = self.acc[self.core, k]
            send_ref[k] = self.acc[1 - self.core, k]
        coupled_ref[...] = pack_moments(self.small, [total])


def pad_small(scratch, small):
    scratch[...] = jnp.zeros(scratch.shape, F4)
    scratch[:, 0 : small.shape[1]] = small
    return scratch[...]


def first_tasks_kernel(core_ref, assign_hbm, ranks_hbm, screen_hbm, mine_ref, other_ref, moments_ref,
                       keep_ref, send_ref, coupled_ref, dens_ref, small_ref, *scratch, count):
    tasks = Tasks(assign_hbm, ranks_hbm, screen_hbm, core_ref, scratch)
    v = mine_ref.shape[1]
    moments = unpack_moments(moments_ref[...], 2 * v)
    inverse = inverse_cholesky(moments[:, 0:v] / count)
    for k in range(mine_ref.shape[0]):
        for which, ref in ((0, mine_ref), (1, other_ref)):
            tasks.set_dens(dens_ref, which, k, apply_small(inverse, ref[k]))
    tasks.run(dens_ref, keep_ref, send_ref, coupled_ref)
    weighted = moments[:, v : 2 * v] / count
    diag = exact(exact(inverse, weighted, NN), inverse, NT)
    small_ref[0] = pad_small(tasks.small, inverse)
    small_ref[1] = pad_small(tasks.small, diag)


def next_tasks_kernel(core_ref, assign_hbm, ranks_hbm, screen_hbm, mine_ref, other_ref, moments_ref,
                      prev_dens_ref, prev_small_ref, keep_ref, send_ref, coupled_ref, dens_ref,
                      small_ref, *scratch, count):
    tasks = Tasks(assign_hbm, ranks_hbm, screen_hbm, core_ref, scratch)
    v = mine_ref.shape[1]
    moments = unpack_moments(moments_ref[...], 4 * v) / count
    pp = moments[:, 0:v]
    mix = moments[:, v : 2 * v]
    inverse = inverse_cholesky(pp - exact(mix, mix, NT))
    both = apply_small(inverse, mix)
    for k in range(mine_ref.shape[0]):
        for which, ref in ((0, mine_ref), (1, other_ref)):
            dens = apply_small(inverse, ref[k])
            dens = dens - apply_small(both, prev_dens_ref[(tasks.core + which) % 2, k])
            tasks.set_dens(dens_ref, which, k, dens)
    tasks.run(dens_ref, keep_ref, send_ref, coupled_ref)
    rp = moments[:, 2 * v : 3 * v]
    rv = moments[:, 3 * v : 4 * v]
    prev_diag = prev_small_ref[1][:, 0:v]
    weighted = rp - exact(rv, mix, NT) - exact(mix, rv, NT) + exact(exact(mix, prev_diag, NN), mix, NT)
    diag = exact(exact(inverse, weighted, NN), inverse, NT)
    small_ref[0] = pad_small(tasks.small, inverse)
    small_ref[1] = pad_small(tasks.small, diag)
    small_ref[2] = pad_small(tasks.small, both)


def rows_kernel(keep_ref, recv_ref, coupled_ref, out_ref):
    groups, tiles, blocks = out_ref.shape[:3]
    local_k = blocks - 1
    for g in range(groups):
        for k in range(local_k):
            rows = (keep_ref[g * local_k + k] + recv_ref[g * local_k + k]).astype(BF)
            for t in range(tiles):
                out_ref[g, t, k] = rows
        for t in range(tiles):
            out_ref[g, t, local_k] = coupled_ref[...]


def sum_rows(recv_ref):
    pairs, _, tiles, blocks, v, _ = recv_ref.shape

    def summed(block, halves):
        total = None
        for g in range(pairs):
            for h in halves:
                for t in range(tiles):
                    part = recv_ref[g, h, t, block].astype(F4)
                    total = part if total is None else total + part
        return total

    rows = []
    for k in range(blocks - 1):
        rows.append(jnp.concatenate([summed(k, (0,)), summed(k, (1,))], 1).astype(BF))
    return rows, unpack_moments(summed(blocks - 1, (0, 1)), v)[:, 0:v]


def after_first_kernel(recv_ref, x_ref, e_ref, c_ref, small_ref, out_ref, v_ref, p_ref, ray_ref, scratch, *, count):
    local_k, v, _ = x_ref.shape
    rows, coupled_part = sum_rows(recv_ref)
    inverse = small_ref[0][:, 0:v]
    ray = small_ref[1][:, 0:v] + coupled_part / count
    ray_ref[...] = pad_small(scratch, ray)
    halves = []
    moments = None
    for k in range(local_k):
        basis = apply_small(inverse, x_ref[k])
        energy = e_ref[k : k + 1, :]
        sigma = energy * basis + mm(rows[k], c_ref[k], NN)
        residual = sigma - apply_small(ray, basis)
        precond = residual / energy
        v_ref[k] = basis
        p_ref[k] = precond
        halves.append(project(precond, c_ref[k]))
        bh, bl = split2(basis)
        rh, rl = split2(residual)
        ph, pw = split2(precond)
        big = mm(jnp.concatenate([ph, rh, pw, rl], 0), jnp.concatenate([ph, bh], 0), NT)
        small = mm(jnp.concatenate([ph, rh], 0), jnp.concatenate([pw, bl], 0), NT)
        part = big[: 2 * v] + big[2 * v :] + small
        moments = part if moments is None else moments + part
    store_for_all(out_ref, halves, pack_moments(scratch, [moments[:v], moments[v:]]))


def last_rows_kernel(recv_ref, v_ref, p_ref, e_ref, c_ref, small_ref, out_ref, res_ref, basis_ref, q_ref, ray_ref, scratch, *, count):
    local_k, v, _ = v_ref.shape
    rows, coupled_part = sum_rows(recv_ref)
    inverse = small_ref[0][:, 0:v]
    both = small_ref[2][:, 0:v]
    ray = small_ref[1][:, 0:v] + coupled_part / count
    ray_ref[...] = pad_small(scratch, ray)
    moments = None
    for k in range(local_k):
        basis = apply_small(inverse, p_ref[k]) - apply_small(both, v_ref[k])
        energy = e_ref[k : k + 1, :]
        sigma = energy * basis + mm(rows[k], c_ref[k], NN)
        residual = sigma - apply_small(ray, basis)
        precond = residual / energy
        res_ref[k] = residual
        basis_ref[k] = basis
        q_ref[k] = precond
        bh, bl = split2(basis)
        ph, pw = split2(precond)
        big = mm(jnp.concatenate([ph, pw], 0), jnp.concatenate([ph, bh], 0), NT)
        part = big[:v] + big[v:] + mm(ph, jnp.concatenate([pw, bl], 0), NT)
        moments = part if moments is None else moments + part
    packed = pack_moments(scratch, [moments])
    for d in range(out_ref.shape[0]):
        out_ref[d] = packed


def finish_kernel(recv_ref, q_ref, b_ref, ray0_ref, ray1_ref, out_ref, ray_ref, *, count):
    local_k, v, _ = q_ref.shape
    total = recv_ref[0].astype(F4)
    for d in range(1, recv_ref.shape[0]):
        total = total + recv_ref[d].astype(F4)
    moments = unpack_moments(total, 2 * v) / count
    mix = moments[:, v : 2 * v]
    inverse = inverse_cholesky(moments[:, 0:v] - exact(mix, mix, NT))
    both = exact(inverse, mix, NN)
    for k in range(local_k):
        out_ref[k] = apply_small(inverse, q_ref[k]) - apply_small(both, b_ref[k])
    ray_ref[0] = ray0_ref[:, 0:v].T
    ray_ref[1] = ray1_ref[:, 0:v].T


VM = pl.BlockSpec(memory_space=pltpu.VMEM)
SM = pl.BlockSpec(memory_space=pltpu.SMEM)
ANY = pl.BlockSpec(memory_space=pltpu.HBM)


def call(body, outs, ins, args, scratch=()):
    args = [
        pltpu.with_memory_space_constraint(arg, pltpu.HBM) if spec is ANY else arg
        for arg, spec in zip(args, ins)
    ]
    return pl.pallas_call(
        body,
        out_shape=outs,
        in_specs=ins,
        out_specs=jax.tree.map(lambda _: VM, outs),
        scratch_shapes=scratch,
        compiler_params=pltpu.CompilerParams(vmem_limit_bytes=16 << 20),
    )(*args)


def per_device(coeff, energy, ranks, assign, screen, initial):
    groups = lax.axis_size("grp")
    tiles = lax.axis_size("tile")
    devices = groups * tiles
    pairs = groups // 2
    local_k, v, width = initial.shape
    levels = coeff.shape[1]
    half = levels // 2
    total_k = local_k * groups
    count = float(total_k * width * tiles)
    core = (lax.axis_index("grp") % 2).reshape(1)
    axes = ("grp", "tile")
    swap = [(g, g ^ 1) for g in range(groups)]
    sds = jax.ShapeDtypeStruct
    small_scratch = pltpu.VMEM((v, half), F4)
    dma = pltpu.SemaphoreType.DMA
    half_shape = sds((total_k, v, half), F4)

    def exchange(blocks, shape):
        sent = blocks.reshape((devices,) + blocks.shape[-3:])
        return lax.all_to_all(sent, axes, 0, 0, tiled=True).reshape(shape + sent.shape[1:])

    def to_all(blocks):
        got = exchange(blocks, (groups, tiles))
        mine, moments = call(gather_kernel, (half_shape, sds((v, half), F4)), [VM], (got,))
        return mine, lax.ppermute(mine, "grp", swap), moments

    def to_owner(keep, send, coupled):
        recv = lax.ppermute(send, "grp", swap)
        shape = sds((groups, tiles, local_k + 1, v, half), BF)
        out = call(rows_kernel, shape, [VM] * 3, (keep, recv, coupled))
        return exchange(out, (pairs, 2, tiles))

    all_shape = sds((pairs, 2, tiles, local_k + 1, v, half), BF)
    task_outs = (half_shape, half_shape, sds((v, half), BF), sds((2, total_k, v, half), F4))
    task_scratch = (
        pltpu.SMEM(assign.shape, jnp.int32),
        pltpu.SMEM(ranks.shape, jnp.int32),
        pltpu.VMEM(screen.shape, BF),
        pltpu.VMEM((2, total_k, v, half), F4),
        pltpu.VMEM((2, total_k, v, half), BF),
        dma((CHUNKS + 2,)),
        small_scratch,
    )
    task_ins = [SM, ANY, ANY, ANY]
    flat = sds((local_k, v, width), F4)
    ray_shape = sds((v, half), F4)

    sent = call(
        start_kernel,
        all_shape,
        [ANY] * 3,
        (initial, energy, coeff),
        (
            pltpu.VMEM(initial.shape, F4),
            pltpu.VMEM(energy.shape, F4),
            pltpu.VMEM(coeff.shape, BF),
            dma((2,)),
            dma((local_k,)),
            small_scratch,
        ),
    )
    mine, other, moments = to_all(sent)
    keep, send, coupled, dens, small = call(
        functools.partial(first_tasks_kernel, count=count),
        task_outs + (sds((2, v, half), F4),),
        task_ins + [VM] * 3,
        (core, assign, ranks, screen, mine, other, moments),
        task_scratch,
    )
    got = to_owner(keep, send, coupled)
    sent, basis, precond, ray0 = call(
        functools.partial(after_first_kernel, count=count),
        (all_shape, flat, flat, ray_shape),
        [VM] * 5,
        (got, initial, energy, coeff, small),
        (small_scratch,),
    )
    mine, other, moments = to_all(sent)
    keep, send, coupled, dens, small = call(
        functools.partial(next_tasks_kernel, count=count),
        task_outs + (sds((3, v, half), F4),),
        task_ins + [VM] * 5,
        (core, assign, ranks, screen, mine, other, moments, dens, small),
        task_scratch,
    )
    got = to_owner(keep, send, coupled)
    sent, residual, basis, precond, ray1 = call(
        functools.partial(last_rows_kernel, count=count),
        (sds((devices, v, half), BF), flat, flat, flat, ray_shape),
        [VM] * 6,
        (got, basis, precond, energy, coeff, small),
        (small_scratch,),
    )
    got = lax.all_to_all(sent, axes, 0, 0, tiled=True)
    basis, rayleigh = call(
        functools.partial(finish_kernel, count=count),
        (flat, sds((2, v, v), F4)),
        [VM] * 5,
        (got, precond, basis, ray0, ray1),
    )
    return (rayleigh, basis, residual)


def solution(mesh):
    placed = (
        P("grp", None, "tile"),
        P("grp", "tile"),
        P(),
        P(("grp", "tile")),
        P(("grp", "tile"), None, None),
        P("grp", None, "tile"),
    )
    return jax.shard_map(
        per_device,
        mesh=mesh,
        in_specs=placed,
        out_specs=(P(), P("grp", None, "tile"), P("grp", None, "tile")),
        check_vma=False,
    )
```

```python
import functools

import jax
import jax.numpy as jnp
from jax import lax
from jax.experimental import pallas as pl
from jax.experimental.pallas import tpu as pltpu
from jax.sharding import PartitionSpec as P

ITERS = 2
LANES = 128
BF = jnp.bfloat16
F4 = jnp.float32
NT = (((1,), (1,)), ((), ()))
NN = (((1,), (0,)), ((), ()))


def split2(x):
    high = x.astype(BF)
    return high, (x - high.astype(F4)).astype(BF)


def mm(left, right, dims):
    return lax.dot_general(left, right, dims, preferred_element_type=F4)


def exact(left, right, dims):
    return lax.dot_general(
        left, right, dims, preferred_element_type=F4, precision=lax.Precision.HIGHEST
    )


def apply_small(weights, block):
    total = weights[:, 0:1] * block[0:1, :]
    for m in range(1, weights.shape[1]):
        total = total + weights[:, m : m + 1] * block[m : m + 1, :]
    return total


def inverse_cholesky(gram):
    v = gram.shape[0]
    row_id = lax.broadcasted_iota(jnp.int32, (v, v), 0)
    col_id = lax.broadcasted_iota(jnp.int32, (v, v), 1)
    inverse = (row_id == col_id).astype(F4)
    rest = gram
    for j in range(v):
        scale = 1.0 / jnp.sqrt(rest[j : j + 1, j : j + 1])
        col = rest[:, j : j + 1] * scale
        row = rest[j : j + 1, :] * scale
        inv_row = inverse[j : j + 1, :] * scale
        below = jnp.where(row_id[:, 0:1] > j, col, 0.0)
        inverse = jnp.where(row_id == j, inv_row, inverse - below * inv_row)
        if j + 1 < v:
            rest = rest - col * row
    return inverse


def pack_moments(scratch, parts):
    total = None
    for i, part in enumerate(parts):
        width = part.shape[1]
        scratch[...] = jnp.zeros(scratch.shape, F4)
        scratch[:, 0:width] = part
        placed = scratch[...]
        if i:
            placed = pltpu.roll(placed, i * width, 1)
        total = placed if total is None else total + placed
    used = sum(part.shape[1] for part in parts)
    first = total.astype(BF).astype(F4)
    left = total - first
    second = left.astype(BF).astype(F4)
    third = (left - second).astype(BF).astype(F4)
    packed = first + pltpu.roll(second, used, 1) + pltpu.roll(third, 2 * used, 1)
    return packed.astype(BF)


def unpack_moments(total, used):
    width = total.shape[1]
    return total + pltpu.roll(total, width - used, 1) + pltpu.roll(total, width - 2 * used, 1)


def store_for_all(out_ref, dens_halves, moments):
    pairs, _, tiles, blocks = out_ref.shape[:4]

    def one(g, carry):
        for h in range(2):
            for t in range(tiles):
                for k in range(blocks - 1):
                    out_ref[g, h, t, k] = dens_halves[k][h]
                out_ref[g, h, t, blocks - 1] = moments
        return carry

    lax.fori_loop(0, pairs, one, 0, unroll=True)


def project(block, coeff):
    high, low = split2(block)
    both = mm(jnp.concatenate([high, low], 0), coeff, NT)
    v = block.shape[0]
    total = both[:v] + both[v:]
    half = total.shape[1] // 2
    return [total[:, :half].astype(BF), total[:, half:].astype(BF)]


def start_kernel(x_hbm, e_hbm, c_hbm, s_hbm, out_ref, x_ref, e_ref, c_ref, s_ref, sems, c_sems, scratch):
    local_k, v, _ = x_ref.shape
    copies = [
        pltpu.make_async_copy(x_hbm, x_ref, sems.at[0]),
        pltpu.make_async_copy(e_hbm, e_ref, sems.at[1]),
    ]
    c_copies = [pltpu.make_async_copy(c_hbm.at[k], c_ref.at[k], c_sems.at[k]) for k in range(local_k)]
    screen_copy = pltpu.make_async_copy(s_hbm, s_ref, sems.at[2])
    for copy in copies + c_copies + [screen_copy]:
        copy.start()
    for copy in copies:
        copy.wait()
    halves = []
    moments = None
    for k in range(local_k):
        x = x_ref[k]
        xh, xl = split2(x)
        eh, el = split2(x * e_ref[k : k + 1, :])
        big = mm(jnp.concatenate([xh, xl], 0), jnp.concatenate([xh, eh], 0), NT)
        small = mm(xh, jnp.concatenate([xl, el], 0), NT)
        part = big[:v] + big[v:] + small
        moments = part if moments is None else moments + part
        c_copies[k].wait()
        halves.append(project(x, c_ref[k]))
    store_for_all(out_ref, halves, pack_moments(scratch, [moments]))
    screen_copy.wait()


def gather_kernel(mine_ref, dens_ref, moments_ref):
    groups, tiles, blocks = mine_ref.shape[:3]
    local_k = blocks - 1
    moments = None
    for g in range(groups):
        for k in range(local_k):
            total = mine_ref[g, 0, k].astype(F4)
            for t in range(1, tiles):
                total = total + mine_ref[g, t, k].astype(F4)
            dens_ref[g * local_k + k] = total
        for t in range(tiles):
            block = mine_ref[g, t, local_k].astype(F4)
            moments = block if moments is None else moments + block
    moments_ref[...] = moments


class Tasks:
    def __init__(self, assign_hbm, ranks_hbm, screen_ref, scratch):
        self.assign, self.ranks, self.acc, self.dens_b, self.sems, self.small = scratch
        self.screen = screen_ref
        self.core = lax.axis_index("grp") % 2
        self.heads = [
            pltpu.make_async_copy(assign_hbm, self.assign, self.sems.at[0]),
            pltpu.make_async_copy(ranks_hbm, self.ranks, self.sems.at[1]),
        ]
        for copy in self.heads:
            copy.start()
        self.acc[...] = jnp.zeros(self.acc.shape, F4)

    def set_dens(self, dens_ref, which, k, dens):
        slot = (self.core + which) % 2
        dens_ref[slot, k] = dens
        self.dens_b[slot, k] = dens.astype(BF)

    def run(self, dens_ref, keep_ref, send_ref, coupled_ref):
        total_k, v, half = self.dens_b.shape[1:]
        lane = lax.broadcasted_iota(jnp.int32, (v, 2 * half), 1)
        for copy in self.heads:
            copy.wait()

        def one(t, carry):
            pair = self.assign[t]
            row = pair // total_k
            col = pair - row * total_k
            keep = lane < self.ranks[row, col]
            vec = jnp.concatenate([self.dens_b[0, col], self.dens_b[1, col]], 1)
            vec = jnp.where(keep, vec, 0.0).astype(BF)
            term = jnp.where(keep, mm(vec, self.screen[t], NT), 0.0)
            self.acc[0, row] = self.acc[0, row] + term[:, :half]
            self.acc[1, row] = self.acc[1, row] + term[:, half:]
            return carry

        lax.fori_loop(0, self.screen.shape[0], one, 0, unroll=True)
        total = None
        for k in range(total_k):
            for h in range(2):
                rh, rl = split2(self.acc[h, k])
                dh, dl = split2(dens_ref[h, k])
                big = mm(jnp.concatenate([rh, rl], 0), dh, NT)
                part = big[:v] + big[v:] + mm(rh, dl, NT)
                total = part if total is None else total + part
            keep_ref[k] = self.acc[self.core, k]
            send_ref[k] = self.acc[1 - self.core, k]
        coupled_ref[...] = pack_moments(self.small, [total])


def pad_small(scratch, small):
    scratch[...] = jnp.zeros(scratch.shape, F4)
    scratch[:, 0 : small.shape[1]] = small
    return scratch[...]


def first_tasks_kernel(assign_hbm, ranks_hbm, screen_ref, mine_ref, other_ref, moments_ref,
                       keep_ref, send_ref, coupled_ref, dens_ref, small_ref, *scratch, count):
    tasks = Tasks(assign_hbm, ranks_hbm, screen_ref, scratch)
    v = mine_ref.shape[1]
    moments = unpack_moments(moments_ref[...], 2 * v)
    inverse = inverse_cholesky(moments[:, 0:v] / count)
    for k in range(mine_ref.shape[0]):
        for which, ref in ((0, mine_ref), (1, other_ref)):
            tasks.set_dens(dens_ref, which, k, apply_small(inverse, ref[k]))
    tasks.run(dens_ref, keep_ref, send_ref, coupled_ref)
    weighted = moments[:, v : 2 * v] / count
    diag = exact(exact(inverse, weighted, NN), inverse, NT)
    small_ref[0] = pad_small(tasks.small, inverse)
    small_ref[1] = pad_small(tasks.small, diag)


def next_tasks_kernel(assign_hbm, ranks_hbm, screen_ref, mine_ref, other_ref, moments_ref,
                      prev_dens_ref, prev_small_ref, keep_ref, send_ref, coupled_ref, small_ref,
                      dens_ref, *scratch, count):
    tasks = Tasks(assign_hbm, ranks_hbm, screen_ref, scratch)
    v = mine_ref.shape[1]
    moments = unpack_moments(moments_ref[...], 4 * v) / count
    pp = moments[:, 0:v]
    mix = moments[:, v : 2 * v]
    inverse = inverse_cholesky(pp - exact(mix, mix, NT))
    both = apply_small(inverse, mix)
    for k in range(mine_ref.shape[0]):
        for which, ref in ((0, mine_ref), (1, other_ref)):
            dens = apply_small(inverse, ref[k])
            dens = dens - apply_small(both, prev_dens_ref[(tasks.core + which) % 2, k])
            tasks.set_dens(dens_ref, which, k, dens)
    tasks.run(dens_ref, keep_ref, send_ref, coupled_ref)
    rp = moments[:, 2 * v : 3 * v]
    rv = moments[:, 3 * v : 4 * v]
    prev_diag = prev_small_ref[1][:, 0:v]
    weighted = rp - exact(rv, mix, NT) - exact(mix, rv, NT) + exact(exact(mix, prev_diag, NN), mix, NT)
    diag = exact(exact(inverse, weighted, NN), inverse, NT)
    small_ref[0] = pad_small(tasks.small, inverse)
    small_ref[1] = pad_small(tasks.small, diag)
    small_ref[2] = pad_small(tasks.small, both)


def rows_kernel(keep_ref, recv_ref, coupled_ref, out_ref):
    groups, tiles, blocks = out_ref.shape[:3]
    local_k = blocks - 1
    for g in range(groups):
        for k in range(local_k):
            rows = (keep_ref[g * local_k + k] + recv_ref[g * local_k + k]).astype(BF)
            for t in range(tiles):
                out_ref[g, t, k] = rows
        for t in range(tiles):
            out_ref[g, t, local_k] = coupled_ref[...]


def sum_rows(recv_ref):
    pairs, _, tiles, blocks, v, _ = recv_ref.shape

    def summed(block, halves):
        total = None
        for g in range(pairs):
            for h in halves:
                for t in range(tiles):
                    part = recv_ref[g, h, t, block].astype(F4)
                    total = part if total is None else total + part
        return total

    rows = []
    for k in range(blocks - 1):
        rows.append(jnp.concatenate([summed(k, (0,)), summed(k, (1,))], 1).astype(BF))
    return rows, unpack_moments(summed(blocks - 1, (0, 1)), v)[:, 0:v]


def after_first_kernel(recv_ref, x_ref, e_ref, c_ref, small_ref, out_ref, v_ref, p_ref, ray_ref, scratch, *, count):
    local_k, v, _ = x_ref.shape
    rows, coupled_part = sum_rows(recv_ref)
    inverse = small_ref[0][:, 0:v]
    ray = small_ref[1][:, 0:v] + coupled_part / count
    ray_ref[...] = pad_small(scratch, ray)
    halves = []
    moments = None
    for k in range(local_k):
        basis = apply_small(inverse, x_ref[k])
        energy = e_ref[k : k + 1, :]
        sigma = energy * basis + mm(rows[k], c_ref[k], NN)
        residual = sigma - apply_small(ray, basis)
        precond = residual / energy
        v_ref[k] = basis
        p_ref[k] = precond
        halves.append(project(precond, c_ref[k]))
        bh, bl = split2(basis)
        rh, rl = split2(residual)
        ph, pw = split2(precond)
        big = mm(jnp.concatenate([ph, rh, pw, rl], 0), jnp.concatenate([ph, bh], 0), NT)
        small = mm(jnp.concatenate([ph, rh], 0), jnp.concatenate([pw, bl], 0), NT)
        part = big[: 2 * v] + big[2 * v :] + small
        moments = part if moments is None else moments + part
    store_for_all(out_ref, halves, pack_moments(scratch, [moments[:v], moments[v:]]))


def last_rows_kernel(recv_ref, v_ref, p_ref, e_ref, c_ref, small_ref, out_ref, res_ref, basis_ref, q_ref, ray_ref, scratch, *, count):
    local_k, v, _ = v_ref.shape
    rows, coupled_part = sum_rows(recv_ref)
    inverse = small_ref[0][:, 0:v]
    both = small_ref[2][:, 0:v]
    ray = small_ref[1][:, 0:v] + coupled_part / count
    ray_ref[...] = pad_small(scratch, ray)
    moments = None
    for k in range(local_k):
        basis = apply_small(inverse, p_ref[k]) - apply_small(both, v_ref[k])
        energy = e_ref[k : k + 1, :]
        sigma = energy * basis + mm(rows[k], c_ref[k], NN)
        residual = sigma - apply_small(ray, basis)
        precond = residual / energy
        res_ref[k] = residual
        basis_ref[k] = basis
        q_ref[k] = precond
        bh, bl = split2(basis)
        ph, pw = split2(precond)
        big = mm(jnp.concatenate([ph, pw], 0), jnp.concatenate([ph, bh], 0), NT)
        part = big[:v] + big[v:] + mm(ph, jnp.concatenate([pw, bl], 0), NT)
        moments = part if moments is None else moments + part
    packed = pack_moments(scratch, [moments])
    for d in range(out_ref.shape[0]):
        out_ref[d] = packed


def finish_kernel(recv_ref, q_ref, b_ref, ray0_ref, ray1_ref, out_ref, ray_ref, *, count):
    local_k, v, _ = q_ref.shape
    total = recv_ref[0].astype(F4)
    for d in range(1, recv_ref.shape[0]):
        total = total + recv_ref[d].astype(F4)
    moments = unpack_moments(total, 2 * v) / count
    mix = moments[:, v : 2 * v]
    inverse = inverse_cholesky(moments[:, 0:v] - exact(mix, mix, NT))
    both = exact(inverse, mix, NN)
    for k in range(local_k):
        out_ref[k] = apply_small(inverse, q_ref[k]) - apply_small(both, b_ref[k])
    ray_ref[0] = ray0_ref[:, 0:v].T
    ray_ref[1] = ray1_ref[:, 0:v].T


VM = pl.BlockSpec(memory_space=pltpu.VMEM)
ANY = pl.BlockSpec(memory_space=pltpu.HBM)


def call(body, outs, ins, args, scratch=(), cost=None):
    args = [
        pltpu.with_memory_space_constraint(arg, pltpu.HBM) if spec is ANY else arg
        for arg, spec in zip(args, ins)
    ]
    return pl.pallas_call(
        body,
        out_shape=outs,
        in_specs=ins,
        out_specs=jax.tree.map(lambda _: VM, outs),
        scratch_shapes=scratch,
        compiler_params=pltpu.CompilerParams(vmem_limit_bytes=16 << 20),
        cost_estimate=cost,
    )(*args)


def per_device(coeff, energy, ranks, assign, screen, initial):
    groups = lax.axis_size("grp")
    tiles = lax.axis_size("tile")
    devices = groups * tiles
    pairs = groups // 2
    local_k, v, width = initial.shape
    levels = coeff.shape[1]
    half = levels // 2
    total_k = local_k * groups
    count = float(total_k * width * tiles)
    axes = ("grp", "tile")
    swap = [(g, g ^ 1) for g in range(groups)]
    sds = jax.ShapeDtypeStruct
    small_scratch = pltpu.VMEM((v, half), F4)
    dma = pltpu.SemaphoreType.DMA
    half_shape = sds((total_k, v, half), F4)

    def exchange(blocks, shape):
        sent = blocks.reshape((devices,) + blocks.shape[-3:])
        return lax.all_to_all(sent, axes, 0, 0, tiled=True).reshape(shape + sent.shape[1:])

    def to_all(blocks):
        got = exchange(blocks, (groups, tiles))
        mine, moments = call(gather_kernel, (half_shape, sds((v, half), F4)), [VM], (got,))
        return mine, lax.ppermute(mine, "grp", swap), moments

    def to_owner(keep, send, coupled):
        recv = lax.ppermute(send, "grp", swap)
        shape = sds((groups, tiles, local_k + 1, v, half), BF)
        out = call(rows_kernel, shape, [VM] * 3, (keep, recv, coupled))
        return exchange(out, (pairs, 2, tiles))

    all_shape = sds((pairs, 2, tiles, local_k + 1, v, half), BF)
    task_outs = (half_shape, half_shape, sds((v, half), BF))
    dens_shape = (2, total_k, v, half)
    task_scratch = (
        pltpu.SMEM(assign.shape, jnp.int32),
        pltpu.SMEM(ranks.shape, jnp.int32),
        pltpu.VMEM((2, total_k, v, half), F4),
        pltpu.VMEM((2, total_k, v, half), BF),
        dma((2,)),
        small_scratch,
    )
    flat = sds((local_k, v, width), F4)
    ray_shape = sds((v, half), F4)

    inputs = (initial, energy, coeff, screen)
    sent, initial, energy, coeff, screen = call(
        start_kernel,
        (all_shape,) + tuple(sds(a.shape, a.dtype) for a in inputs),
        [ANY] * 4,
        inputs,
        (
            dma((3,)),
            dma((local_k,)),
            small_scratch,
        ),
    )
    mine, other, moments = to_all(sent)
    keep, send, coupled, dens, small = call(
        functools.partial(first_tasks_kernel, count=count),
        task_outs + (sds(dens_shape, F4), sds((2, v, half), F4)),
        [ANY, ANY] + [VM] * 4,
        (assign, ranks, screen, mine, other, moments),
        task_scratch,
    )
    got = to_owner(keep, send, coupled)
    sent, basis, precond, ray0 = call(
        functools.partial(after_first_kernel, count=count),
        (all_shape, flat, flat, ray_shape),
        [VM] * 5,
        (got, initial, energy, coeff, small),
        (small_scratch,),
    )
    mine, other, moments = to_all(sent)
    keep, send, coupled, small = call(
        functools.partial(next_tasks_kernel, count=count),
        task_outs + (sds((3, v, half), F4),),
        [ANY, ANY] + [VM] * 6,
        (assign, ranks, screen, mine, other, moments, dens, small),
        (pltpu.VMEM(dens_shape, F4),) + task_scratch,
    )
    got = to_owner(keep, send, coupled)
    sent, residual, basis, precond, ray1 = call(
        functools.partial(last_rows_kernel, count=count),
        (sds((devices, v, half), BF), flat, flat, flat, ray_shape),
        [VM] * 6,
        (got, basis, precond, energy, coeff, small),
        (small_scratch,),
    )
    got = lax.all_to_all(sent, axes, 0, 0, tiled=True)
    basis, rayleigh = call(
        functools.partial(finish_kernel, count=count),
        (flat, sds((2, v, v), F4)),
        [VM] * 5,
        (got, precond, basis, ray0, ray1),
    )
    return (rayleigh, basis, residual)


def solution(mesh):
    placed = (
        P("grp", None, "tile"),
        P("grp", "tile"),
        P(),
        P(("grp", "tile")),
        P(("grp", "tile"), None, None),
        P("grp", None, "tile"),
    )
    return jax.shard_map(
        per_device,
        mesh=mesh,
        in_specs=placed,
        out_specs=(P(), P("grp", None, "tile"), P("grp", None, "tile")),
        check_vma=False,
    )
```

```python
import functools

import jax
import jax.numpy as jnp
from jax import lax
from jax.experimental import pallas as pl
from jax.experimental.pallas import tpu as pltpu
from jax.sharding import PartitionSpec as P

ITERS = 2
LANES = 128
BF = jnp.bfloat16
F4 = jnp.float32
NT = (((1,), (1,)), ((), ()))
NN = (((1,), (0,)), ((), ()))


def split2(x):
    high = x.astype(BF)
    return high, (x - high.astype(F4)).astype(BF)


def mm(left, right, dims):
    return lax.dot_general(left, right, dims, preferred_element_type=F4)


def exact(left, right, dims):
    return lax.dot_general(
        left, right, dims, preferred_element_type=F4, precision=lax.Precision.HIGHEST
    )


def apply_small(weights, block):
    total = weights[:, 0:1] * block[0:1, :]
    for m in range(1, weights.shape[1]):
        total = total + weights[:, m : m + 1] * block[m : m + 1, :]
    return total


def inverse_cholesky(gram):
    v = gram.shape[0]
    row_id = lax.broadcasted_iota(jnp.int32, (v, v), 0)
    col_id = lax.broadcasted_iota(jnp.int32, (v, v), 1)
    inverse = (row_id == col_id).astype(F4)
    rest = gram
    for j in range(v):
        scale = 1.0 / jnp.sqrt(rest[j : j + 1, j : j + 1])
        col = rest[:, j : j + 1] * scale
        row = rest[j : j + 1, :] * scale
        inv_row = inverse[j : j + 1, :] * scale
        below = jnp.where(row_id[:, 0:1] > j, col, 0.0)
        inverse = jnp.where(row_id == j, inv_row, inverse - below * inv_row)
        if j + 1 < v:
            rest = rest - col * row
    return inverse


def pack_moments(scratch, parts):
    total = None
    for i, part in enumerate(parts):
        width = part.shape[1]
        scratch[...] = jnp.zeros(scratch.shape, F4)
        scratch[:, 0:width] = part
        placed = scratch[...]
        if i:
            placed = pltpu.roll(placed, i * width, 1)
        total = placed if total is None else total + placed
    used = sum(part.shape[1] for part in parts)
    first = total.astype(BF).astype(F4)
    left = total - first
    second = left.astype(BF).astype(F4)
    third = (left - second).astype(BF).astype(F4)
    packed = first + pltpu.roll(second, used, 1) + pltpu.roll(third, 2 * used, 1)
    return packed.astype(BF)


def unpack_moments(total, used):
    width = total.shape[1]
    return total + pltpu.roll(total, width - used, 1) + pltpu.roll(total, width - 2 * used, 1)


def store_for_all(out_ref, dens_halves, moments):
    pairs, _, tiles, blocks = out_ref.shape[:4]

    def one(g, carry):
        for h in range(2):
            for t in range(tiles):
                for k in range(blocks - 1):
                    out_ref[g, h, t, k] = dens_halves[k][h]
                out_ref[g, h, t, blocks - 1] = moments
        return carry

    lax.fori_loop(0, pairs, one, 0, unroll=True)


def project(block, coeff):
    high, low = split2(block)
    both = mm(jnp.concatenate([high, low], 0), coeff, NT)
    v = block.shape[0]
    total = both[:v] + both[v:]
    half = total.shape[1] // 2
    return [total[:, :half].astype(BF), total[:, half:].astype(BF)]


def start_kernel(x_hbm, e_hbm, c_hbm, s_hbm, out_ref, x_ref, e_ref, c_ref, s_ref, sems, c_sems, scratch):
    local_k, v, _ = x_ref.shape
    copies = [
        pltpu.make_async_copy(x_hbm, x_ref, sems.at[0]),
        pltpu.make_async_copy(e_hbm, e_ref, sems.at[1]),
    ]
    c_copies = [pltpu.make_async_copy(c_hbm.at[k], c_ref.at[k], c_sems.at[k]) for k in range(local_k)]
    screen_copy = pltpu.make_async_copy(s_hbm, s_ref, sems.at[2])
    for copy in copies + c_copies + [screen_copy]:
        copy.start()
    for copy in copies:
        copy.wait()
    halves = []
    moments = None
    for k in range(local_k):
        x = x_ref[k]
        xh, xl = split2(x)
        eh, el = split2(x * e_ref[k : k + 1, :])
        big = mm(jnp.concatenate([xh, xl], 0), jnp.concatenate([xh, eh], 0), NT)
        small = mm(xh, jnp.concatenate([xl, el], 0), NT)
        part = big[:v] + big[v:] + small
        moments = part if moments is None else moments + part
        c_copies[k].wait()
        halves.append(project(x, c_ref[k]))
    store_for_all(out_ref, halves, pack_moments(scratch, [moments]))
    screen_copy.wait()


def gather_kernel(mine_ref, dens_ref, moments_ref):
    groups, tiles, blocks = mine_ref.shape[:3]
    local_k = blocks - 1
    moments = None
    for g in range(groups):
        for k in range(local_k):
            total = mine_ref[g, 0, k].astype(F4)
            for t in range(1, tiles):
                total = total + mine_ref[g, t, k].astype(F4)
            dens_ref[g * local_k + k] = total
        for t in range(tiles):
            block = mine_ref[g, t, local_k].astype(F4)
            moments = block if moments is None else moments + block
    moments_ref[...] = moments


def pad_small(scratch, small):
    scratch[...] = jnp.zeros(scratch.shape, F4)
    scratch[:, 0 : small.shape[1]] = small
    return scratch[...]


def first_factor_kernel(moments_ref, small_ref, scratch, *, count):
    v = moments_ref.shape[0]
    moments = unpack_moments(moments_ref[...], 2 * v)
    small_ref[0] = pad_small(scratch, inverse_cholesky(moments[:, 0:v] / count))


def next_factor_kernel(moments_ref, small_ref, scratch, *, count):
    v = moments_ref.shape[0]
    moments = unpack_moments(moments_ref[...], 4 * v) / count
    mix = moments[:, v : 2 * v]
    inverse = inverse_cholesky(moments[:, 0:v] - exact(mix, mix, NT))
    small_ref[0] = pad_small(scratch, inverse)
    small_ref[1] = pad_small(scratch, apply_small(inverse, mix))


def own_core():
    return lax.axis_index("grp") % 2


def tasks_kernel(assign_hbm, ranks_hbm, screen_ref, mine_ref, other_ref, small_ref, *refs):
    prev_dens_ref = None
    if len(refs) > 8:
        prev_dens_ref, refs = refs[0], refs[1:]
    keep_ref, send_ref, dens_ref, assign_ref, ranks_ref, acc_ref, terms_ref, sems = refs
    heads = [
        pltpu.make_async_copy(assign_hbm, assign_ref, sems.at[0]),
        pltpu.make_async_copy(ranks_hbm, ranks_ref, sems.at[1]),
    ]
    for copy in heads:
        copy.start()
    acc_ref[...] = jnp.zeros(acc_ref.shape, F4)
    core = own_core()
    total_k, v, half = mine_ref.shape
    inverse = small_ref[0][:, 0:v]
    for k in range(total_k):
        for which, ref in ((0, mine_ref), (1, other_ref)):
            slot = (core + which) % 2
            dens = apply_small(inverse, ref[k])
            if prev_dens_ref is not None:
                dens = dens - apply_small(small_ref[1][:, 0:v], prev_dens_ref[slot, k])
            dens_ref[slot, k] = dens
            terms_ref[slot, k] = jnp.concatenate(split2(dens), 0)
    lane = lax.broadcasted_iota(jnp.int32, (2 * v, 2 * half), 1)
    for copy in heads:
        copy.wait()

    def one(t, carry):
        pair = assign_ref[t]
        row = pair // total_k
        col = pair - row * total_k
        keep = lane < ranks_ref[row, col]
        vec = jnp.concatenate([terms_ref[0, col], terms_ref[1, col]], 1)
        vec = jnp.where(keep, vec, jnp.zeros_like(vec))
        term = mm(vec, screen_ref[t], NT)
        term = jnp.where(keep[:v], term[:v] + term[v:], 0.0)
        acc_ref[0, row] = acc_ref[0, row] + term[:, :half]
        acc_ref[1, row] = acc_ref[1, row] + term[:, half:]
        return carry

    lax.fori_loop(0, screen_ref.shape[0], one, 0, unroll=True)
    for k in range(total_k):
        keep_ref[k] = acc_ref[core, k]
        send_ref[k] = acc_ref[1 - core, k]


def coupled_part(keep_ref, send_ref, dens_ref):
    total_k, v, _ = keep_ref.shape
    core = own_core()
    total = None
    for k in range(total_k):
        for which, ref in ((0, keep_ref), (1, send_ref)):
            rh, rl = split2(ref[k])
            dh, dl = split2(dens_ref[(core + which) % 2, k])
            big = mm(jnp.concatenate([rh, rl], 0), dh, NT)
            part = big[:v] + big[v:] + mm(rh, dl, NT)
            total = part if total is None else total + part
    return total


def first_coupled_kernel(keep_ref, send_ref, dens_ref, moments_ref, small_ref, coupled_ref, diag_ref, scratch, *, count):
    v = moments_ref.shape[0]
    coupled_ref[...] = pack_moments(scratch, [coupled_part(keep_ref, send_ref, dens_ref)])
    weighted = unpack_moments(moments_ref[...], 2 * v)[:, v : 2 * v] / count
    inverse = small_ref[0][:, 0:v]
    diag_ref[...] = pad_small(scratch, exact(exact(inverse, weighted, NN), inverse, NT))


def next_coupled_kernel(keep_ref, send_ref, dens_ref, moments_ref, small_ref, prev_diag_ref, coupled_ref, diag_ref, scratch, *, count):
    v = moments_ref.shape[0]
    coupled_ref[...] = pack_moments(scratch, [coupled_part(keep_ref, send_ref, dens_ref)])
    moments = unpack_moments(moments_ref[...], 4 * v) / count
    mix = moments[:, v : 2 * v]
    rp = moments[:, 2 * v : 3 * v]
    rv = moments[:, 3 * v : 4 * v]
    mixed = exact(exact(mix, prev_diag_ref[:, 0:v], NN), mix, NT)
    weighted = rp - exact(rv, mix, NT) - exact(mix, rv, NT) + mixed
    inverse = small_ref[0][:, 0:v]
    diag_ref[...] = pad_small(scratch, exact(exact(inverse, weighted, NN), inverse, NT))


def rows_kernel(keep_ref, recv_ref, coupled_ref, out_ref):
    groups, tiles, blocks = out_ref.shape[:3]
    local_k = blocks - 1
    for g in range(groups):
        for k in range(local_k):
            rows = (keep_ref[g * local_k + k] + recv_ref[g * local_k + k]).astype(BF)
            for t in range(tiles):
                out_ref[g, t, k] = rows
        for t in range(tiles):
            out_ref[g, t, local_k] = coupled_ref[...]


def sum_rows(recv_ref):
    pairs, _, tiles, blocks, v, _ = recv_ref.shape

    def summed(block, halves):
        total = None
        for g in range(pairs):
            for h in halves:
                for t in range(tiles):
                    part = recv_ref[g, h, t, block].astype(F4)
                    total = part if total is None else total + part
        return total

    rows = []
    for k in range(blocks - 1):
        rows.append(jnp.concatenate([summed(k, (0,)), summed(k, (1,))], 1))
    return rows, unpack_moments(summed(blocks - 1, (0, 1)), v)[:, 0:v]


def expand(rows, coeff):
    both = mm(jnp.concatenate(split2(rows), 0), coeff, NN)
    v = rows.shape[0]
    return both[:v] + both[v:]


def after_first_kernel(recv_ref, x_ref, e_ref, c_ref, small_ref, diag_ref, out_ref, v_ref, p_ref, ray_ref, scratch, *, count):
    local_k, v, _ = x_ref.shape
    rows, coupled = sum_rows(recv_ref)
    inverse = small_ref[0][:, 0:v]
    ray = diag_ref[:, 0:v] + coupled / count
    ray_ref[...] = pad_small(scratch, ray)
    halves = []
    moments = None
    for k in range(local_k):
        basis = apply_small(inverse, x_ref[k])
        energy = e_ref[k : k + 1, :]
        sigma = energy * basis + expand(rows[k], c_ref[k])
        residual = sigma - apply_small(ray, basis)
        precond = residual / energy
        v_ref[k] = basis
        p_ref[k] = precond
        halves.append(project(precond, c_ref[k]))
        bh, bl = split2(basis)
        rh, rl = split2(residual)
        ph, pw = split2(precond)
        big = mm(jnp.concatenate([ph, rh, pw, rl], 0), jnp.concatenate([ph, bh], 0), NT)
        small = mm(jnp.concatenate([ph, rh], 0), jnp.concatenate([pw, bl], 0), NT)
        part = big[: 2 * v] + big[2 * v :] + small
        moments = part if moments is None else moments + part
    store_for_all(out_ref, halves, pack_moments(scratch, [moments[:v], moments[v:]]))


def last_rows_kernel(recv_ref, v_ref, p_ref, e_ref, c_ref, small_ref, diag_ref, out_ref, res_ref, basis_ref, q_ref, ray_ref, scratch, *, count):
    local_k, v, _ = v_ref.shape
    rows, coupled = sum_rows(recv_ref)
    inverse = small_ref[0][:, 0:v]
    both = small_ref[1][:, 0:v]
    ray = diag_ref[:, 0:v] + coupled / count
    ray_ref[...] = pad_small(scratch, ray)
    moments = None
    for k in range(local_k):
        basis = apply_small(inverse, p_ref[k]) - apply_small(both, v_ref[k])
        energy = e_ref[k : k + 1, :]
        sigma = energy * basis + expand(rows[k], c_ref[k])
        residual = sigma - apply_small(ray, basis)
        precond = residual / energy
        res_ref[k] = residual
        basis_ref[k] = basis
        q_ref[k] = precond
        bh, bl = split2(basis)
        ph, pw = split2(precond)
        big = mm(jnp.concatenate([ph, pw], 0), jnp.concatenate([ph, bh], 0), NT)
        part = big[:v] + big[v:] + mm(ph, jnp.concatenate([pw, bl], 0), NT)
        moments = part if moments is None else moments + part
    packed = pack_moments(scratch, [moments])
    for d in range(out_ref.shape[0]):
        out_ref[d] = packed


def finish_kernel(recv_ref, q_ref, b_ref, ray0_ref, ray1_ref, out_ref, ray_ref, *, count):
    local_k, v, _ = q_ref.shape
    total = recv_ref[0].astype(F4)
    for d in range(1, recv_ref.shape[0]):
        total = total + recv_ref[d].astype(F4)
    moments = unpack_moments(total, 2 * v) / count
    mix = moments[:, v : 2 * v]
    inverse = inverse_cholesky(moments[:, 0:v] - exact(mix, mix, NT))
    both = exact(inverse, mix, NN)
    for k in range(local_k):
        out_ref[k] = apply_small(inverse, q_ref[k]) - apply_small(both, b_ref[k])
    ray_ref[0] = ray0_ref[:, 0:v].T
    ray_ref[1] = ray1_ref[:, 0:v].T


VM = pl.BlockSpec(memory_space=pltpu.VMEM)
ANY = pl.BlockSpec(memory_space=pltpu.HBM)


def call(body, outs, ins, args, scratch=(), cost=None):
    args = [
        pltpu.with_memory_space_constraint(arg, pltpu.HBM) if spec is ANY else arg
        for arg, spec in zip(args, ins)
    ]
    return pl.pallas_call(
        body,
        out_shape=outs,
        in_specs=ins,
        out_specs=jax.tree.map(lambda _: VM, outs),
        scratch_shapes=scratch,
        compiler_params=pltpu.CompilerParams(vmem_limit_bytes=16 << 20),
        cost_estimate=cost,
    )(*args)


def per_device(coeff, energy, ranks, assign, screen, initial):
    groups = lax.axis_size("grp")
    tiles = lax.axis_size("tile")
    devices = groups * tiles
    pairs = groups // 2
    local_k, v, width = initial.shape
    levels = coeff.shape[1]
    half = levels // 2
    total_k = local_k * groups
    count = float(total_k * width * tiles)
    axes = ("grp", "tile")
    swap = [(g, g ^ 1) for g in range(groups)]
    sds = jax.ShapeDtypeStruct
    small_scratch = pltpu.VMEM((v, half), F4)
    dma = pltpu.SemaphoreType.DMA
    half_shape = sds((total_k, v, half), F4)
    small_shape = sds((v, half), F4)

    def exchange(blocks, shape):
        sent = blocks.reshape((devices,) + blocks.shape[-3:])
        return lax.all_to_all(sent, axes, 0, 0, tiled=True).reshape(shape + sent.shape[1:])

    def to_all(blocks):
        got = exchange(blocks, (groups, tiles))
        mine, moments = call(gather_kernel, (half_shape, small_shape), [VM], (got,))
        return mine, lax.ppermute(mine, "grp", swap), moments

    def to_owner(keep, recv, coupled):
        shape = sds((groups, tiles, local_k + 1, v, half), BF)
        out = call(rows_kernel, shape, [VM] * 3, (keep, recv, coupled))
        return exchange(out, (pairs, 2, tiles))

    def factor(body, matrices, moments):
        shape = sds((matrices, v, half), F4)
        return call(functools.partial(body, count=count), shape, [VM], (moments,), (small_scratch,))

    def run_tasks(*args):
        dens_shape = (2, total_k, v, half)
        return call(
            tasks_kernel,
            (half_shape, half_shape, sds(dens_shape, F4)),
            [ANY, ANY] + [VM] * (len(args) + 1),
            (assign, ranks, screen) + args,
            (
                pltpu.SMEM(assign.shape, jnp.int32),
                pltpu.SMEM(ranks.shape, jnp.int32),
                pltpu.VMEM(dens_shape, F4),
                pltpu.VMEM((2, total_k, 2 * v, half), BF),
                dma((2,)),
            ),
        )

    def couple(body, *args):
        outs = (sds((v, half), BF), small_shape)
        return call(functools.partial(body, count=count), outs, [VM] * len(args), args, (small_scratch,))

    all_shape = sds((pairs, 2, tiles, local_k + 1, v, half), BF)
    flat = sds((local_k, v, width), F4)

    inputs = (initial, energy, coeff, screen)
    sent, initial, energy, coeff, screen = call(
        start_kernel,
        (all_shape,) + tuple(sds(a.shape, a.dtype) for a in inputs),
        [ANY] * 4,
        inputs,
        (dma((3,)), dma((local_k,)), small_scratch),
    )
    mine, other, moments = to_all(sent)
    small = factor(first_factor_kernel, 1, moments)
    keep, send, dens = run_tasks(mine, other, small)
    recv = lax.ppermute(send, "grp", swap)
    coupled, diag = couple(first_coupled_kernel, keep, send, dens, moments, small)
    got = to_owner(keep, recv, coupled)
    sent, basis, precond, ray0 = call(
        functools.partial(after_first_kernel, count=count),
        (all_shape, flat, flat, small_shape),
        [VM] * 6,
        (got, initial, energy, coeff, small, diag),
        (small_scratch,),
    )
    mine, other, moments = to_all(sent)
    small = factor(next_factor_kernel, 2, moments)
    keep, send, dens = run_tasks(mine, other, small, dens)
    recv = lax.ppermute(send, "grp", swap)
    coupled, diag = couple(next_coupled_kernel, keep, send, dens, moments, small, diag)
    got = to_owner(keep, recv, coupled)
    sent, residual, basis, precond, ray1 = call(
        functools.partial(last_rows_kernel, count=count),
        (sds((devices, v, half), BF), flat, flat, flat, small_shape),
        [VM] * 7,
        (got, basis, precond, energy, coeff, small, diag),
        (small_scratch,),
    )
    got = lax.all_to_all(sent, axes, 0, 0, tiled=True)
    basis, rayleigh = call(
        functools.partial(finish_kernel, count=count),
        (flat, sds((2, v, v), F4)),
        [VM] * 5,
        (got, precond, basis, ray0, ray1),
    )
    return (rayleigh, basis, residual)


def solution(mesh):
    placed = (
        P("grp", None, "tile"),
        P("grp", "tile"),
        P(),
        P(("grp", "tile")),
        P(("grp", "tile"), None, None),
        P("grp", None, "tile"),
    )
    return jax.shard_map(
        per_device,
        mesh=mesh,
        in_specs=placed,
        out_specs=(P(), P("grp", None, "tile"), P("grp", None, "tile")),
        check_vma=False,
    )
```

```python
import functools

import jax
import jax.numpy as jnp
from jax import lax
from jax.experimental import pallas as pl
from jax.experimental.pallas import tpu as pltpu
from jax.sharding import PartitionSpec as P

ITERS = 2
LANES = 128
BF = jnp.bfloat16
F4 = jnp.float32
NT = (((1,), (1,)), ((), ()))
NN = (((1,), (0,)), ((), ()))


def split2(x):
    high = x.astype(BF)
    return high, (x - high.astype(F4)).astype(BF)


def mm(left, right, dims):
    return lax.dot_general(left, right, dims, preferred_element_type=F4)


def exact(left, right, dims):
    return lax.dot_general(
        left, right, dims, preferred_element_type=F4, precision=lax.Precision.HIGHEST
    )


def apply_small(weights, block):
    total = weights[:, 0:1] * block[0:1, :]
    for m in range(1, weights.shape[1]):
        total = total + weights[:, m : m + 1] * block[m : m + 1, :]
    return total


def inverse_cholesky(gram):
    v = gram.shape[0]
    row_id = lax.broadcasted_iota(jnp.int32, (v, v), 0)
    col_id = lax.broadcasted_iota(jnp.int32, (v, v), 1)
    inverse = (row_id == col_id).astype(F4)
    rest = gram
    for j in range(v - 1):
        col = jnp.broadcast_to(rest[:, j : j + 1], (v, v))
        factor = jnp.where(row_id > j, col * (1.0 / col[j : j + 1, :]), 0.0)
        rest = rest - factor * rest[j : j + 1, :]
        inverse = inverse - factor * inverse[j : j + 1, :]
    pivots = jnp.sum(jnp.where(row_id == col_id, rest, 0.0), 1, keepdims=True)
    return inverse * (1.0 / jnp.sqrt(pivots))


def pieces(block):
    sub = block.shape[0] // 2
    return [block[:sub].astype(BF), block[sub:].astype(BF)]


def terms_of(used, lanes):
    return min(3, lanes // 2 // used)


def pack_moments(scratch, parts):
    total = None
    for i, part in enumerate(parts):
        width = part.shape[1]
        placed = pad_small(scratch, part)
        if i:
            placed = pltpu.roll(placed, i * width, 1)
        total = placed if total is None else total + placed
    used = sum(part.shape[1] for part in parts)
    packed = None
    for i in range(terms_of(used, total.shape[1])):
        term = total.astype(BF).astype(F4)
        total = total - term
        packed = term if packed is None else packed + pltpu.roll(term, i * used, 1)
    sub = packed.shape[0] // 2
    return (packed[:sub] + pltpu.roll(packed, packed.shape[1] // 2, 1)[sub:]).astype(BF)


def unpack_moments(block, used):
    width = block.shape[1]
    total = jnp.concatenate([block, pltpu.roll(block, width // 2, 1)], 0)
    result = total
    for i in range(1, terms_of(used, width)):
        result = result + pltpu.roll(total, width - i * used, 1)
    return result


def pad_small(scratch, small):
    scratch[...] = jnp.zeros(scratch.shape, F4)
    scratch[:, 0 : small.shape[1]] = small
    return scratch[...]


def store_for_all(out_ref, dens_halves, moments):
    pairs, _, tiles, blocks = out_ref.shape[:4]

    def one(g, carry):
        for h in range(2):
            for t in range(tiles):
                for k in range(blocks - 1):
                    out_ref[g, h, t, k] = dens_halves[k // 2][h][k % 2]
                out_ref[g, h, t, blocks - 1] = moments
        return carry

    lax.fori_loop(0, pairs, one, 0, unroll=True)


def project(block, coeff):
    high, low = split2(block)
    both = mm(jnp.concatenate([high, low], 0), coeff, NT)
    v = block.shape[0]
    total = both[:v] + both[v:]
    half = total.shape[1] // 2
    return [pieces(total[:, :half]), pieces(total[:, half:])]


def start_kernel(x_hbm, e_hbm, c_hbm, s_hbm, out_ref, x_ref, e_ref, c_ref, s_ref, sems, c_sems, scratch):
    local_k, v, _ = x_ref.shape
    copies = [
        pltpu.make_async_copy(x_hbm, x_ref, sems.at[0]),
        pltpu.make_async_copy(e_hbm, e_ref, sems.at[1]),
    ]
    c_copies = [pltpu.make_async_copy(c_hbm.at[k], c_ref.at[k], c_sems.at[k]) for k in range(local_k)]
    screen_copy = pltpu.make_async_copy(s_hbm, s_ref, sems.at[2])
    for copy in copies + c_copies + [screen_copy]:
        copy.start()
    for copy in copies:
        copy.wait()
    halves = []
    moments = None
    for k in range(local_k):
        x = x_ref[k]
        xh, xl = split2(x)
        eh, el = split2(x * e_ref[k : k + 1, :])
        big = mm(jnp.concatenate([xh, xl], 0), jnp.concatenate([xh, eh], 0), NT)
        small = mm(xh, jnp.concatenate([xl, el], 0), NT)
        part = big[:v] + big[v:] + small
        moments = part if moments is None else moments + part
        c_copies[k].wait()
        halves.append(project(x, c_ref[k]))
    store_for_all(out_ref, halves, pack_moments(scratch, [moments]))
    screen_copy.wait()


def gather_kernel(mine_ref, dens_ref, moments_ref):
    groups, tiles, blocks, sub, _ = mine_ref.shape
    local_k = blocks // 2
    moments = None
    for g in range(groups):
        for b in range(blocks - 1):
            total = mine_ref[g, 0, b].astype(F4)
            for t in range(1, tiles):
                total = total + mine_ref[g, t, b].astype(F4)
            row = b % 2 * sub
            dens_ref[g * local_k + b // 2, row : row + sub, :] = total
        for t in range(tiles):
            block = mine_ref[g, t, blocks - 1].astype(F4)
            moments = block if moments is None else moments + block
    moments_ref[...] = moments


def first_factor_kernel(moments_ref, small_ref, scratch, *, count):
    v = 2 * moments_ref.shape[0]
    moments = unpack_moments(moments_ref[...], 2 * v)
    small_ref[0] = pad_small(scratch, inverse_cholesky(moments[:, 0:v] / count))


def next_factor_kernel(moments_ref, small_ref, scratch, *, count):
    v = 2 * moments_ref.shape[0]
    moments = unpack_moments(moments_ref[...], 4 * v) / count
    mix = moments[:, v : 2 * v]
    inverse = inverse_cholesky(moments[:, 0:v] - exact(mix, mix, NT))
    small_ref[0] = pad_small(scratch, inverse)
    small_ref[1] = pad_small(scratch, apply_small(inverse, mix))


def own_core():
    return lax.axis_index("grp") % 2


def tasks_kernel(assign_hbm, ranks_hbm, screen_ref, mine_ref, other_ref, small_ref, *refs):
    prev_dens_ref = None
    if len(refs) > 8:
        prev_dens_ref, refs = refs[0], refs[1:]
    keep_ref, send_ref, dens_ref, assign_ref, ranks_ref, acc_ref, terms_ref, sems = refs
    heads = [
        pltpu.make_async_copy(assign_hbm, assign_ref, sems.at[0]),
        pltpu.make_async_copy(ranks_hbm, ranks_ref, sems.at[1]),
    ]
    for copy in heads:
        copy.start()
    acc_ref[...] = jnp.zeros(acc_ref.shape, F4)
    core = own_core()
    total_k, v, half = mine_ref.shape
    inverse = small_ref[0][:, 0:v]
    for k in range(total_k):
        for which, ref in ((0, mine_ref), (1, other_ref)):
            slot = (core + which) % 2
            dens = apply_small(inverse, ref[k])
            if prev_dens_ref is not None:
                dens = dens - apply_small(small_ref[1][:, 0:v], prev_dens_ref[slot, k])
            dens_ref[slot, k] = dens
            terms_ref[slot, k] = jnp.concatenate(split2(dens), 0)
    lane = lax.broadcasted_iota(jnp.int32, (2 * v, 2 * half), 1)
    for copy in heads:
        copy.wait()

    def one(t, carry):
        pair = assign_ref[t]
        row = pair // total_k
        col = pair - row * total_k
        keep = lane < ranks_ref[row, col]
        vec = jnp.concatenate([terms_ref[0, col], terms_ref[1, col]], 1)
        vec = jnp.where(keep, vec, jnp.zeros_like(vec))
        term = mm(vec, screen_ref[t], NT)
        term = jnp.where(keep[:v], term[:v] + term[v:], 0.0)
        acc_ref[0, row] = acc_ref[0, row] + term[:, :half]
        acc_ref[1, row] = acc_ref[1, row] + term[:, half:]
        return carry

    lax.fori_loop(0, screen_ref.shape[0], one, 0, unroll=True)
    for k in range(total_k):
        keep_ref[k] = acc_ref[core, k]
        send_ref[k] = acc_ref[1 - core, k]


def coupled_part(keep_ref, send_ref, dens_ref):
    total_k, v, _ = keep_ref.shape
    core = own_core()
    total = None
    for k in range(total_k):
        for which, ref in ((0, keep_ref), (1, send_ref)):
            rh, rl = split2(ref[k])
            dh, dl = split2(dens_ref[(core + which) % 2, k])
            big = mm(jnp.concatenate([rh, rl], 0), dh, NT)
            part = big[:v] + big[v:] + mm(rh, dl, NT)
            total = part if total is None else total + part
    return total


def first_coupled_kernel(keep_ref, send_ref, dens_ref, moments_ref, small_ref, coupled_ref, diag_ref, scratch, *, count):
    v = 2 * moments_ref.shape[0]
    coupled_ref[...] = pack_moments(scratch, [coupled_part(keep_ref, send_ref, dens_ref)])
    weighted = unpack_moments(moments_ref[...], 2 * v)[:, v : 2 * v] / count
    inverse = small_ref[0][:, 0:v]
    diag_ref[...] = pad_small(scratch, exact(exact(inverse, weighted, NN), inverse, NT))


def next_coupled_kernel(keep_ref, send_ref, dens_ref, moments_ref, small_ref, prev_diag_ref, coupled_ref, diag_ref, scratch, *, count):
    v = 2 * moments_ref.shape[0]
    coupled_ref[...] = pack_moments(scratch, [coupled_part(keep_ref, send_ref, dens_ref)])
    moments = unpack_moments(moments_ref[...], 4 * v) / count
    mix = moments[:, v : 2 * v]
    rp = moments[:, 2 * v : 3 * v]
    rv = moments[:, 3 * v : 4 * v]
    mixed = exact(exact(mix, prev_diag_ref[:, 0:v], NN), mix, NT)
    weighted = rp - exact(rv, mix, NT) - exact(mix, rv, NT) + mixed
    inverse = small_ref[0][:, 0:v]
    diag_ref[...] = pad_small(scratch, exact(exact(inverse, weighted, NN), inverse, NT))


def rows_kernel(keep_ref, recv_ref, coupled_ref, out_ref):
    groups, tiles, blocks = out_ref.shape[:3]
    local_k = blocks // 2
    for g in range(groups):
        for k in range(local_k):
            rows = pieces(keep_ref[g * local_k + k] + recv_ref[g * local_k + k])
            for t in range(tiles):
                out_ref[g, t, 2 * k] = rows[0]
                out_ref[g, t, 2 * k + 1] = rows[1]
        for t in range(tiles):
            out_ref[g, t, blocks - 1] = coupled_ref[...]


def sum_rows(recv_ref):
    pairs, _, tiles, blocks, sub, _ = recv_ref.shape

    def summed(block, halves):
        total = None
        for g in range(pairs):
            for h in halves:
                for t in range(tiles):
                    part = recv_ref[g, h, t, block].astype(F4)
                    total = part if total is None else total + part
        return total

    def both(k, half):
        return jnp.concatenate([summed(2 * k, (half,)), summed(2 * k + 1, (half,))], 0)

    rows = [jnp.concatenate([both(k, 0), both(k, 1)], 1) for k in range(blocks // 2)]
    return rows, unpack_moments(summed(blocks - 1, (0, 1)), 2 * sub)[:, 0 : 2 * sub]


def expand(rows, coeff):
    both = mm(jnp.concatenate(split2(rows), 0), coeff, NN)
    v = rows.shape[0]
    return both[:v] + both[v:]


def after_first_kernel(recv_ref, x_ref, e_ref, c_ref, small_ref, diag_ref, out_ref, v_ref, p_ref, ray_ref, scratch, *, count):
    local_k, v, _ = x_ref.shape
    rows, coupled = sum_rows(recv_ref)
    inverse = small_ref[0][:, 0:v]
    ray = diag_ref[:, 0:v] + coupled / count
    ray_ref[...] = pad_small(scratch, ray)
    halves = []
    moments = None
    for k in range(local_k):
        basis = apply_small(inverse, x_ref[k])
        energy = e_ref[k : k + 1, :]
        sigma = energy * basis + expand(rows[k], c_ref[k])
        residual = sigma - apply_small(ray, basis)
        precond = residual / energy
        v_ref[k] = basis
        p_ref[k] = precond
        halves.append(project(precond, c_ref[k]))
        bh, bl = split2(basis)
        rh, rl = split2(residual)
        ph, pw = split2(precond)
        big = mm(jnp.concatenate([ph, rh, pw, rl], 0), jnp.concatenate([ph, bh], 0), NT)
        small = mm(jnp.concatenate([ph, rh], 0), jnp.concatenate([pw, bl], 0), NT)
        part = big[: 2 * v] + big[2 * v :] + small
        moments = part if moments is None else moments + part
    store_for_all(out_ref, halves, pack_moments(scratch, [moments[:v], moments[v:]]))


def last_rows_kernel(recv_ref, v_ref, p_ref, e_ref, c_ref, small_ref, diag_ref, out_ref, res_hbm, basis_ref, q_ref, ray_ref, res_ref, sems, scratch, *, count):
    local_k, v, _ = v_ref.shape
    rows, coupled = sum_rows(recv_ref)
    inverse = small_ref[0][:, 0:v]
    both = small_ref[1][:, 0:v]
    ray = diag_ref[:, 0:v] + coupled / count
    ray_ref[...] = pad_small(scratch, ray)
    copies = []
    moments = None
    for k in range(local_k):
        basis = apply_small(inverse, p_ref[k]) - apply_small(both, v_ref[k])
        energy = e_ref[k : k + 1, :]
        sigma = energy * basis + expand(rows[k], c_ref[k])
        residual = sigma - apply_small(ray, basis)
        precond = residual / energy
        res_ref[k] = residual
        copies.append(pltpu.make_async_copy(res_ref.at[k], res_hbm.at[k], sems.at[k]))
        copies[-1].start()
        basis_ref[k] = basis
        q_ref[k] = precond
        bh, bl = split2(basis)
        ph, pw = split2(precond)
        big = mm(jnp.concatenate([ph, pw], 0), jnp.concatenate([ph, bh], 0), NT)
        part = big[:v] + big[v:] + mm(ph, jnp.concatenate([pw, bl], 0), NT)
        moments = part if moments is None else moments + part
    packed = to_row(pad_small(scratch, moments), 2 * v)
    for d in range(out_ref.shape[0]):
        out_ref[d] = packed
    for copy in copies:
        copy.wait()


def diagonal_lanes(shape, width):
    row_id = lax.broadcasted_iota(jnp.int32, shape, 0)
    return lax.broadcasted_iota(jnp.int32, shape, 1) // width == row_id


def fold_lanes(block, width):
    shift = width
    while shift < block.shape[1]:
        block = block + pltpu.roll(block, shift, 1)
        shift *= 2
    return block


def to_row(block, width):
    spread = fold_lanes(block, width)
    return jnp.sum(jnp.where(diagonal_lanes(block.shape, width), spread, 0.0), 0, keepdims=True)


def from_row(row, rows, width):
    block = jnp.broadcast_to(row, (rows, row.shape[1]))
    return fold_lanes(jnp.where(diagonal_lanes(block.shape, width), block, 0.0), width)


def finish_kernel(recv_ref, q_ref, b_ref, ray0_ref, ray1_ref, out_hbm, ray_hbm, out_ref, ray_ref, sems, *, count):
    local_k, v, _ = q_ref.shape
    ray_ref[0] = ray0_ref[:, 0:v].T
    ray_ref[1] = ray1_ref[:, 0:v].T
    copies = [pltpu.make_async_copy(ray_ref, ray_hbm, sems.at[local_k])]
    copies[0].start()
    row = jnp.sum(recv_ref[:, 0, :], 0, keepdims=True)
    moments = from_row(row, v, 2 * v) / count
    mix = moments[:, v : 2 * v]
    inverse = inverse_cholesky(moments[:, 0:v] - exact(mix, mix, NT))
    both = apply_small(inverse, mix)
    for k in range(local_k):
        out_ref[k] = apply_small(inverse, q_ref[k]) - apply_small(both, b_ref[k])
        copies.append(pltpu.make_async_copy(out_ref.at[k], out_hbm.at[k], sems.at[k]))
        copies[-1].start()
    for copy in copies:
        copy.wait()


VM = pl.BlockSpec(memory_space=pltpu.VMEM)
ANY = pl.BlockSpec(memory_space=pltpu.HBM)


def call(body, outs, ins, args, scratch=(), to_hbm=()):
    specs = VM
    if isinstance(outs, tuple):
        specs = tuple(ANY if i in to_hbm else VM for i in range(len(outs)))
    args = [
        pltpu.with_memory_space_constraint(arg, pltpu.HBM) if spec is ANY else arg
        for arg, spec in zip(args, ins)
    ]
    return pl.pallas_call(
        body,
        out_shape=outs,
        in_specs=ins,
        out_specs=specs,
        scratch_shapes=scratch,
        compiler_params=pltpu.CompilerParams(vmem_limit_bytes=16 << 20),
    )(*args)


def per_device(coeff, energy, ranks, assign, screen, initial):
    groups = lax.axis_size("grp")
    tiles = lax.axis_size("tile")
    devices = groups * tiles
    pairs = groups // 2
    local_k, v, width = initial.shape
    levels = coeff.shape[1]
    half = levels // 2
    total_k = local_k * groups
    count = float(total_k * width * tiles)
    axes = ("grp", "tile")
    swap = [(g, g ^ 1) for g in range(groups)]
    sds = jax.ShapeDtypeStruct
    small_scratch = pltpu.VMEM((v, half), F4)
    dma = pltpu.SemaphoreType.DMA
    half_shape = sds((total_k, v, half), F4)
    small_shape = sds((v, half), F4)

    def exchange(blocks, shape):
        sent = blocks.reshape((devices,) + blocks.shape[-3:])
        return lax.all_to_all(sent, axes, 0, 0, tiled=True).reshape(shape + sent.shape[1:])

    def to_all(blocks):
        got = exchange(blocks, (groups, tiles))
        mine, moments = call(gather_kernel, (half_shape, sds((v // 2, half), F4)), [VM], (got,))
        return mine, lax.ppermute(mine, "grp", swap), moments

    def to_owner(keep, recv, coupled):
        shape = sds((groups, tiles, 2 * local_k + 1, v // 2, half), BF)
        out = call(rows_kernel, shape, [VM] * 3, (keep, recv, coupled))
        return exchange(out, (pairs, 2, tiles))

    def factor(body, matrices, moments):
        shape = sds((matrices, v, half), F4)
        return call(functools.partial(body, count=count), shape, [VM], (moments,), (small_scratch,))

    def run_tasks(*args):
        dens_shape = (2, total_k, v, half)
        return call(
            tasks_kernel,
            (half_shape, half_shape, sds(dens_shape, F4)),
            [ANY, ANY] + [VM] * (len(args) + 1),
            (assign, ranks, screen) + args,
            (
                pltpu.SMEM(assign.shape, jnp.int32),
                pltpu.SMEM(ranks.shape, jnp.int32),
                pltpu.VMEM(dens_shape, F4),
                pltpu.VMEM((2, total_k, 2 * v, half), BF),
                dma((2,)),
            ),
        )

    def couple(body, *args):
        outs = (sds((v // 2, half), BF), small_shape)
        return call(functools.partial(body, count=count), outs, [VM] * len(args), args, (small_scratch,))

    all_shape = sds((pairs, 2, tiles, 2 * local_k + 1, v // 2, half), BF)
    flat = sds((local_k, v, width), F4)

    inputs = (initial, energy, coeff, screen)
    sent, initial, energy, coeff, screen = call(
        start_kernel,
        (all_shape,) + tuple(sds(a.shape, a.dtype) for a in inputs),
        [ANY] * 4,
        inputs,
        (dma((3,)), dma((local_k,)), small_scratch),
    )
    mine, other, moments = to_all(sent)
    small = factor(first_factor_kernel, 1, moments)
    keep, send, dens = run_tasks(mine, other, small)
    recv = lax.ppermute(send, "grp", swap)
    coupled, diag = couple(first_coupled_kernel, keep, send, dens, moments, small)
    got = to_owner(keep, recv, coupled)
    sent, basis, precond, ray0 = call(
        functools.partial(after_first_kernel, count=count),
        (all_shape, flat, flat, small_shape),
        [VM] * 6,
        (got, initial, energy, coeff, small, diag),
        (small_scratch,),
    )
    mine, other, moments = to_all(sent)
    small = factor(next_factor_kernel, 2, moments)
    keep, send, dens = run_tasks(mine, other, small, dens)
    recv = lax.ppermute(send, "grp", swap)
    coupled, diag = couple(next_coupled_kernel, keep, send, dens, moments, small, diag)
    got = to_owner(keep, recv, coupled)
    sent, residual, basis, precond, ray1 = call(
        functools.partial(last_rows_kernel, count=count),
        (sds((devices, 1, half), F4), flat, flat, flat, small_shape),
        [VM] * 7,
        (got, basis, precond, energy, coeff, small, diag),
        (pltpu.VMEM(flat.shape, F4), dma((local_k,)), small_scratch),
        (1,),
    )
    got = lax.all_to_all(sent, axes, 0, 0, tiled=True)
    basis, rayleigh = call(
        functools.partial(finish_kernel, count=count),
        (flat, sds((2, v, v), F4)),
        [VM] * 5,
        (got, precond, basis, ray0, ray1),
        (pltpu.VMEM(flat.shape, F4), pltpu.VMEM((2, v, v), F4), dma((local_k + 1,))),
        (0, 1),
    )
    return (rayleigh, basis, residual)


def solution(mesh):
    placed = (
        P("grp", None, "tile"),
        P("grp", "tile"),
        P(),
        P(("grp", "tile")),
        P(("grp", "tile"), None, None),
        P("grp", None, "tile"),
    )
    return jax.shard_map(
        per_device,
        mesh=mesh,
        in_specs=placed,
        out_specs=(P(), P("grp", None, "tile"), P("grp", None, "tile")),
        check_vma=False,
    )
```

```python
import functools

import jax
import jax.numpy as jnp
from jax import lax
from jax.experimental import pallas as pl
from jax.experimental.pallas import tpu as pltpu
from jax.sharding import PartitionSpec as P

ITERS = 2
LANES = 128
BF = jnp.bfloat16
F4 = jnp.float32
NT = (((1,), (1,)), ((), ()))
NN = (((1,), (0,)), ((), ()))


def split2(x):
    high = x.astype(BF)
    return high, (x - high.astype(F4)).astype(BF)


def mm(left, right, dims):
    return lax.dot_general(left, right, dims, preferred_element_type=F4)


def exact(left, right, dims):
    return lax.dot_general(
        left, right, dims, preferred_element_type=F4, precision=lax.Precision.HIGHEST
    )


def apply_small(weights, block):
    total = weights[:, 0:1] * block[0:1, :]
    for m in range(1, weights.shape[1]):
        total = total + weights[:, m : m + 1] * block[m : m + 1, :]
    return total


def inverse_cholesky(gram):
    v = gram.shape[0]
    row_id = lax.broadcasted_iota(jnp.int32, (v, v), 0)
    col_id = lax.broadcasted_iota(jnp.int32, (v, v), 1)
    inverse = (row_id == col_id).astype(F4)
    rest = gram
    for j in range(v - 1):
        col = jnp.broadcast_to(rest[:, j : j + 1], (v, v))
        factor = jnp.where(row_id > j, col * (1.0 / col[j : j + 1, :]), 0.0)
        rest = rest - factor * rest[j : j + 1, :]
        inverse = inverse - factor * inverse[j : j + 1, :]
    pivots = jnp.sum(jnp.where(row_id == col_id, rest, 0.0), 1, keepdims=True)
    return inverse * (1.0 / jnp.sqrt(pivots))


def pieces(block):
    sub = block.shape[0] // 2
    return [block[:sub].astype(BF), block[sub:].astype(BF)]


def terms_of(used, lanes):
    return min(3, lanes // 2 // used)


def pack_moments(scratch, parts):
    total = None
    for i, part in enumerate(parts):
        width = part.shape[1]
        placed = pad_small(scratch, part)
        if i:
            placed = pltpu.roll(placed, i * width, 1)
        total = placed if total is None else total + placed
    used = sum(part.shape[1] for part in parts)
    packed = None
    for i in range(terms_of(used, total.shape[1])):
        term = total.astype(BF).astype(F4)
        total = total - term
        packed = term if packed is None else packed + pltpu.roll(term, i * used, 1)
    sub = packed.shape[0] // 2
    return (packed[:sub] + pltpu.roll(packed, packed.shape[1] // 2, 1)[sub:]).astype(BF)


def unpack_moments(block, used):
    width = block.shape[1]
    total = jnp.concatenate([block, pltpu.roll(block, width // 2, 1)], 0)
    result = total
    for i in range(1, terms_of(used, width)):
        result = result + pltpu.roll(total, width - i * used, 1)
    return result


def pad_small(scratch, small):
    scratch[...] = jnp.zeros(scratch.shape, F4)
    scratch[:, 0 : small.shape[1]] = small
    return scratch[...]


def store_for_all(out_ref, dens_halves, moments):
    pairs, _, tiles, blocks = out_ref.shape[:4]

    def one(g, carry):
        for h in range(2):
            for t in range(tiles):
                for k in range(blocks - 1):
                    out_ref[g, h, t, k] = dens_halves[k // 2][h][k % 2]
                out_ref[g, h, t, blocks - 1] = moments
        return carry

    lax.fori_loop(0, pairs, one, 0, unroll=True)


def project(block, coeff):
    high, low = split2(block)
    both = mm(jnp.concatenate([high, low], 0), coeff, NT)
    v = block.shape[0]
    total = both[:v] + both[v:]
    half = total.shape[1] // 2
    return [pieces(total[:, :half]), pieces(total[:, half:])]


def start_kernel(x_hbm, e_hbm, c_hbm, s_hbm, out_ref, x_ref, e_ref, c_ref, s_ref, sems, c_sems, scratch):
    local_k, v, _ = x_ref.shape
    copies = [
        pltpu.make_async_copy(x_hbm, x_ref, sems.at[0]),
        pltpu.make_async_copy(e_hbm, e_ref, sems.at[1]),
    ]
    c_copies = [pltpu.make_async_copy(c_hbm.at[k], c_ref.at[k], c_sems.at[k]) for k in range(local_k)]
    screen_copy = pltpu.make_async_copy(s_hbm.at[pl.ds(0, s_ref.shape[0])], s_ref, sems.at[2])
    for copy in copies + c_copies + [screen_copy]:
        copy.start()
    for copy in copies:
        copy.wait()
    moments = None
    for k in range(local_k):
        x = x_ref[k]
        xh, xl = split2(x)
        eh, el = split2(x * e_ref[k : k + 1, :])
        big = mm(jnp.concatenate([xh, xl], 0), jnp.concatenate([xh, eh], 0), NT)
        small = mm(xh, jnp.concatenate([xl, el], 0), NT)
        part = big[:v] + big[v:] + small
        moments = part if moments is None else moments + part
    packed = pack_moments(scratch, [moments])
    for copy in c_copies:
        copy.wait()
    halves = [project(x_ref[k], c_ref[k]) for k in range(local_k)]
    store_for_all(out_ref, halves, packed)
    screen_copy.wait()


def gather_kernel(mine_ref, dens_ref, moments_ref):
    groups, tiles, blocks, sub, _ = mine_ref.shape
    local_k = blocks // 2
    moments = None
    for g in range(groups):
        for b in range(blocks - 1):
            total = mine_ref[g, 0, b].astype(F4)
            for t in range(1, tiles):
                total = total + mine_ref[g, t, b].astype(F4)
            row = b % 2 * sub
            dens_ref[g * local_k + b // 2, row : row + sub, :] = total
        for t in range(tiles):
            block = mine_ref[g, t, blocks - 1].astype(F4)
            moments = block if moments is None else moments + block
    moments_ref[...] = moments


def first_factor_kernel(moments_ref, small_ref, scratch, *, count):
    v = 2 * moments_ref.shape[0]
    moments = unpack_moments(moments_ref[...], 2 * v)
    small_ref[0] = pad_small(scratch, inverse_cholesky(moments[:, 0:v] / count))


def next_factor_kernel(moments_ref, small_ref, scratch, *, count):
    v = 2 * moments_ref.shape[0]
    moments = unpack_moments(moments_ref[...], 4 * v) / count
    mix = moments[:, v : 2 * v]
    inverse = inverse_cholesky(moments[:, 0:v] - exact(mix, mix, NT))
    small_ref[0] = pad_small(scratch, inverse)
    small_ref[1] = pad_small(scratch, apply_small(inverse, mix))


def own_core():
    return lax.axis_index("grp") % 2


def tasks_kernel(assign_hbm, ranks_hbm, head_ref, tail_ref, mine_ref, other_ref, small_ref, *refs, first):
    prev_dens_ref = None
    if first:
        tail_hbm, tail_ref = tail_ref, refs[3]
        refs = refs[:3] + refs[4:]
    else:
        prev_dens_ref, refs = refs[0], refs[1:]
    keep_ref, send_ref, dens_ref, assign_ref, ranks_ref, acc_ref, terms_ref, sems = refs
    heads = head_ref.shape[0]
    tails = tail_ref.shape[0]
    tables = [
        pltpu.make_async_copy(assign_hbm, assign_ref, sems.at[0]),
        pltpu.make_async_copy(ranks_hbm, ranks_ref, sems.at[1]),
    ]
    for copy in tables:
        copy.start()
    if first:
        tail_copy = pltpu.make_async_copy(tail_hbm.at[pl.ds(heads, tails)], tail_ref, sems.at[2])
        tail_copy.start()
    acc_ref[...] = jnp.zeros(acc_ref.shape, F4)
    core = own_core()
    total_k, v, half = mine_ref.shape
    inverse = small_ref[0][:, 0:v]
    for k in range(total_k):
        for which, ref in ((0, mine_ref), (1, other_ref)):
            slot = (core + which) % 2
            dens = apply_small(inverse, ref[k])
            if prev_dens_ref is not None:
                dens = dens - apply_small(small_ref[1][:, 0:v], prev_dens_ref[slot, k])
            dens_ref[slot, k] = dens
            terms_ref[slot, k] = jnp.concatenate(split2(dens), 0)
    lane = lax.broadcasted_iota(jnp.int32, (2 * v, 2 * half), 1)
    for copy in tables:
        copy.wait()

    def one(screen_ref, offset, t, carry):
        pair = assign_ref[offset + t]
        row = pair // total_k
        col = pair - row * total_k
        keep = lane < ranks_ref[row, col]
        vec = jnp.concatenate([terms_ref[0, col], terms_ref[1, col]], 1)
        vec = jnp.where(keep, vec, jnp.zeros_like(vec))
        term = mm(vec, screen_ref[t], NT)
        term = jnp.where(keep[:v], term[:v] + term[v:], 0.0)
        acc_ref[0, row] = acc_ref[0, row] + term[:, :half]
        acc_ref[1, row] = acc_ref[1, row] + term[:, half:]
        return carry

    lax.fori_loop(0, heads, functools.partial(one, head_ref, 0), 0, unroll=True)
    if first:
        tail_copy.wait()
    lax.fori_loop(0, tails, functools.partial(one, tail_ref, heads), 0, unroll=True)
    for k in range(total_k):
        keep_ref[k] = acc_ref[core, k]
        send_ref[k] = acc_ref[1 - core, k]


def coupled_part(keep_ref, send_ref, dens_ref):
    total_k, v, _ = keep_ref.shape
    core = own_core()
    total = None
    for k in range(total_k):
        for which, ref in ((0, keep_ref), (1, send_ref)):
            rh, rl = split2(ref[k])
            dh, dl = split2(dens_ref[(core + which) % 2, k])
            big = mm(jnp.concatenate([rh, rl], 0), dh, NT)
            part = big[:v] + big[v:] + mm(rh, dl, NT)
            total = part if total is None else total + part
    return total


def first_coupled_kernel(keep_ref, send_ref, dens_ref, moments_ref, small_ref, coupled_ref, diag_ref, scratch, *, count):
    v = 2 * moments_ref.shape[0]
    coupled_ref[...] = pack_moments(scratch, [coupled_part(keep_ref, send_ref, dens_ref)])
    weighted = unpack_moments(moments_ref[...], 2 * v)[:, v : 2 * v] / count
    inverse = small_ref[0][:, 0:v]
    diag_ref[...] = pad_small(scratch, exact(exact(inverse, weighted, NN), inverse, NT))


def next_coupled_kernel(keep_ref, send_ref, dens_ref, moments_ref, small_ref, prev_diag_ref, coupled_ref, diag_ref, scratch, *, count):
    v = 2 * moments_ref.shape[0]
    coupled_ref[...] = pack_moments(scratch, [coupled_part(keep_ref, send_ref, dens_ref)])
    moments = unpack_moments(moments_ref[...], 4 * v) / count
    mix = moments[:, v : 2 * v]
    rp = moments[:, 2 * v : 3 * v]
    rv = moments[:, 3 * v : 4 * v]
    mixed = exact(exact(mix, prev_diag_ref[:, 0:v], NN), mix, NT)
    weighted = rp - exact(rv, mix, NT) - exact(mix, rv, NT) + mixed
    inverse = small_ref[0][:, 0:v]
    diag_ref[...] = pad_small(scratch, exact(exact(inverse, weighted, NN), inverse, NT))


def rows_kernel(keep_ref, recv_ref, coupled_ref, out_ref):
    groups, tiles, blocks = out_ref.shape[:3]
    local_k = blocks // 2
    for g in range(groups):
        for k in range(local_k):
            rows = pieces(keep_ref[g * local_k + k] + recv_ref[g * local_k + k])
            for t in range(tiles):
                out_ref[g, t, 2 * k] = rows[0]
                out_ref[g, t, 2 * k + 1] = rows[1]
        for t in range(tiles):
            out_ref[g, t, blocks - 1] = coupled_ref[...]


def sum_rows(recv_ref):
    pairs, _, tiles, blocks, sub, _ = recv_ref.shape

    def summed(block, halves):
        total = None
        for g in range(pairs):
            for h in halves:
                for t in range(tiles):
                    part = recv_ref[g, h, t, block].astype(F4)
                    total = part if total is None else total + part
        return total

    def both(k, half):
        return jnp.concatenate([summed(2 * k, (half,)), summed(2 * k + 1, (half,))], 0)

    rows = [jnp.concatenate([both(k, 0), both(k, 1)], 1) for k in range(blocks // 2)]
    return rows, unpack_moments(summed(blocks - 1, (0, 1)), 2 * sub)[:, 0 : 2 * sub]


def expand(rows, coeff):
    both = mm(jnp.concatenate(split2(rows), 0), coeff, NN)
    v = rows.shape[0]
    return both[:v] + both[v:]


def after_first_kernel(recv_ref, x_ref, e_ref, c_ref, small_ref, diag_ref, out_ref, v_ref, p_ref, ray_ref, scratch, *, count):
    local_k, v, _ = x_ref.shape
    rows, coupled = sum_rows(recv_ref)
    expanded = [expand(rows[k], c_ref[k]) for k in range(local_k)]
    inverse = small_ref[0][:, 0:v]
    ray = diag_ref[:, 0:v] + coupled / count
    ray_ref[...] = pad_small(scratch, ray)
    inverse_energy = 1.0 / e_ref[...]
    residuals = []
    for k in range(local_k):
        basis = apply_small(inverse, x_ref[k])
        residual = e_ref[k : k + 1, :] * basis + expanded[k] - apply_small(ray, basis)
        residuals.append(residual)
        v_ref[k] = basis
        p_ref[k] = residual * inverse_energy[k : k + 1, :]
    halves = [project(p_ref[k], c_ref[k]) for k in range(local_k)]
    moments = None
    for k in range(local_k):
        bh, bl = split2(v_ref[k])
        rh, rl = split2(residuals[k])
        ph, pw = split2(p_ref[k])
        big = mm(jnp.concatenate([ph, rh, pw, rl], 0), jnp.concatenate([ph, bh], 0), NT)
        small = mm(jnp.concatenate([ph, rh], 0), jnp.concatenate([pw, bl], 0), NT)
        part = big[: 2 * v] + big[2 * v :] + small
        moments = part if moments is None else moments + part
    store_for_all(out_ref, halves, pack_moments(scratch, [moments[:v], moments[v:]]))


def last_rows_kernel(recv_ref, v_ref, p_ref, e_ref, c_ref, small_ref, diag_ref, out_ref, res_hbm, basis_ref, q_ref, ray_ref, res_ref, sems, scratch, *, count):
    local_k, v, _ = v_ref.shape
    rows, coupled = sum_rows(recv_ref)
    expanded = [expand(rows[k], c_ref[k]) for k in range(local_k)]
    inverse = small_ref[0][:, 0:v]
    both = small_ref[1][:, 0:v]
    ray = diag_ref[:, 0:v] + coupled / count
    ray_ref[...] = pad_small(scratch, ray)
    inverse_energy = 1.0 / e_ref[...]
    copies = []
    for k in range(local_k):
        basis = apply_small(inverse, p_ref[k]) - apply_small(both, v_ref[k])
        residual = e_ref[k : k + 1, :] * basis + expanded[k] - apply_small(ray, basis)
        res_ref[k] = residual
        copies.append(pltpu.make_async_copy(res_ref.at[k], res_hbm.at[k], sems.at[k]))
        copies[-1].start()
        basis_ref[k] = basis
        q_ref[k] = residual * inverse_energy[k : k + 1, :]
    moments = None
    for k in range(local_k):
        bh, bl = split2(basis_ref[k])
        ph, pw = split2(q_ref[k])
        big = mm(jnp.concatenate([ph, pw], 0), jnp.concatenate([ph, bh], 0), NT)
        part = big[:v] + big[v:] + mm(ph, jnp.concatenate([pw, bl], 0), NT)
        moments = part if moments is None else moments + part
    packed = to_row(pad_small(scratch, moments), 2 * v)
    for d in range(out_ref.shape[0]):
        out_ref[d] = packed
    for copy in copies:
        copy.wait()


def diagonal_lanes(shape, width):
    row_id = lax.broadcasted_iota(jnp.int32, shape, 0)
    return lax.broadcasted_iota(jnp.int32, shape, 1) // width == row_id


def fold_lanes(block, width):
    shift = width
    while shift < block.shape[1]:
        block = block + pltpu.roll(block, shift, 1)
        shift *= 2
    return block


def to_row(block, width):
    spread = fold_lanes(block, width)
    return jnp.sum(jnp.where(diagonal_lanes(block.shape, width), spread, 0.0), 0, keepdims=True)


def from_row(row, rows, width):
    block = jnp.broadcast_to(row, (rows, row.shape[1]))
    return fold_lanes(jnp.where(diagonal_lanes(block.shape, width), block, 0.0), width)


def finish_kernel(recv_ref, q_ref, b_ref, ray0_ref, ray1_ref, out_hbm, ray_hbm, out_ref, ray_ref, sems, *, count):
    local_k, v, _ = q_ref.shape
    ray_ref[0] = ray0_ref[:, 0:v].T
    ray_ref[1] = ray1_ref[:, 0:v].T
    copies = [pltpu.make_async_copy(ray_ref, ray_hbm, sems.at[local_k])]
    copies[0].start()
    row = jnp.sum(recv_ref[:, 0, :], 0, keepdims=True)
    moments = from_row(row, v, 2 * v) / count
    mix = moments[:, v : 2 * v]
    inverse = inverse_cholesky(moments[:, 0:v] - exact(mix, mix, NT))
    both = apply_small(inverse, mix)
    for k in range(local_k):
        out_ref[k] = apply_small(inverse, q_ref[k]) - apply_small(both, b_ref[k])
        copies.append(pltpu.make_async_copy(out_ref.at[k], out_hbm.at[k], sems.at[k]))
        copies[-1].start()
    for copy in copies:
        copy.wait()


VM = pl.BlockSpec(memory_space=pltpu.VMEM)
ANY = pl.BlockSpec(memory_space=pltpu.HBM)


def call(body, outs, ins, args, scratch=(), to_hbm=()):
    specs = VM
    if isinstance(outs, tuple):
        specs = tuple(ANY if i in to_hbm else VM for i in range(len(outs)))
    args = [
        pltpu.with_memory_space_constraint(arg, pltpu.HBM) if spec is ANY else arg
        for arg, spec in zip(args, ins)
    ]
    return pl.pallas_call(
        body,
        out_shape=outs,
        in_specs=ins,
        out_specs=specs,
        scratch_shapes=scratch,
        compiler_params=pltpu.CompilerParams(vmem_limit_bytes=16 << 20),
    )(*args)


def per_device(coeff, energy, ranks, assign, screen, initial):
    groups = lax.axis_size("grp")
    tiles = lax.axis_size("tile")
    devices = groups * tiles
    pairs = groups // 2
    local_k, v, width = initial.shape
    levels = coeff.shape[1]
    half = levels // 2
    total_k = local_k * groups
    count = float(total_k * width * tiles)
    axes = ("grp", "tile")
    swap = [(g, g ^ 1) for g in range(groups)]
    sds = jax.ShapeDtypeStruct
    small_scratch = pltpu.VMEM((v, half), F4)
    dma = pltpu.SemaphoreType.DMA
    half_shape = sds((total_k, v, half), F4)
    small_shape = sds((v, half), F4)

    def exchange(blocks, shape):
        sent = blocks.reshape((devices,) + blocks.shape[-3:])
        return lax.all_to_all(sent, axes, 0, 0, tiled=True).reshape(shape + sent.shape[1:])

    def to_all(blocks):
        got = exchange(blocks, (groups, tiles))
        mine, moments = call(gather_kernel, (half_shape, sds((v // 2, half), F4)), [VM], (got,))
        return mine, lax.ppermute(mine, "grp", swap), moments

    def to_owner(keep, recv, coupled):
        shape = sds((groups, tiles, 2 * local_k + 1, v // 2, half), BF)
        out = call(rows_kernel, shape, [VM] * 3, (keep, recv, coupled))
        return exchange(out, (pairs, 2, tiles))

    def factor(body, matrices, moments):
        shape = sds((matrices, v, half), F4)
        return call(functools.partial(body, count=count), shape, [VM], (moments,), (small_scratch,))

    def run_tasks(tail, *args):
        dens_shape = (2, total_k, v, half)
        outs = (half_shape, half_shape, sds(dens_shape, F4))
        first = tail is screen
        if first:
            outs = outs + (sds((tails,) + screen.shape[1:], BF),)
        return call(
            functools.partial(tasks_kernel, first=first),
            outs,
            [ANY, ANY, VM, ANY if first else VM] + [VM] * len(args),
            (assign, ranks, head, tail) + args,
            (
                pltpu.SMEM(assign.shape, jnp.int32),
                pltpu.SMEM(ranks.shape, jnp.int32),
                pltpu.VMEM(dens_shape, F4),
                pltpu.VMEM((2, total_k, 2 * v, half), BF),
                dma((3,)),
            ),
        )

    def couple(body, *args):
        outs = (sds((v // 2, half), BF), small_shape)
        return call(functools.partial(body, count=count), outs, [VM] * len(args), args, (small_scratch,))

    all_shape = sds((pairs, 2, tiles, 2 * local_k + 1, v // 2, half), BF)
    flat = sds((local_k, v, width), F4)

    tails = screen.shape[0] // 4
    inputs = (initial, energy, coeff)
    head_shape = sds((screen.shape[0] - tails,) + screen.shape[1:], BF)
    sent, initial, energy, coeff, head = call(
        start_kernel,
        (all_shape,) + tuple(sds(a.shape, a.dtype) for a in inputs) + (head_shape,),
        [ANY] * 4,
        inputs + (screen,),
        (dma((3,)), dma((local_k,)), small_scratch),
    )
    mine, other, moments = to_all(sent)
    small = factor(first_factor_kernel, 1, moments)
    keep, send, dens, tail = run_tasks(screen, mine, other, small)
    recv = lax.ppermute(send, "grp", swap)
    coupled, diag = couple(first_coupled_kernel, keep, send, dens, moments, small)
    got = to_owner(keep, recv, coupled)
    sent, basis, precond, ray0 = call(
        functools.partial(after_first_kernel, count=count),
        (all_shape, flat, flat, small_shape),
        [VM] * 6,
        (got, initial, energy, coeff, small, diag),
        (small_scratch,),
    )
    mine, other, moments = to_all(sent)
    small = factor(next_factor_kernel, 2, moments)
    keep, send, dens = run_tasks(tail, mine, other, small, dens)
    recv = lax.ppermute(send, "grp", swap)
    coupled, diag = couple(next_coupled_kernel, keep, send, dens, moments, small, diag)
    got = to_owner(keep, recv, coupled)
    sent, residual, basis, precond, ray1 = call(
        functools.partial(last_rows_kernel, count=count),
        (sds((devices, 1, half), F4), flat, flat, flat, small_shape),
        [VM] * 7,
        (got, basis, precond, energy, coeff, small, diag),
        (pltpu.VMEM(flat.shape, F4), dma((local_k,)), small_scratch),
        (1,),
    )
    got = lax.all_to_all(sent, axes, 0, 0, tiled=True)
    basis, rayleigh = call(
        functools.partial(finish_kernel, count=count),
        (flat, sds((2, v, v), F4)),
        [VM] * 5,
        (got, precond, basis, ray0, ray1),
        (pltpu.VMEM(flat.shape, F4), pltpu.VMEM((2, v, v), F4), dma((local_k + 1,))),
        (0, 1),
    )
    return (rayleigh, basis, residual)


def solution(mesh):
    placed = (
        P("grp", None, "tile"),
        P("grp", "tile"),
        P(),
        P(("grp", "tile")),
        P(("grp", "tile"), None, None),
        P("grp", None, "tile"),
    )
    return jax.shard_map(
        per_device,
        mesh=mesh,
        in_specs=placed,
        out_specs=(P(), P("grp", None, "tile"), P("grp", None, "tile")),
        check_vma=False,
    )
```

```python
import functools

import jax
import jax.numpy as jnp
from jax import lax
from jax.experimental import pallas as pl
from jax.experimental.pallas import tpu as pltpu
from jax.sharding import PartitionSpec as P

ITERS = 2
LANES = 128
BF = jnp.bfloat16
F4 = jnp.float32
NT = (((1,), (1,)), ((), ()))
NN = (((1,), (0,)), ((), ()))


def split2(x):
    high = x.astype(BF)
    return high, (x - high.astype(F4)).astype(BF)


def mm(left, right, dims):
    return lax.dot_general(left, right, dims, preferred_element_type=F4)


def exact(left, right, dims):
    return lax.dot_general(
        left, right, dims, preferred_element_type=F4, precision=lax.Precision.HIGHEST
    )


def apply_small(weights, block):
    total = weights[:, 0:1] * block[0:1, :]
    for m in range(1, weights.shape[1]):
        total = total + weights[:, m : m + 1] * block[m : m + 1, :]
    return total


def inverse_cholesky(gram):
    v = gram.shape[0]
    row_id = lax.broadcasted_iota(jnp.int32, (v, v), 0)
    col_id = lax.broadcasted_iota(jnp.int32, (v, v), 1)
    inverse = (row_id == col_id).astype(F4)
    rest = gram
    for j in range(v - 1):
        col = jnp.broadcast_to(rest[:, j : j + 1], (v, v))
        factor = jnp.where(row_id > j, col * (1.0 / col[j : j + 1, :]), 0.0)
        rest = rest - factor * rest[j : j + 1, :]
        inverse = inverse - factor * inverse[j : j + 1, :]
    pivots = jnp.sum(jnp.where(row_id == col_id, rest, 0.0), 1, keepdims=True)
    return inverse * (1.0 / jnp.sqrt(pivots))


def unit_factors(gram):
    v = gram.shape[0]
    row_id = lax.broadcasted_iota(jnp.int32, (v, v), 0)
    col_id = lax.broadcasted_iota(jnp.int32, (v, v), 1)
    lower = (row_id == col_id).astype(F4)
    inverse = lower
    rest = gram + 1e-4 * lower * gram
    for j in range(v - 1):
        col = jnp.broadcast_to(rest[:, j : j + 1], (v, v))
        pivot = jnp.maximum(col[j : j + 1, :], 1e-30)
        factor = jnp.where(row_id > j, col * (1.0 / pivot), 0.0)
        rest = rest - factor * rest[j : j + 1, :]
        inverse = inverse - factor * inverse[j : j + 1, :]
        lower = lower + jnp.where(col_id == j, factor, 0.0)
    return lower, inverse


def pieces(block):
    sub = block.shape[0] // 2
    return [block[:sub].astype(BF), block[sub:].astype(BF)]


def terms_of(used, lanes):
    return min(3, lanes // 2 // used)


def pack_moments(scratch, parts):
    total = None
    used = 0
    for part in parts:
        placed = pad_small(scratch, part)
        if used:
            placed = pltpu.roll(placed, used, 1)
        total = placed if total is None else total + placed
        used += part.shape[1]
    packed = None
    for i in range(terms_of(used, total.shape[1])):
        term = total.astype(BF).astype(F4)
        total = total - term
        packed = term if packed is None else packed + pltpu.roll(term, i * used, 1)
    sub = packed.shape[0] // 2
    return (packed[:sub] + pltpu.roll(packed, packed.shape[1] // 2, 1)[sub:]).astype(BF)


def unpack_moments(block, used):
    width = block.shape[1]
    total = jnp.concatenate([block, pltpu.roll(block, width // 2, 1)], 0)
    result = total
    for i in range(1, terms_of(used, width)):
        result = result + pltpu.roll(total, width - i * used, 1)
    return result


def pad_small(scratch, small):
    scratch[...] = jnp.zeros(scratch.shape, F4)
    scratch[:, 0 : small.shape[1]] = small
    return scratch[...]


def store_for_all(out_ref, dens_halves, moments):
    pairs, _, tiles, blocks = out_ref.shape[:4]

    def one(g, carry):
        for h in range(2):
            for t in range(tiles):
                for k in range(blocks - 1):
                    out_ref[g, h, t, k] = dens_halves[k // 2][h][k % 2]
                out_ref[g, h, t, blocks - 1] = moments
        return carry

    lax.fori_loop(0, pairs, one, 0, unroll=True)


def project(block, coeff):
    high, low = split2(block)
    both = mm(jnp.concatenate([high, low], 0), coeff, NT)
    v = block.shape[0]
    return both[:v] + both[v:]


def halves_of(total):
    half = total.shape[1] // 2
    return [pieces(total[:, :half]), pieces(total[:, half:])]


def start_kernel(x_hbm, e_hbm, c_hbm, s_hbm, out_ref, x_ref, e_ref, c_ref, s_ref, sems, c_sems, scratch):
    local_k, v, _ = x_ref.shape
    copies = [
        pltpu.make_async_copy(x_hbm, x_ref, sems.at[0]),
        pltpu.make_async_copy(e_hbm, e_ref, sems.at[1]),
    ]
    c_copies = [pltpu.make_async_copy(c_hbm.at[k], c_ref.at[k], c_sems.at[k]) for k in range(local_k)]
    screen_copy = pltpu.make_async_copy(s_hbm.at[pl.ds(0, s_ref.shape[0])], s_ref, sems.at[2])
    for copy in copies + c_copies + [screen_copy]:
        copy.start()
    for copy in copies:
        copy.wait()
    moments = None
    for k in range(local_k):
        x = x_ref[k]
        xh, xl = split2(x)
        eh, el = split2(x * e_ref[k : k + 1, :])
        big = mm(jnp.concatenate([xh, xl], 0), jnp.concatenate([xh, eh], 0), NT)
        small = mm(xh, jnp.concatenate([xl, el], 0), NT)
        part = big[:v] + big[v:] + small
        moments = part if moments is None else moments + part
    for copy in c_copies:
        copy.wait()
    projected = [project(x_ref[k], c_ref[k]) for k in range(local_k)]
    lower, inverse = unit_factors(moments[:, 0:v])
    halves = [halves_of(apply_small(inverse, block)) for block in projected]
    store_for_all(out_ref, halves, pack_moments(scratch, [moments, lower]))
    screen_copy.wait()


def gather_kernel(mine_ref, dens_ref, moments_ref):
    groups, tiles, blocks, sub, _ = mine_ref.shape
    local_k = blocks // 2
    moments = None
    for g in range(groups):
        for b in range(blocks - 1):
            total = mine_ref[g, 0, b].astype(F4)
            for t in range(1, tiles):
                total = total + mine_ref[g, t, b].astype(F4)
            row = b % 2 * sub
            dens_ref[g * local_k + b // 2, row : row + sub, :] = total
        for t in range(tiles):
            block = mine_ref[g, t, blocks - 1].astype(F4)
            moments = block if moments is None else moments + block
    moments_ref[...] = moments


def first_gather_kernel(mine_ref, dens_ref, moments_ref):
    groups, tiles, blocks, sub, lanes = mine_ref.shape
    local_k = blocks // 2
    v = 2 * sub
    lane = lax.broadcasted_iota(jnp.int32, (v, lanes), 1)
    own = (lane >= 2 * v) & (lane < 3 * v)
    moments = None
    for g in range(groups):
        factors = None
        for t in range(tiles):
            block = mine_ref[g, t, blocks - 1].astype(F4)
            moments = block if moments is None else moments + block
            lower = jnp.where(own, unpack_moments(block, 3 * v), 0.0)
            lower = pltpu.roll(lower, (lanes + (t - 2) * v) % lanes, 1)
            factors = lower if factors is None else factors + lower
        left = jnp.concatenate(split2(factors[:, : tiles * v]), 0)
        for k in range(local_k):
            sent = [mine_ref[g, t, 2 * k + i].astype(F4) for t in range(tiles) for i in range(2)]
            both = mm(left, jnp.concatenate(sent, 0).astype(BF), NN)
            dens_ref[g * local_k + k] = both[:v] + both[v:]
    moments_ref[...] = moments


def first_factor_kernel(moments_ref, small_ref, scratch, *, count):
    v = 2 * moments_ref.shape[0]
    moments = unpack_moments(moments_ref[...], 3 * v)
    small_ref[0] = pad_small(scratch, inverse_cholesky(moments[:, 0:v] / count))


def next_factor_kernel(moments_ref, small_ref, scratch, *, count):
    v = 2 * moments_ref.shape[0]
    moments = unpack_moments(moments_ref[...], 4 * v) / count
    mix = moments[:, v : 2 * v]
    inverse = inverse_cholesky(moments[:, 0:v] - exact(mix, mix, NT))
    small_ref[0] = pad_small(scratch, inverse)
    small_ref[1] = pad_small(scratch, apply_small(inverse, mix))


def own_core():
    return lax.axis_index("grp") % 2


def tasks_kernel(assign_hbm, ranks_hbm, head_ref, tail_ref, mine_ref, other_ref, small_ref, *refs, first):
    prev_dens_ref = None
    if first:
        tail_hbm, tail_ref = tail_ref, refs[3]
        refs = refs[:3] + refs[4:]
    else:
        prev_dens_ref, refs = refs[0], refs[1:]
    keep_ref, send_ref, dens_ref, assign_ref, ranks_ref, acc_ref, terms_ref, sems = refs
    heads = head_ref.shape[0]
    tails = tail_ref.shape[0]
    tables = [
        pltpu.make_async_copy(assign_hbm, assign_ref, sems.at[0]),
        pltpu.make_async_copy(ranks_hbm, ranks_ref, sems.at[1]),
    ]
    for copy in tables:
        copy.start()
    if first:
        tail_copy = pltpu.make_async_copy(tail_hbm.at[pl.ds(heads, tails)], tail_ref, sems.at[2])
        tail_copy.start()
    acc_ref[...] = jnp.zeros(acc_ref.shape, F4)
    core = own_core()
    total_k, v, half = mine_ref.shape
    inverse = small_ref[0][:, 0:v]
    for k in range(total_k):
        for which, ref in ((0, mine_ref), (1, other_ref)):
            slot = (core + which) % 2
            dens = apply_small(inverse, ref[k])
            if prev_dens_ref is not None:
                dens = dens - apply_small(small_ref[1][:, 0:v], prev_dens_ref[slot, k])
            dens_ref[slot, k] = dens
            terms_ref[slot, k] = jnp.concatenate(split2(dens), 0)
    lane = lax.broadcasted_iota(jnp.int32, (2 * v, 2 * half), 1)
    for copy in tables:
        copy.wait()

    def one(screen_ref, offset, t, carry):
        pair = assign_ref[offset + t]
        row = pair // total_k
        col = pair - row * total_k
        keep = lane < ranks_ref[row, col]
        vec = jnp.concatenate([terms_ref[0, col], terms_ref[1, col]], 1)
        vec = jnp.where(keep, vec, jnp.zeros_like(vec))
        term = mm(vec, screen_ref[t], NT)
        term = jnp.where(keep[:v], term[:v] + term[v:], 0.0)
        acc_ref[0, row] = acc_ref[0, row] + term[:, :half]
        acc_ref[1, row] = acc_ref[1, row] + term[:, half:]
        return carry

    lax.fori_loop(0, heads, functools.partial(one, head_ref, 0), 0, unroll=True)
    if first:
        tail_copy.wait()
    lax.fori_loop(0, tails, functools.partial(one, tail_ref, heads), 0, unroll=True)
    for k in range(total_k):
        keep_ref[k] = acc_ref[core, k]
        send_ref[k] = acc_ref[1 - core, k]


def coupled_part(keep_ref, send_ref, dens_ref):
    total_k, v, _ = keep_ref.shape
    core = own_core()
    total = None
    for k in range(total_k):
        for which, ref in ((0, keep_ref), (1, send_ref)):
            rh, rl = split2(ref[k])
            dh, dl = split2(dens_ref[(core + which) % 2, k])
            big = mm(jnp.concatenate([rh, rl], 0), dh, NT)
            part = big[:v] + big[v:] + mm(rh, dl, NT)
            total = part if total is None else total + part
    return total


def first_coupled_kernel(keep_ref, send_ref, dens_ref, moments_ref, small_ref, coupled_ref, diag_ref, scratch, *, count):
    v = 2 * moments_ref.shape[0]
    coupled_ref[...] = pack_moments(scratch, [coupled_part(keep_ref, send_ref, dens_ref)])
    weighted = unpack_moments(moments_ref[...], 3 * v)[:, v : 2 * v] / count
    inverse = small_ref[0][:, 0:v]
    diag_ref[...] = pad_small(scratch, exact(exact(inverse, weighted, NN), inverse, NT))


def next_coupled_kernel(keep_ref, send_ref, dens_ref, moments_ref, small_ref, prev_diag_ref, coupled_ref, diag_ref, scratch, *, count):
    v = 2 * moments_ref.shape[0]
    coupled_ref[...] = pack_moments(scratch, [coupled_part(keep_ref, send_ref, dens_ref)])
    moments = unpack_moments(moments_ref[...], 4 * v) / count
    mix = moments[:, v : 2 * v]
    rp = moments[:, 2 * v : 3 * v]
    rv = moments[:, 3 * v : 4 * v]
    mixed = exact(exact(mix, prev_diag_ref[:, 0:v], NN), mix, NT)
    weighted = rp - exact(rv, mix, NT) - exact(mix, rv, NT) + mixed
    inverse = small_ref[0][:, 0:v]
    diag_ref[...] = pad_small(scratch, exact(exact(inverse, weighted, NN), inverse, NT))


def rows_kernel(keep_ref, recv_ref, coupled_ref, out_ref):
    groups, tiles, blocks = out_ref.shape[:3]
    local_k = blocks // 2
    for g in range(groups):
        for k in range(local_k):
            rows = pieces(keep_ref[g * local_k + k] + recv_ref[g * local_k + k])
            for t in range(tiles):
                out_ref[g, t, 2 * k] = rows[0]
                out_ref[g, t, 2 * k + 1] = rows[1]
        for t in range(tiles):
            out_ref[g, t, blocks - 1] = coupled_ref[...]


def sum_rows(recv_ref):
    pairs, _, tiles, blocks, sub, _ = recv_ref.shape

    def summed(block, halves):
        total = None
        for g in range(pairs):
            for h in halves:
                for t in range(tiles):
                    part = recv_ref[g, h, t, block].astype(F4)
                    total = part if total is None else total + part
        return total

    def both(k, half):
        return jnp.concatenate([summed(2 * k, (half,)), summed(2 * k + 1, (half,))], 0)

    rows = [jnp.concatenate([both(k, 0), both(k, 1)], 1) for k in range(blocks // 2)]
    return rows, unpack_moments(summed(blocks - 1, (0, 1)), 2 * sub)[:, 0 : 2 * sub]


def expand(rows, coeff):
    both = mm(jnp.concatenate(split2(rows), 0), coeff, NN)
    v = rows.shape[0]
    return both[:v] + both[v:]


def after_first_kernel(recv_ref, x_ref, e_ref, c_ref, small_ref, diag_ref, out_ref, v_ref, p_ref, ray_ref, scratch, *, count):
    local_k, v, _ = x_ref.shape
    rows, coupled = sum_rows(recv_ref)
    expanded = [expand(rows[k], c_ref[k]) for k in range(local_k)]
    inverse = small_ref[0][:, 0:v]
    ray = diag_ref[:, 0:v] + coupled / count
    ray_ref[...] = pad_small(scratch, ray)
    inverse_energy = 1.0 / e_ref[...]
    residuals = []
    for k in range(local_k):
        basis = apply_small(inverse, x_ref[k])
        residual = e_ref[k : k + 1, :] * basis + expanded[k] - apply_small(ray, basis)
        residuals.append(residual)
        v_ref[k] = basis
        p_ref[k] = residual * inverse_energy[k : k + 1, :]
    halves = [halves_of(project(p_ref[k], c_ref[k])) for k in range(local_k)]
    moments = None
    for k in range(local_k):
        bh, bl = split2(v_ref[k])
        rh, rl = split2(residuals[k])
        ph, pw = split2(p_ref[k])
        big = mm(jnp.concatenate([ph, rh, pw, rl], 0), jnp.concatenate([ph, bh], 0), NT)
        small = mm(jnp.concatenate([ph, rh], 0), jnp.concatenate([pw, bl], 0), NT)
        part = big[: 2 * v] + big[2 * v :] + small
        moments = part if moments is None else moments + part
    store_for_all(out_ref, halves, pack_moments(scratch, [moments[:v], moments[v:]]))


def last_rows_kernel(recv_ref, v_ref, p_ref, e_ref, c_ref, small_ref, diag_ref, out_ref, res_hbm, basis_ref, q_ref, ray_ref, res_ref, sems, scratch, *, count):
    local_k, v, _ = v_ref.shape
    rows, coupled = sum_rows(recv_ref)
    expanded = [expand(rows[k], c_ref[k]) for k in range(local_k)]
    inverse = small_ref[0][:, 0:v]
    both = small_ref[1][:, 0:v]
    ray = diag_ref[:, 0:v] + coupled / count
    ray_ref[...] = pad_small(scratch, ray)
    inverse_energy = 1.0 / e_ref[...]
    copies = []
    for k in range(local_k):
        basis = apply_small(inverse, p_ref[k]) - apply_small(both, v_ref[k])
        residual = e_ref[k : k + 1, :] * basis + expanded[k] - apply_small(ray, basis)
        res_ref[k] = residual
        copies.append(pltpu.make_async_copy(res_ref.at[k], res_hbm.at[k], sems.at[k]))
        copies[-1].start()
        basis_ref[k] = basis
        q_ref[k] = residual * inverse_energy[k : k + 1, :]
    moments = None
    for k in range(local_k):
        bh, bl = split2(basis_ref[k])
        ph, pw = split2(q_ref[k])
        big = mm(jnp.concatenate([ph, pw], 0), jnp.concatenate([ph, bh], 0), NT)
        part = big[:v] + big[v:] + mm(ph, jnp.concatenate([pw, bl], 0), NT)
        moments = part if moments is None else moments + part
    packed = to_row(pad_small(scratch, moments), 2 * v)
    for d in range(out_ref.shape[0]):
        out_ref[d] = packed
    for copy in copies:
        copy.wait()


def diagonal_lanes(shape, width):
    row_id = lax.broadcasted_iota(jnp.int32, shape, 0)
    return lax.broadcasted_iota(jnp.int32, shape, 1) // width == row_id


def fold_lanes(block, width):
    shift = width
    while shift < block.shape[1]:
        block = block + pltpu.roll(block, shift, 1)
        shift *= 2
    return block


def to_row(block, width):
    spread = fold_lanes(block, width)
    return jnp.sum(jnp.where(diagonal_lanes(block.shape, width), spread, 0.0), 0, keepdims=True)


def from_row(row, rows, width):
    block = jnp.broadcast_to(row, (rows, row.shape[1]))
    return fold_lanes(jnp.where(diagonal_lanes(block.shape, width), block, 0.0), width)


def finish_kernel(recv_ref, q_ref, b_ref, ray0_ref, ray1_ref, out_hbm, ray_hbm, out_ref, ray_ref, sems, *, count):
    local_k, v, _ = q_ref.shape
    ray_ref[0] = ray0_ref[:, 0:v].T
    ray_ref[1] = ray1_ref[:, 0:v].T
    copies = [pltpu.make_async_copy(ray_ref, ray_hbm, sems.at[local_k])]
    copies[0].start()
    row = jnp.sum(recv_ref[:, 0, :], 0, keepdims=True)
    moments = from_row(row, v, 2 * v) / count
    mix = moments[:, v : 2 * v]
    inverse = inverse_cholesky(moments[:, 0:v] - exact(mix, mix, NT))
    both = apply_small(inverse, mix)
    for k in range(local_k):
        out_ref[k] = apply_small(inverse, q_ref[k]) - apply_small(both, b_ref[k])
        copies.append(pltpu.make_async_copy(out_ref.at[k], out_hbm.at[k], sems.at[k]))
        copies[-1].start()
    for copy in copies:
        copy.wait()


VM = pl.BlockSpec(memory_space=pltpu.VMEM)
ANY = pl.BlockSpec(memory_space=pltpu.HBM)


def call(body, outs, ins, args, scratch=(), to_hbm=()):
    specs = VM
    if isinstance(outs, tuple):
        specs = tuple(ANY if i in to_hbm else VM for i in range(len(outs)))
    args = [
        pltpu.with_memory_space_constraint(arg, pltpu.HBM) if spec is ANY else arg
        for arg, spec in zip(args, ins)
    ]
    return pl.pallas_call(
        body,
        out_shape=outs,
        in_specs=ins,
        out_specs=specs,
        scratch_shapes=scratch,
        compiler_params=pltpu.CompilerParams(vmem_limit_bytes=16 << 20),
    )(*args)


def per_device(coeff, energy, ranks, assign, screen, initial):
    groups = lax.axis_size("grp")
    tiles = lax.axis_size("tile")
    devices = groups * tiles
    pairs = groups // 2
    local_k, v, width = initial.shape
    levels = coeff.shape[1]
    half = levels // 2
    total_k = local_k * groups
    count = float(total_k * width * tiles)
    axes = ("grp", "tile")
    swap = [(g, g ^ 1) for g in range(groups)]
    sds = jax.ShapeDtypeStruct
    small_scratch = pltpu.VMEM((v, half), F4)
    dma = pltpu.SemaphoreType.DMA
    half_shape = sds((total_k, v, half), F4)
    small_shape = sds((v, half), F4)

    def exchange(blocks, shape):
        sent = blocks.reshape((devices,) + blocks.shape[-3:])
        return lax.all_to_all(sent, axes, 0, 0, tiled=True).reshape(shape + sent.shape[1:])

    def to_all(blocks, body):
        got = exchange(blocks, (groups, tiles))
        mine, moments = call(body, (half_shape, sds((v // 2, half), F4)), [VM], (got,))
        return mine, lax.ppermute(mine, "grp", swap), moments

    def to_owner(keep, recv, coupled):
        shape = sds((groups, tiles, 2 * local_k + 1, v // 2, half), BF)
        out = call(rows_kernel, shape, [VM] * 3, (keep, recv, coupled))
        return exchange(out, (pairs, 2, tiles))

    def factor(body, matrices, moments):
        shape = sds((matrices, v, half), F4)
        return call(functools.partial(body, count=count), shape, [VM], (moments,), (small_scratch,))

    def run_tasks(tail, *args):
        dens_shape = (2, total_k, v, half)
        outs = (half_shape, half_shape, sds(dens_shape, F4))
        first = tail is screen
        if first:
            outs = outs + (sds((tails,) + screen.shape[1:], BF),)
        return call(
            functools.partial(tasks_kernel, first=first),
            outs,
            [ANY, ANY, VM, ANY if first else VM] + [VM] * len(args),
            (assign, ranks, head, tail) + args,
            (
                pltpu.SMEM(assign.shape, jnp.int32),
                pltpu.SMEM(ranks.shape, jnp.int32),
                pltpu.VMEM(dens_shape, F4),
                pltpu.VMEM((2, total_k, 2 * v, half), BF),
                dma((3,)),
            ),
        )

    def couple(body, *args):
        outs = (sds((v // 2, half), BF), small_shape)
        return call(functools.partial(body, count=count), outs, [VM] * len(args), args, (small_scratch,))

    all_shape = sds((pairs, 2, tiles, 2 * local_k + 1, v // 2, half), BF)
    flat = sds((local_k, v, width), F4)

    tails = screen.shape[0] // 4
    inputs = (initial, energy, coeff)
    head_shape = sds((screen.shape[0] - tails,) + screen.shape[1:], BF)
    sent, initial, energy, coeff, head = call(
        start_kernel,
        (all_shape,) + tuple(sds(a.shape, a.dtype) for a in inputs) + (head_shape,),
        [ANY] * 4,
        inputs + (screen,),
        (dma((3,)), dma((local_k,)), small_scratch),
    )
    mine, other, moments = to_all(sent, first_gather_kernel)
    small = factor(first_factor_kernel, 1, moments)
    keep, send, dens, tail = run_tasks(screen, mine, other, small)
    recv = lax.ppermute(send, "grp", swap)
    coupled, diag = couple(first_coupled_kernel, keep, send, dens, moments, small)
    got = to_owner(keep, recv, coupled)
    sent, basis, precond, ray0 = call(
        functools.partial(after_first_kernel, count=count),
        (all_shape, flat, flat, small_shape),
        [VM] * 6,
        (got, initial, energy, coeff, small, diag),
        (small_scratch,),
    )
    mine, other, moments = to_all(sent, gather_kernel)
    small = factor(next_factor_kernel, 2, moments)
    keep, send, dens = run_tasks(tail, mine, other, small, dens)
    recv = lax.ppermute(send, "grp", swap)
    coupled, diag = couple(next_coupled_kernel, keep, send, dens, moments, small, diag)
    got = to_owner(keep, recv, coupled)
    sent, residual, basis, precond, ray1 = call(
        functools.partial(last_rows_kernel, count=count),
        (sds((devices, 1, half), F4), flat, flat, flat, small_shape),
        [VM] * 7,
        (got, basis, precond, energy, coeff, small, diag),
        (pltpu.VMEM(flat.shape, F4), dma((local_k,)), small_scratch),
        (1,),
    )
    got = lax.all_to_all(sent, axes, 0, 0, tiled=True)
    basis, rayleigh = call(
        functools.partial(finish_kernel, count=count),
        (flat, sds((2, v, v), F4)),
        [VM] * 5,
        (got, precond, basis, ray0, ray1),
        (pltpu.VMEM(flat.shape, F4), pltpu.VMEM((2, v, v), F4), dma((local_k + 1,))),
        (0, 1),
    )
    return (rayleigh, basis, residual)


def solution(mesh):
    placed = (
        P("grp", None, "tile"),
        P("grp", "tile"),
        P(),
        P(("grp", "tile")),
        P(("grp", "tile"), None, None),
        P("grp", None, "tile"),
    )
    return jax.shard_map(
        per_device,
        mesh=mesh,
        in_specs=placed,
        out_specs=(P(), P("grp", None, "tile"), P("grp", None, "tile")),
        check_vma=False,
    )
```

```python
import functools

import jax
import jax.numpy as jnp
from jax import lax
from jax.experimental import pallas as pl
from jax.experimental.pallas import tpu as pltpu
from jax.sharding import PartitionSpec as P

ITERS = 2
LANES = 128
BF = jnp.bfloat16
F4 = jnp.float32
NT = (((1,), (1,)), ((), ()))
NN = (((1,), (0,)), ((), ()))


def split2(x):
    high = x.astype(BF)
    return high, (x - high.astype(F4)).astype(BF)


def mm(left, right, dims):
    return lax.dot_general(left, right, dims, preferred_element_type=F4)


def exact(left, right, dims):
    return lax.dot_general(
        left, right, dims, preferred_element_type=F4, precision=lax.Precision.HIGHEST
    )


def apply_small(weights, block):
    total = weights[:, 0:1] * block[0:1, :]
    for m in range(1, weights.shape[1]):
        total = total + weights[:, m : m + 1] * block[m : m + 1, :]
    return total


def inverse_cholesky(gram):
    v = gram.shape[0]
    row_id = lax.broadcasted_iota(jnp.int32, (v, v), 0)
    col_id = lax.broadcasted_iota(jnp.int32, (v, v), 1)
    inverse = (row_id == col_id).astype(F4)
    rest = gram
    for j in range(v - 1):
        col = jnp.broadcast_to(rest[:, j : j + 1], (v, v))
        factor = jnp.where(row_id > j, col * (1.0 / col[j : j + 1, :]), 0.0)
        rest = rest - factor * rest[j : j + 1, :]
        inverse = inverse - factor * inverse[j : j + 1, :]
    pivots = jnp.sum(jnp.where(row_id == col_id, rest, 0.0), 1, keepdims=True)
    return inverse * (1.0 / jnp.sqrt(pivots))


def unit_factors(gram):
    v = gram.shape[0]
    row_id = lax.broadcasted_iota(jnp.int32, (v, v), 0)
    col_id = lax.broadcasted_iota(jnp.int32, (v, v), 1)
    lower = (row_id == col_id).astype(F4)
    inverse = lower
    rest = gram + 1e-4 * lower * gram
    for j in range(v - 1):
        col = jnp.broadcast_to(rest[:, j : j + 1], (v, v))
        pivot = jnp.maximum(col[j : j + 1, :], 1e-30)
        factor = jnp.where(row_id > j, col * (1.0 / pivot), 0.0)
        rest = rest - factor * rest[j : j + 1, :]
        inverse = inverse - factor * inverse[j : j + 1, :]
        lower = lower + jnp.where(col_id == j, factor, 0.0)
    return lower, inverse


def pieces(block):
    sub = block.shape[0] // 2
    return [block[:sub].astype(BF), block[sub:].astype(BF)]


def terms_of(used, lanes):
    return min(3, lanes // 2 // used)


def pack_moments(scratch, parts):
    total = None
    used = 0
    for part in parts:
        placed = pad_small(scratch, part)
        if used:
            placed = pltpu.roll(placed, used, 1)
        total = placed if total is None else total + placed
        used += part.shape[1]
    packed = None
    for i in range(terms_of(used, total.shape[1])):
        term = total.astype(BF).astype(F4)
        total = total - term
        packed = term if packed is None else packed + pltpu.roll(term, i * used, 1)
    sub = packed.shape[0] // 2
    return (packed[:sub] + pltpu.roll(packed, packed.shape[1] // 2, 1)[sub:]).astype(BF)


def unpack_moments(block, used):
    width = block.shape[1]
    total = jnp.concatenate([block, pltpu.roll(block, width // 2, 1)], 0)
    result = total
    for i in range(1, terms_of(used, width)):
        result = result + pltpu.roll(total, width - i * used, 1)
    return result


def pad_small(scratch, small):
    scratch[...] = jnp.zeros(scratch.shape, F4)
    scratch[:, 0 : small.shape[1]] = small
    return scratch[...]


def store_for_all(out_ref, dens_halves, moments):
    pairs, _, tiles, blocks = out_ref.shape[:4]

    def one(g, carry):
        for h in range(2):
            for t in range(tiles):
                for k in range(blocks - 1):
                    out_ref[g, h, t, k] = dens_halves[k // 2][h][k % 2]
                out_ref[g, h, t, blocks - 1] = moments
        return carry

    lax.fori_loop(0, pairs, one, 0, unroll=True)


def project(block, coeff):
    high, low = split2(block)
    both = mm(jnp.concatenate([high, low], 0), coeff, NT)
    v = block.shape[0]
    return both[:v] + both[v:]


def halves_of(total):
    half = total.shape[1] // 2
    return [pieces(total[:, :half]), pieces(total[:, half:])]


def start_kernel(x_hbm, e_hbm, c_hbm, s_hbm, out_ref, x_ref, e_ref, c_ref, s_ref, sems, c_sems, scratch):
    local_k, v, _ = x_ref.shape
    copies = [
        pltpu.make_async_copy(x_hbm, x_ref, sems.at[0]),
        pltpu.make_async_copy(e_hbm, e_ref, sems.at[1]),
    ]
    c_copies = [pltpu.make_async_copy(c_hbm.at[k], c_ref.at[k], c_sems.at[k]) for k in range(local_k)]
    screen_copy = pltpu.make_async_copy(s_hbm.at[pl.ds(0, s_ref.shape[0])], s_ref, sems.at[2])
    for copy in copies + c_copies + [screen_copy]:
        copy.start()
    for copy in copies:
        copy.wait()
    moments = None
    for k in range(local_k):
        x = x_ref[k]
        xh, xl = split2(x)
        eh, el = split2(x * e_ref[k : k + 1, :])
        big = mm(jnp.concatenate([xh, xl], 0), jnp.concatenate([xh, eh], 0), NT)
        small = mm(xh, jnp.concatenate([xl, el], 0), NT)
        part = big[:v] + big[v:] + small
        moments = part if moments is None else moments + part
    for copy in c_copies:
        copy.wait()
    projected = [project(x_ref[k], c_ref[k]) for k in range(local_k)]
    lower, inverse = unit_factors(moments[:, 0:v])
    halves = [halves_of(apply_small(inverse, block)) for block in projected]
    store_for_all(out_ref, halves, pack_moments(scratch, [moments, lower]))
    screen_copy.wait()


def gather_kernel(mine_ref, dens_ref, moments_ref):
    groups, tiles, blocks, sub, _ = mine_ref.shape
    local_k = blocks // 2
    moments = None
    for g in range(groups):
        for b in range(blocks - 1):
            total = mine_ref[g, 0, b].astype(F4)
            for t in range(1, tiles):
                total = total + mine_ref[g, t, b].astype(F4)
            row = b % 2 * sub
            dens_ref[g * local_k + b // 2, row : row + sub, :] = total
        for t in range(tiles):
            block = mine_ref[g, t, blocks - 1].astype(F4)
            moments = block if moments is None else moments + block
    moments_ref[...] = moments


def first_gather_kernel(mine_ref, dens_ref, moments_ref):
    groups, tiles, blocks, sub, lanes = mine_ref.shape
    local_k = blocks // 2
    v = 2 * sub
    lane = lax.broadcasted_iota(jnp.int32, (v, lanes), 1)
    own = (lane >= 2 * v) & (lane < 3 * v)
    moments = None
    for g in range(groups):
        factors = None
        for t in range(tiles):
            block = mine_ref[g, t, blocks - 1].astype(F4)
            moments = block if moments is None else moments + block
            lower = jnp.where(own, unpack_moments(block, 3 * v), 0.0)
            lower = pltpu.roll(lower, (lanes + (t - 2) * v) % lanes, 1)
            factors = lower if factors is None else factors + lower
        left = jnp.concatenate(split2(factors[:, : tiles * v]), 0)
        for k in range(local_k):
            sent = [mine_ref[g, t, 2 * k + i].astype(F4) for t in range(tiles) for i in range(2)]
            both = mm(left, jnp.concatenate(sent, 0).astype(BF), NN)
            dens_ref[g * local_k + k] = both[:v] + both[v:]
    moments_ref[...] = moments


def first_factor_kernel(moments_ref, small_ref, scratch, *, count):
    v = 2 * moments_ref.shape[0]
    moments = unpack_moments(moments_ref[...], 3 * v)
    small_ref[0] = pad_small(scratch, inverse_cholesky(moments[:, 0:v] / count))


def next_factor_kernel(moments_ref, small_ref, scratch, *, count):
    v = 2 * moments_ref.shape[0]
    moments = unpack_moments(moments_ref[...], 4 * v) / count
    mix = moments[:, v : 2 * v]
    inverse = inverse_cholesky(moments[:, 0:v] - exact(mix, mix, NT))
    small_ref[0] = pad_small(scratch, inverse)
    small_ref[1] = pad_small(scratch, apply_small(inverse, mix))


def own_core():
    return lax.axis_index("grp") % 2


def tasks_kernel(assign_hbm, ranks_hbm, head_ref, tail_ref, mine_ref, other_ref, small_ref, *refs, first):
    prev_dens_ref = None
    if first:
        tail_hbm, tail_ref = tail_ref, refs[3]
        refs = refs[:3] + refs[4:]
    else:
        prev_dens_ref, refs = refs[0], refs[1:]
    keep_ref, send_ref, dens_ref, assign_ref, ranks_ref, acc_ref, terms_ref, sems = refs
    heads = head_ref.shape[0]
    tails = tail_ref.shape[0]
    tables = [
        pltpu.make_async_copy(assign_hbm, assign_ref, sems.at[0]),
        pltpu.make_async_copy(ranks_hbm, ranks_ref, sems.at[1]),
    ]
    for copy in tables:
        copy.start()
    if first:
        tail_copy = pltpu.make_async_copy(tail_hbm.at[pl.ds(heads, tails)], tail_ref, sems.at[2])
        tail_copy.start()
    acc_ref[...] = jnp.zeros(acc_ref.shape, F4)
    core = own_core()
    total_k, v, half = mine_ref.shape
    inverse = small_ref[0][:, 0:v]
    for k in range(total_k):
        for which, ref in ((0, mine_ref), (1, other_ref)):
            slot = (core + which) % 2
            dens = apply_small(inverse, ref[k])
            if prev_dens_ref is not None:
                dens = dens - apply_small(small_ref[1][:, 0:v], prev_dens_ref[slot, k])
            dens_ref[slot, k] = dens
            terms_ref[slot, k] = jnp.concatenate(split2(dens), 0)
    lane = lax.broadcasted_iota(jnp.int32, (2 * v, 2 * half), 1)
    for copy in tables:
        copy.wait()

    def one(screen_ref, offset, t, carry):
        pair = assign_ref[offset + t]
        row = pair // total_k
        col = pair - row * total_k
        keep = lane < ranks_ref[row, col]
        vec = jnp.concatenate([terms_ref[0, col], terms_ref[1, col]], 1)
        vec = jnp.where(keep, vec, jnp.zeros_like(vec))
        term = mm(vec, screen_ref[t], NT)
        term = jnp.where(keep[:v], term[:v] + term[v:], 0.0)
        acc_ref[0, row] = acc_ref[0, row] + term[:, :half]
        acc_ref[1, row] = acc_ref[1, row] + term[:, half:]
        return carry

    lax.fori_loop(0, heads, functools.partial(one, head_ref, 0), 0, unroll=True)
    if first:
        tail_copy.wait()
    lax.fori_loop(0, tails, functools.partial(one, tail_ref, heads), 0, unroll=True)
    for k in range(total_k):
        keep_ref[k] = acc_ref[core, k]
        send_ref[k] = acc_ref[1 - core, k]


def coupled_part(keep_ref, send_ref, dens_ref):
    total_k, v, _ = keep_ref.shape
    core = own_core()
    total = None
    for k in range(total_k):
        for which, ref in ((0, keep_ref), (1, send_ref)):
            rh, rl = split2(ref[k])
            dh, dl = split2(dens_ref[(core + which) % 2, k])
            big = mm(jnp.concatenate([rh, rl], 0), dh, NT)
            part = big[:v] + big[v:] + mm(rh, dl, NT)
            total = part if total is None else total + part
    return total


def first_coupled_kernel(keep_ref, send_ref, dens_ref, moments_ref, small_ref, coupled_ref, diag_ref, scratch, *, count):
    v = 2 * moments_ref.shape[0]
    coupled_ref[...] = pack_moments(scratch, [coupled_part(keep_ref, send_ref, dens_ref)])
    weighted = unpack_moments(moments_ref[...], 3 * v)[:, v : 2 * v] / count
    inverse = small_ref[0][:, 0:v]
    diag_ref[...] = pad_small(scratch, exact(exact(inverse, weighted, NN), inverse, NT))


def next_coupled_kernel(keep_ref, send_ref, dens_ref, moments_ref, small_ref, prev_diag_ref, coupled_ref, diag_ref, scratch, *, count):
    v = 2 * moments_ref.shape[0]
    coupled_ref[...] = pack_moments(scratch, [coupled_part(keep_ref, send_ref, dens_ref)])
    moments = unpack_moments(moments_ref[...], 4 * v) / count
    mix = moments[:, v : 2 * v]
    rp = moments[:, 2 * v : 3 * v]
    rv = moments[:, 3 * v : 4 * v]
    mixed = exact(exact(mix, prev_diag_ref[:, 0:v], NN), mix, NT)
    weighted = rp - exact(rv, mix, NT) - exact(mix, rv, NT) + mixed
    inverse = small_ref[0][:, 0:v]
    diag_ref[...] = pad_small(scratch, exact(exact(inverse, weighted, NN), inverse, NT))


def rows_kernel(keep_ref, recv_ref, coupled_ref, out_ref):
    groups, tiles, blocks = out_ref.shape[:3]
    local_k = blocks // 2
    for g in range(groups):
        for k in range(local_k):
            rows = pieces(keep_ref[g * local_k + k] + recv_ref[g * local_k + k])
            for t in range(tiles):
                out_ref[g, t, 2 * k] = rows[0]
                out_ref[g, t, 2 * k + 1] = rows[1]
        for t in range(tiles):
            out_ref[g, t, blocks - 1] = coupled_ref[...]


def sum_rows(recv_ref):
    pairs, _, tiles, blocks, sub, _ = recv_ref.shape

    def summed(block, halves):
        total = None
        for g in range(pairs):
            for h in halves:
                for t in range(tiles):
                    part = recv_ref[g, h, t, block].astype(F4)
                    total = part if total is None else total + part
        return total

    def both(k, half):
        return jnp.concatenate([summed(2 * k, (half,)), summed(2 * k + 1, (half,))], 0)

    rows = [jnp.concatenate([both(k, 0), both(k, 1)], 1) for k in range(blocks // 2)]
    return rows, unpack_moments(summed(blocks - 1, (0, 1)), 2 * sub)[:, 0 : 2 * sub]


def expand(rows, coeff):
    both = mm(jnp.concatenate(split2(rows), 0), coeff, NN)
    v = rows.shape[0]
    return both[:v] + both[v:]


def after_first_kernel(recv_ref, x_ref, e_ref, c_ref, small_ref, diag_ref, out_ref, v_ref, p_ref, ray_ref, scratch, *, count):
    local_k, v, _ = x_ref.shape
    rows, coupled = sum_rows(recv_ref)
    expanded = [expand(rows[k], c_ref[k]) for k in range(local_k)]
    inverse = small_ref[0][:, 0:v]
    ray = diag_ref[:, 0:v] + coupled / count
    ray_ref[...] = pad_small(scratch, ray)
    inverse_energy = 1.0 / e_ref[...]
    residuals = []
    for k in range(local_k):
        basis = apply_small(inverse, x_ref[k])
        residual = e_ref[k : k + 1, :] * basis + expanded[k] - apply_small(ray, basis)
        residuals.append(residual)
        v_ref[k] = basis
        p_ref[k] = residual * inverse_energy[k : k + 1, :]
    halves = [halves_of(project(p_ref[k], c_ref[k])) for k in range(local_k)]
    moments = None
    for k in range(local_k):
        bh, bl = split2(v_ref[k])
        rh, rl = split2(residuals[k])
        ph, pw = split2(p_ref[k])
        big = mm(jnp.concatenate([ph, rh, pw, rl], 0), jnp.concatenate([ph, bh], 0), NT)
        small = mm(jnp.concatenate([ph, rh], 0), jnp.concatenate([pw, bl], 0), NT)
        part = big[: 2 * v] + big[2 * v :] + small
        moments = part if moments is None else moments + part
    store_for_all(out_ref, halves, pack_moments(scratch, [moments[:v], moments[v:]]))


def last_rows_kernel(recv_ref, v_ref, p_ref, e_ref, c_ref, small_ref, diag_ref, out_ref, res_hbm, basis_ref, q_ref, ray_ref, res_ref, sems, scratch, *, count):
    local_k, v, _ = v_ref.shape
    rows, coupled = sum_rows(recv_ref)
    expanded = [expand(rows[k], c_ref[k]) for k in range(local_k)]
    inverse = small_ref[0][:, 0:v]
    both = small_ref[1][:, 0:v]
    ray = diag_ref[:, 0:v] + coupled / count
    ray_ref[...] = pad_small(scratch, ray)
    inverse_energy = 1.0 / e_ref[...]
    copies = []
    for k in range(local_k):
        basis = apply_small(inverse, p_ref[k]) - apply_small(both, v_ref[k])
        residual = e_ref[k : k + 1, :] * basis + expanded[k] - apply_small(ray, basis)
        res_ref[k] = residual
        copies.append(pltpu.make_async_copy(res_ref.at[k], res_hbm.at[k], sems.at[k]))
        copies[-1].start()
        basis_ref[k] = basis
        q_ref[k] = residual * inverse_energy[k : k + 1, :]
    moments = None
    for k in range(local_k):
        bh, bl = split2(basis_ref[k])
        ph, pw = split2(q_ref[k])
        big = mm(jnp.concatenate([ph, pw], 0), jnp.concatenate([ph, bh], 0), NT)
        part = big[:v] + big[v:] + mm(ph, jnp.concatenate([pw, bl], 0), NT)
        moments = part if moments is None else moments + part
    packed = to_row(pad_small(scratch, moments), 2 * v)
    for d in range(out_ref.shape[0]):
        out_ref[d] = packed
    for copy in copies:
        copy.wait()


def diagonal_lanes(shape, width):
    row_id = lax.broadcasted_iota(jnp.int32, shape, 0)
    return lax.broadcasted_iota(jnp.int32, shape, 1) // width == row_id


def fold_lanes(block, width):
    shift = width
    while shift < block.shape[1]:
        block = block + pltpu.roll(block, shift, 1)
        shift *= 2
    return block


def to_row(block, width):
    spread = fold_lanes(block, width)
    return jnp.sum(jnp.where(diagonal_lanes(block.shape, width), spread, 0.0), 0, keepdims=True)


def from_row(row, rows, width):
    block = jnp.broadcast_to(row, (rows, row.shape[1]))
    return fold_lanes(jnp.where(diagonal_lanes(block.shape, width), block, 0.0), width)


def finish_kernel(recv_ref, q_ref, b_ref, ray0_ref, ray1_ref, out_hbm, ray_hbm, out_ref, ray_ref, sems, *, count):
    local_k, v, _ = q_ref.shape
    ray_ref[0] = ray0_ref[:, 0:v].T
    ray_ref[1] = ray1_ref[:, 0:v].T
    copies = [pltpu.make_async_copy(ray_ref, ray_hbm, sems.at[local_k])]
    copies[0].start()
    row = jnp.sum(recv_ref[:, 0, :], 0, keepdims=True)
    moments = from_row(row, v, 2 * v) / count
    mix = moments[:, v : 2 * v]
    inverse = inverse_cholesky(moments[:, 0:v] - exact(mix, mix, NT))
    both = apply_small(inverse, mix)
    for k in range(local_k):
        out_ref[k] = apply_small(inverse, q_ref[k]) - apply_small(both, b_ref[k])
        copies.append(pltpu.make_async_copy(out_ref.at[k], out_hbm.at[k], sems.at[k]))
        copies[-1].start()
    for copy in copies:
        copy.wait()


VM = pl.BlockSpec(memory_space=pltpu.VMEM)
ANY = pl.BlockSpec(memory_space=pltpu.HBM)


def call(body, outs, ins, args, scratch=(), to_hbm=()):
    specs = VM
    if isinstance(outs, tuple):
        specs = tuple(ANY if i in to_hbm else VM for i in range(len(outs)))
    args = [
        pltpu.with_memory_space_constraint(arg, pltpu.HBM) if spec is ANY else arg
        for arg, spec in zip(args, ins)
    ]
    return pl.pallas_call(
        body,
        out_shape=outs,
        in_specs=ins,
        out_specs=specs,
        scratch_shapes=scratch,
        compiler_params=pltpu.CompilerParams(vmem_limit_bytes=16 << 20),
    )(*args)


def per_device(coeff, energy, ranks, assign, screen, initial):
    groups = lax.axis_size("grp")
    tiles = lax.axis_size("tile")
    devices = groups * tiles
    pairs = groups // 2
    local_k, v, width = initial.shape
    levels = coeff.shape[1]
    half = levels // 2
    total_k = local_k * groups
    count = float(total_k * width * tiles)
    axes = ("grp", "tile")
    swap = [(g, g ^ 1) for g in range(groups)]
    sds = jax.ShapeDtypeStruct
    small_scratch = pltpu.VMEM((v, half), F4)
    dma = pltpu.SemaphoreType.DMA
    half_shape = sds((total_k, v, half), F4)
    small_shape = sds((v, half), F4)

    def exchange(blocks, shape):
        sent = blocks.reshape((devices,) + blocks.shape[-3:])
        return lax.all_to_all(sent, axes, 0, 0, tiled=True).reshape(shape + sent.shape[1:])

    def to_all(blocks, body):
        got = exchange(blocks, (groups, tiles))
        mine, moments = call(body, (half_shape, sds((v // 2, half), F4)), [VM], (got,))
        return mine, lax.ppermute(mine, "grp", swap), moments

    def to_owner(keep, recv, coupled):
        shape = sds((groups, tiles, 2 * local_k + 1, v // 2, half), BF)
        out = call(rows_kernel, shape, [VM] * 3, (keep, recv, coupled))
        return exchange(out, (pairs, 2, tiles))

    def factor(body, matrices, moments):
        shape = sds((matrices, v, half), F4)
        return call(functools.partial(body, count=count), shape, [VM], (moments,), (small_scratch,))

    def run_tasks(tail, *args):
        dens_shape = (2, total_k, v, half)
        outs = (half_shape, half_shape, sds(dens_shape, F4))
        first = tail is screen
        if first:
            outs = outs + (sds((tails,) + screen.shape[1:], BF),)
        return call(
            functools.partial(tasks_kernel, first=first),
            outs,
            [ANY, ANY, VM, ANY if first else VM] + [VM] * len(args),
            (assign, ranks, head, tail) + args,
            (
                pltpu.SMEM(assign.shape, jnp.int32),
                pltpu.SMEM(ranks.shape, jnp.int32),
                pltpu.VMEM(dens_shape, F4),
                pltpu.VMEM((2, total_k, 2 * v, half), BF),
                dma((3,)),
            ),
        )

    def couple(body, *args):
        outs = (sds((v // 2, half), BF), small_shape)
        return call(functools.partial(body, count=count), outs, [VM] * len(args), args, (small_scratch,))

    all_shape = sds((pairs, 2, tiles, 2 * local_k + 1, v // 2, half), BF)
    flat = sds((local_k, v, width), F4)

    tails = screen.shape[0] // 2
    inputs = (initial, energy, coeff)
    head_shape = sds((screen.shape[0] - tails,) + screen.shape[1:], BF)
    sent, initial, energy, coeff, head = call(
        start_kernel,
        (all_shape,) + tuple(sds(a.shape, a.dtype) for a in inputs) + (head_shape,),
        [ANY] * 4,
        inputs + (screen,),
        (dma((3,)), dma((local_k,)), small_scratch),
    )
    mine, other, moments = to_all(sent, first_gather_kernel)
    small = factor(first_factor_kernel, 1, moments)
    keep, send, dens, tail = run_tasks(screen, mine, other, small)
    recv = lax.ppermute(send, "grp", swap)
    coupled, diag = couple(first_coupled_kernel, keep, send, dens, moments, small)
    got = to_owner(keep, recv, coupled)
    sent, basis, precond, ray0 = call(
        functools.partial(after_first_kernel, count=count),
        (all_shape, flat, flat, small_shape),
        [VM] * 6,
        (got, initial, energy, coeff, small, diag),
        (small_scratch,),
    )
    mine, other, moments = to_all(sent, gather_kernel)
    small = factor(next_factor_kernel, 2, moments)
    keep, send, dens = run_tasks(tail, mine, other, small, dens)
    recv = lax.ppermute(send, "grp", swap)
    coupled, diag = couple(next_coupled_kernel, keep, send, dens, moments, small, diag)
    got = to_owner(keep, recv, coupled)
    sent, residual, basis, precond, ray1 = call(
        functools.partial(last_rows_kernel, count=count),
        (sds((devices, 1, half), F4), flat, flat, flat, small_shape),
        [VM] * 7,
        (got, basis, precond, energy, coeff, small, diag),
        (pltpu.VMEM(flat.shape, F4), dma((local_k,)), small_scratch),
        (1,),
    )
    got = lax.all_to_all(sent, axes, 0, 0, tiled=True)
    basis, rayleigh = call(
        functools.partial(finish_kernel, count=count),
        (flat, sds((2, v, v), F4)),
        [VM] * 5,
        (got, precond, basis, ray0, ray1),
        (pltpu.VMEM(flat.shape, F4), pltpu.VMEM((2, v, v), F4), dma((local_k + 1,))),
        (0, 1),
    )
    return (rayleigh, basis, residual)


def solution(mesh):
    placed = (
        P("grp", None, "tile"),
        P("grp", "tile"),
        P(),
        P(("grp", "tile")),
        P(("grp", "tile"), None, None),
        P("grp", None, "tile"),
    )
    return jax.shard_map(
        per_device,
        mesh=mesh,
        in_specs=placed,
        out_specs=(P(), P("grp", None, "tile"), P("grp", None, "tile")),
        check_vma=False,
    )
```

```python
import functools

import jax
import jax.numpy as jnp
from jax import lax
from jax.experimental import pallas as pl
from jax.experimental.pallas import tpu as pltpu
from jax.sharding import PartitionSpec as P

ITERS = 2
LANES = 128
BF = jnp.bfloat16
F4 = jnp.float32
NT = (((1,), (1,)), ((), ()))
NN = (((1,), (0,)), ((), ()))


def split2(x):
    high = x.astype(BF)
    return high, (x - high.astype(F4)).astype(BF)


def mm(left, right, dims):
    return lax.dot_general(left, right, dims, preferred_element_type=F4)


def exact(left, right, dims):
    return lax.dot_general(
        left, right, dims, preferred_element_type=F4, precision=lax.Precision.HIGHEST
    )


def apply_small(weights, block):
    total = weights[:, 0:1] * block[0:1, :]
    for m in range(1, weights.shape[1]):
        total = total + weights[:, m : m + 1] * block[m : m + 1, :]
    return total


def inverse_cholesky(gram):
    v = gram.shape[0]
    row_id = lax.broadcasted_iota(jnp.int32, (v, v), 0)
    col_id = lax.broadcasted_iota(jnp.int32, (v, v), 1)
    inverse = (row_id == col_id).astype(F4)
    rest = gram
    for j in range(v - 1):
        col = jnp.broadcast_to(rest[:, j : j + 1], (v, v))
        factor = jnp.where(row_id > j, col * (1.0 / col[j : j + 1, :]), 0.0)
        rest = rest - factor * rest[j : j + 1, :]
        inverse = inverse - factor * inverse[j : j + 1, :]
    pivots = jnp.sum(jnp.where(row_id == col_id, rest, 0.0), 1, keepdims=True)
    return inverse * (1.0 / jnp.sqrt(pivots))


def unit_factors(gram):
    v = gram.shape[0]
    row_id = lax.broadcasted_iota(jnp.int32, (v, v), 0)
    col_id = lax.broadcasted_iota(jnp.int32, (v, v), 1)
    lower = (row_id == col_id).astype(F4)
    inverse = lower
    rest = gram + 1e-4 * lower * gram
    for j in range(v - 1):
        col = jnp.broadcast_to(rest[:, j : j + 1], (v, v))
        pivot = jnp.maximum(col[j : j + 1, :], 1e-30)
        factor = jnp.where(row_id > j, col * (1.0 / pivot), 0.0)
        rest = rest - factor * rest[j : j + 1, :]
        inverse = inverse - factor * inverse[j : j + 1, :]
        lower = lower + jnp.where(col_id == j, factor, 0.0)
    return lower, inverse


def pieces(block):
    sub = block.shape[0] // 2
    return [block[:sub].astype(BF), block[sub:].astype(BF)]


def terms_of(used, lanes):
    return min(3, lanes // 2 // used)


def pack_moments(scratch, parts):
    total = None
    used = 0
    for part in parts:
        placed = pad_small(scratch, part)
        if used:
            placed = pltpu.roll(placed, used, 1)
        total = placed if total is None else total + placed
        used += part.shape[1]
    packed = None
    for i in range(terms_of(used, total.shape[1])):
        term = total.astype(BF).astype(F4)
        total = total - term
        packed = term if packed is None else packed + pltpu.roll(term, i * used, 1)
    sub = packed.shape[0] // 2
    return (packed[:sub] + pltpu.roll(packed, packed.shape[1] // 2, 1)[sub:]).astype(BF)


def unpack_moments(block, used):
    width = block.shape[1]
    total = jnp.concatenate([block, pltpu.roll(block, width // 2, 1)], 0)
    result = total
    for i in range(1, terms_of(used, width)):
        result = result + pltpu.roll(total, width - i * used, 1)
    return result


def pad_small(scratch, small):
    scratch[...] = jnp.zeros(scratch.shape, F4)
    scratch[:, 0 : small.shape[1]] = small
    return scratch[...]


def store_for_all(out_ref, dens_halves, moments):
    pairs, _, tiles, blocks = out_ref.shape[:4]

    def one(g, carry):
        for h in range(2):
            for t in range(tiles):
                for k in range(blocks - 1):
                    out_ref[g, h, t, k] = dens_halves[k // 2][h][k % 2]
                out_ref[g, h, t, blocks - 1] = moments
        return carry

    lax.fori_loop(0, pairs, one, 0, unroll=True)


def project(block, coeff):
    high, low = split2(block)
    both = mm(jnp.concatenate([high, low], 0), coeff, NT)
    v = block.shape[0]
    return both[:v] + both[v:]


def halves_of(total):
    half = total.shape[1] // 2
    return [pieces(total[:, :half]), pieces(total[:, half:])]


def start_kernel(x_hbm, e_hbm, c_hbm, s_hbm, out_ref, x_ref, e_ref, c_ref, s_ref, sems, c_sems, scratch):
    local_k, v, _ = x_ref.shape
    copies = [
        pltpu.make_async_copy(x_hbm, x_ref, sems.at[0]),
        pltpu.make_async_copy(e_hbm, e_ref, sems.at[1]),
    ]
    c_copies = [pltpu.make_async_copy(c_hbm.at[k], c_ref.at[k], c_sems.at[k]) for k in range(local_k)]
    screen_copy = pltpu.make_async_copy(s_hbm.at[pl.ds(0, s_ref.shape[0])], s_ref, sems.at[2])
    for copy in copies + c_copies + [screen_copy]:
        copy.start()
    for copy in copies:
        copy.wait()
    moments = None
    for k in range(local_k):
        x = x_ref[k]
        xh, xl = split2(x)
        eh, el = split2(x * e_ref[k : k + 1, :])
        big = mm(jnp.concatenate([xh, xl], 0), jnp.concatenate([xh, eh], 0), NT)
        small = mm(xh, jnp.concatenate([xl, el], 0), NT)
        part = big[:v] + big[v:] + small
        moments = part if moments is None else moments + part
    for copy in c_copies:
        copy.wait()
    projected = [project(x_ref[k], c_ref[k]) for k in range(local_k)]
    lower, inverse = unit_factors(moments[:, 0:v])
    halves = [halves_of(apply_small(inverse, block)) for block in projected]
    store_for_all(out_ref, halves, pack_moments(scratch, [moments, lower]))
    screen_copy.wait()


def gather_kernel(mine_ref, dens_ref, moments_ref):
    groups, tiles, blocks, sub, _ = mine_ref.shape
    local_k = blocks // 2
    moments = None
    for g in range(groups):
        for b in range(blocks - 1):
            total = mine_ref[g, 0, b].astype(F4)
            for t in range(1, tiles):
                total = total + mine_ref[g, t, b].astype(F4)
            row = b % 2 * sub
            dens_ref[g * local_k + b // 2, row : row + sub, :] = total
        for t in range(tiles):
            block = mine_ref[g, t, blocks - 1].astype(F4)
            moments = block if moments is None else moments + block
    moments_ref[...] = moments


def first_gather_kernel(mine_ref, dens_ref, moments_ref):
    groups, tiles, blocks, sub, lanes = mine_ref.shape
    local_k = blocks // 2
    v = 2 * sub
    lane = lax.broadcasted_iota(jnp.int32, (v, lanes), 1)
    own = (lane >= 2 * v) & (lane < 3 * v)
    moments = None
    for g in range(groups):
        factors = None
        for t in range(tiles):
            block = mine_ref[g, t, blocks - 1].astype(F4)
            moments = block if moments is None else moments + block
            lower = jnp.where(own, unpack_moments(block, 3 * v), 0.0)
            lower = pltpu.roll(lower, (lanes + (t - 2) * v) % lanes, 1)
            factors = lower if factors is None else factors + lower
        left = jnp.concatenate(split2(factors[:, : tiles * v]), 0)
        columns = []
        for k in range(local_k):
            sent = [mine_ref[g, t, 2 * k + i].astype(F4) for t in range(tiles) for i in range(2)]
            columns.append(jnp.concatenate(sent, 0).astype(BF))
        both = mm(left, jnp.concatenate(columns, 1), NN)
        both = both[:v] + both[v:]
        for k in range(local_k):
            dens_ref[g * local_k + k] = both[:, k * lanes : (k + 1) * lanes]
    moments_ref[...] = moments


def first_factor_kernel(moments_ref, small_ref, scratch, *, count):
    v = 2 * moments_ref.shape[0]
    moments = unpack_moments(moments_ref[...], 3 * v)
    small_ref[0] = pad_small(scratch, inverse_cholesky(moments[:, 0:v] / count))


def next_factor_kernel(moments_ref, small_ref, scratch, *, count):
    v = 2 * moments_ref.shape[0]
    moments = unpack_moments(moments_ref[...], 4 * v) / count
    mix = moments[:, v : 2 * v]
    inverse = inverse_cholesky(moments[:, 0:v] - exact(mix, mix, NT))
    small_ref[0] = pad_small(scratch, inverse)
    small_ref[1] = pad_small(scratch, apply_small(inverse, mix))


def own_core():
    return lax.axis_index("grp") % 2


def tasks_kernel(assign_hbm, ranks_hbm, head_ref, tail_ref, mine_ref, other_ref, small_ref, *refs, first):
    prev_dens_ref = None
    if first:
        tail_hbm, tail_ref = tail_ref, refs[3]
        refs = refs[:3] + refs[4:]
    else:
        prev_dens_ref, refs = refs[0], refs[1:]
    keep_ref, send_ref, dens_ref, assign_ref, ranks_ref, acc_ref, terms_ref, sems = refs
    heads = head_ref.shape[0]
    tails = tail_ref.shape[0]
    tables = [
        pltpu.make_async_copy(assign_hbm, assign_ref, sems.at[0]),
        pltpu.make_async_copy(ranks_hbm, ranks_ref, sems.at[1]),
    ]
    for copy in tables:
        copy.start()
    if first:
        tail_copy = pltpu.make_async_copy(tail_hbm.at[pl.ds(heads, tails)], tail_ref, sems.at[2])
        tail_copy.start()
    acc_ref[...] = jnp.zeros(acc_ref.shape, F4)
    core = own_core()
    total_k, v, half = mine_ref.shape
    inverse = small_ref[0][:, 0:v]
    for k in range(total_k):
        for which, ref in ((0, mine_ref), (1, other_ref)):
            slot = (core + which) % 2
            dens = apply_small(inverse, ref[k])
            if prev_dens_ref is not None:
                dens = dens - apply_small(small_ref[1][:, 0:v], prev_dens_ref[slot, k])
            dens_ref[slot, k] = dens
            terms_ref[slot, k] = jnp.concatenate(split2(dens), 0)
    lane = lax.broadcasted_iota(jnp.int32, (2 * v, 2 * half), 1)
    for copy in tables:
        copy.wait()

    def one(screen_ref, offset, t, carry):
        pair = assign_ref[offset + t]
        row = pair // total_k
        col = pair - row * total_k
        keep = lane < ranks_ref[row, col]
        vec = jnp.concatenate([terms_ref[0, col], terms_ref[1, col]], 1)
        vec = jnp.where(keep, vec, jnp.zeros_like(vec))
        term = mm(vec, screen_ref[t], NT)
        term = jnp.where(keep[:v], term[:v] + term[v:], 0.0)
        acc_ref[0, row] = acc_ref[0, row] + term[:, :half]
        acc_ref[1, row] = acc_ref[1, row] + term[:, half:]
        return carry

    lax.fori_loop(0, heads, functools.partial(one, head_ref, 0), 0, unroll=True)
    if first:
        tail_copy.wait()
    lax.fori_loop(0, tails, functools.partial(one, tail_ref, heads), 0, unroll=True)
    for k in range(total_k):
        keep_ref[k] = acc_ref[core, k]
        send_ref[k] = acc_ref[1 - core, k]


def coupled_part(keep_ref, send_ref, dens_ref):
    total_k, v, _ = keep_ref.shape
    core = own_core()
    total = None
    for k in range(total_k):
        for which, ref in ((0, keep_ref), (1, send_ref)):
            rh, rl = split2(ref[k])
            dh, dl = split2(dens_ref[(core + which) % 2, k])
            big = mm(jnp.concatenate([rh, rl], 0), dh, NT)
            part = big[:v] + big[v:] + mm(rh, dl, NT)
            total = part if total is None else total + part
    return total


def first_coupled_kernel(keep_ref, send_ref, dens_ref, moments_ref, small_ref, coupled_ref, diag_ref, scratch, *, count):
    v = 2 * moments_ref.shape[0]
    coupled_ref[...] = pack_moments(scratch, [coupled_part(keep_ref, send_ref, dens_ref)])
    weighted = unpack_moments(moments_ref[...], 3 * v)[:, v : 2 * v] / count
    inverse = small_ref[0][:, 0:v]
    diag_ref[...] = pad_small(scratch, exact(exact(inverse, weighted, NN), inverse, NT))


def next_coupled_kernel(keep_ref, send_ref, dens_ref, moments_ref, small_ref, prev_diag_ref, coupled_ref, diag_ref, scratch, *, count):
    v = 2 * moments_ref.shape[0]
    coupled_ref[...] = pack_moments(scratch, [coupled_part(keep_ref, send_ref, dens_ref)])
    moments = unpack_moments(moments_ref[...], 4 * v) / count
    mix = moments[:, v : 2 * v]
    rp = moments[:, 2 * v : 3 * v]
    rv = moments[:, 3 * v : 4 * v]
    mixed = exact(exact(mix, prev_diag_ref[:, 0:v], NN), mix, NT)
    weighted = rp - exact(rv, mix, NT) - exact(mix, rv, NT) + mixed
    inverse = small_ref[0][:, 0:v]
    diag_ref[...] = pad_small(scratch, exact(exact(inverse, weighted, NN), inverse, NT))


def rows_kernel(keep_ref, recv_ref, coupled_ref, out_ref):
    groups, tiles, blocks = out_ref.shape[:3]
    local_k = blocks // 2
    for g in range(groups):
        for k in range(local_k):
            rows = pieces(keep_ref[g * local_k + k] + recv_ref[g * local_k + k])
            for t in range(tiles):
                out_ref[g, t, 2 * k] = rows[0]
                out_ref[g, t, 2 * k + 1] = rows[1]
        for t in range(tiles):
            out_ref[g, t, blocks - 1] = coupled_ref[...]


def sum_rows(recv_ref):
    pairs, _, tiles, blocks, sub, _ = recv_ref.shape

    def summed(block, halves):
        total = None
        for g in range(pairs):
            for h in halves:
                for t in range(tiles):
                    part = recv_ref[g, h, t, block].astype(F4)
                    total = part if total is None else total + part
        return total

    def both(k, half):
        return jnp.concatenate([summed(2 * k, (half,)), summed(2 * k + 1, (half,))], 0)

    rows = [jnp.concatenate([both(k, 0), both(k, 1)], 1) for k in range(blocks // 2)]
    return rows, unpack_moments(summed(blocks - 1, (0, 1)), 2 * sub)[:, 0 : 2 * sub]


def expand(rows, coeff):
    both = mm(jnp.concatenate(split2(rows), 0), coeff, NN)
    v = rows.shape[0]
    return both[:v] + both[v:]


def after_first_kernel(recv_ref, x_ref, e_ref, c_ref, small_ref, diag_ref, out_ref, v_ref, p_ref, ray_ref, scratch, *, count):
    local_k, v, _ = x_ref.shape
    rows, coupled = sum_rows(recv_ref)
    expanded = [expand(rows[k], c_ref[k]) for k in range(local_k)]
    inverse = small_ref[0][:, 0:v]
    ray = diag_ref[:, 0:v] + coupled / count
    ray_ref[...] = pad_small(scratch, ray)
    inverse_energy = 1.0 / e_ref[...]
    residuals = []
    for k in range(local_k):
        basis = apply_small(inverse, x_ref[k])
        residual = e_ref[k : k + 1, :] * basis + expanded[k] - apply_small(ray, basis)
        residuals.append(residual)
        v_ref[k] = basis
        p_ref[k] = residual * inverse_energy[k : k + 1, :]
    halves = [halves_of(project(p_ref[k], c_ref[k])) for k in range(local_k)]
    moments = None
    for k in range(local_k):
        bh, bl = split2(v_ref[k])
        rh, rl = split2(residuals[k])
        ph, pw = split2(p_ref[k])
        big = mm(jnp.concatenate([ph, rh, pw, rl], 0), jnp.concatenate([ph, bh], 0), NT)
        small = mm(jnp.concatenate([ph, rh], 0), jnp.concatenate([pw, bl], 0), NT)
        part = big[: 2 * v] + big[2 * v :] + small
        moments = part if moments is None else moments + part
    store_for_all(out_ref, halves, pack_moments(scratch, [moments[:v], moments[v:]]))


def last_rows_kernel(recv_ref, v_ref, p_ref, e_ref, c_ref, small_ref, diag_ref, out_ref, res_hbm, basis_ref, q_ref, ray_ref, res_ref, sems, scratch, *, count):
    local_k, v, _ = v_ref.shape
    rows, coupled = sum_rows(recv_ref)
    expanded = [expand(rows[k], c_ref[k]) for k in range(local_k)]
    inverse = small_ref[0][:, 0:v]
    both = small_ref[1][:, 0:v]
    ray = diag_ref[:, 0:v] + coupled / count
    ray_ref[...] = pad_small(scratch, ray)
    inverse_energy = 1.0 / e_ref[...]
    copies = []
    for k in range(local_k):
        basis = apply_small(inverse, p_ref[k]) - apply_small(both, v_ref[k])
        residual = e_ref[k : k + 1, :] * basis + expanded[k] - apply_small(ray, basis)
        res_ref[k] = residual
        copies.append(pltpu.make_async_copy(res_ref.at[k], res_hbm.at[k], sems.at[k]))
        copies[-1].start()
        basis_ref[k] = basis
        q_ref[k] = residual * inverse_energy[k : k + 1, :]
    moments = None
    for k in range(local_k):
        bh, bl = split2(basis_ref[k])
        ph, pw = split2(q_ref[k])
        big = mm(jnp.concatenate([ph, pw], 0), jnp.concatenate([ph, bh], 0), NT)
        part = big[:v] + big[v:] + mm(ph, jnp.concatenate([pw, bl], 0), NT)
        moments = part if moments is None else moments + part
    packed = to_row(pad_small(scratch, moments), 2 * v)
    for d in range(out_ref.shape[0]):
        out_ref[d] = packed
    for copy in copies:
        copy.wait()


def diagonal_lanes(shape, width):
    row_id = lax.broadcasted_iota(jnp.int32, shape, 0)
    return lax.broadcasted_iota(jnp.int32, shape, 1) // width == row_id


def fold_lanes(block, width):
    shift = width
    while shift < block.shape[1]:
        block = block + pltpu.roll(block, shift, 1)
        shift *= 2
    return block


def to_row(block, width):
    spread = fold_lanes(block, width)
    return jnp.sum(jnp.where(diagonal_lanes(block.shape, width), spread, 0.0), 0, keepdims=True)


def from_row(row, rows, width):
    block = jnp.broadcast_to(row, (rows, row.shape[1]))
    return fold_lanes(jnp.where(diagonal_lanes(block.shape, width), block, 0.0), width)


def finish_kernel(recv_ref, q_ref, b_ref, ray0_ref, ray1_ref, out_hbm, ray_hbm, out_ref, ray_ref, sems, *, count):
    local_k, v, _ = q_ref.shape
    ray_ref[0] = ray0_ref[:, 0:v].T
    ray_ref[1] = ray1_ref[:, 0:v].T
    copies = [pltpu.make_async_copy(ray_ref, ray_hbm, sems.at[local_k])]
    copies[0].start()
    row = jnp.sum(recv_ref[:, 0, :], 0, keepdims=True)
    moments = from_row(row, v, 2 * v) / count
    mix = moments[:, v : 2 * v]
    inverse = inverse_cholesky(moments[:, 0:v] - exact(mix, mix, NT))
    both = apply_small(inverse, mix)
    for k in range(local_k):
        out_ref[k] = apply_small(inverse, q_ref[k]) - apply_small(both, b_ref[k])
        copies.append(pltpu.make_async_copy(out_ref.at[k], out_hbm.at[k], sems.at[k]))
        copies[-1].start()
    for copy in copies:
        copy.wait()


VM = pl.BlockSpec(memory_space=pltpu.VMEM)
ANY = pl.BlockSpec(memory_space=pltpu.HBM)


def call(body, outs, ins, args, scratch=(), to_hbm=()):
    specs = VM
    if isinstance(outs, tuple):
        specs = tuple(ANY if i in to_hbm else VM for i in range(len(outs)))
    args = [
        pltpu.with_memory_space_constraint(arg, pltpu.HBM) if spec is ANY else arg
        for arg, spec in zip(args, ins)
    ]
    return pl.pallas_call(
        body,
        out_shape=outs,
        in_specs=ins,
        out_specs=specs,
        scratch_shapes=scratch,
        compiler_params=pltpu.CompilerParams(vmem_limit_bytes=16 << 20),
    )(*args)


def per_device(coeff, energy, ranks, assign, screen, initial):
    groups = lax.axis_size("grp")
    tiles = lax.axis_size("tile")
    devices = groups * tiles
    pairs = groups // 2
    local_k, v, width = initial.shape
    levels = coeff.shape[1]
    half = levels // 2
    total_k = local_k * groups
    count = float(total_k * width * tiles)
    axes = ("grp", "tile")
    swap = [(g, g ^ 1) for g in range(groups)]
    sds = jax.ShapeDtypeStruct
    small_scratch = pltpu.VMEM((v, half), F4)
    dma = pltpu.SemaphoreType.DMA
    half_shape = sds((total_k, v, half), F4)
    small_shape = sds((v, half), F4)

    def exchange(blocks, shape):
        sent = blocks.reshape((devices,) + blocks.shape[-3:])
        return lax.all_to_all(sent, axes, 0, 0, tiled=True).reshape(shape + sent.shape[1:])

    def to_all(blocks, body):
        got = exchange(blocks, (groups, tiles))
        mine, moments = call(body, (half_shape, sds((v // 2, half), F4)), [VM], (got,))
        return mine, lax.ppermute(mine, "grp", swap), moments

    def to_owner(keep, recv, coupled):
        shape = sds((groups, tiles, 2 * local_k + 1, v // 2, half), BF)
        out = call(rows_kernel, shape, [VM] * 3, (keep, recv, coupled))
        return exchange(out, (pairs, 2, tiles))

    def factor(body, matrices, moments):
        shape = sds((matrices, v, half), F4)
        return call(functools.partial(body, count=count), shape, [VM], (moments,), (small_scratch,))

    def run_tasks(tail, *args):
        dens_shape = (2, total_k, v, half)
        outs = (half_shape, half_shape, sds(dens_shape, F4))
        first = tail is screen
        if first:
            outs = outs + (sds((tails,) + screen.shape[1:], BF),)
        return call(
            functools.partial(tasks_kernel, first=first),
            outs,
            [ANY, ANY, VM, ANY if first else VM] + [VM] * len(args),
            (assign, ranks, head, tail) + args,
            (
                pltpu.SMEM(assign.shape, jnp.int32),
                pltpu.SMEM(ranks.shape, jnp.int32),
                pltpu.VMEM(dens_shape, F4),
                pltpu.VMEM((2, total_k, 2 * v, half), BF),
                dma((3,)),
            ),
        )

    def couple(body, *args):
        outs = (sds((v // 2, half), BF), small_shape)
        return call(functools.partial(body, count=count), outs, [VM] * len(args), args, (small_scratch,))

    all_shape = sds((pairs, 2, tiles, 2 * local_k + 1, v // 2, half), BF)
    flat = sds((local_k, v, width), F4)

    tails = screen.shape[0] // 2
    inputs = (initial, energy, coeff)
    head_shape = sds((screen.shape[0] - tails,) + screen.shape[1:], BF)
    sent, initial, energy, coeff, head = call(
        start_kernel,
        (all_shape,) + tuple(sds(a.shape, a.dtype) for a in inputs) + (head_shape,),
        [ANY] * 4,
        inputs + (screen,),
        (dma((3,)), dma((local_k,)), small_scratch),
    )
    mine, other, moments = to_all(sent, first_gather_kernel)
    small = factor(first_factor_kernel, 1, moments)
    keep, send, dens, tail = run_tasks(screen, mine, other, small)
    recv = lax.ppermute(send, "grp", swap)
    coupled, diag = couple(first_coupled_kernel, keep, send, dens, moments, small)
    got = to_owner(keep, recv, coupled)
    sent, basis, precond, ray0 = call(
        functools.partial(after_first_kernel, count=count),
        (all_shape, flat, flat, small_shape),
        [VM] * 6,
        (got, initial, energy, coeff, small, diag),
        (small_scratch,),
    )
    mine, other, moments = to_all(sent, gather_kernel)
    small = factor(next_factor_kernel, 2, moments)
    keep, send, dens = run_tasks(tail, mine, other, small, dens)
    recv = lax.ppermute(send, "grp", swap)
    coupled, diag = couple(next_coupled_kernel, keep, send, dens, moments, small, diag)
    got = to_owner(keep, recv, coupled)
    sent, residual, basis, precond, ray1 = call(
        functools.partial(last_rows_kernel, count=count),
        (sds((devices, 1, half), F4), flat, flat, flat, small_shape),
        [VM] * 7,
        (got, basis, precond, energy, coeff, small, diag),
        (pltpu.VMEM(flat.shape, F4), dma((local_k,)), small_scratch),
        (1,),
    )
    got = lax.all_to_all(sent, axes, 0, 0, tiled=True)
    basis, rayleigh = call(
        functools.partial(finish_kernel, count=count),
        (flat, sds((2, v, v), F4)),
        [VM] * 5,
        (got, precond, basis, ray0, ray1),
        (pltpu.VMEM(flat.shape, F4), pltpu.VMEM((2, v, v), F4), dma((local_k + 1,))),
        (0, 1),
    )
    return (rayleigh, basis, residual)


def solution(mesh):
    placed = (
        P("grp", None, "tile"),
        P("grp", "tile"),
        P(),
        P(("grp", "tile")),
        P(("grp", "tile"), None, None),
        P("grp", None, "tile"),
    )
    return jax.shard_map(
        per_device,
        mesh=mesh,
        in_specs=placed,
        out_specs=(P(), P("grp", None, "tile"), P("grp", None, "tile")),
        check_vma=False,
    )
```
